256 devices in a mesh: dp: 16 (over x, y), tensor: 16 (over z, core).
Axes of the slice: x: 4, y: 4, z: 8, core: 2. Of those that a mesh axis runs over, the one named last changes fastest.
Arguments:
- hidden: bfloat16 [32768, 1280], P(('dp', 'tensor')), may hold values from -6 to 6
- lengths: int32 [16, 8], P('dp'), may hold values from 1 to 1024, 2048 in all within a row
- request_prompt: int32 [16, 8], P('dp'), may hold values from 0 to 31
- request_adapter: int32 [16, 8], P('dp'), may hold values from 0 to 63
- prompt_page_table: int32 [32, 4], replicated, may hold values from 0 to 63
- prefix_page_cache: bfloat16 [64, 64, 2048], P('dp', None, 'tensor'), may hold values from -6 to 6
- query_key_value_weight: bfloat16 [1280, 3072], P(None, 'tensor'), may hold values from -0.15625 to 0.15625
- adapter_down: bfloat16 [64, 1280, 16], P('dp'), may hold values from -0.15625 to 0.15625
- adapter_up: bfloat16 [64, 16, 3072], P('dp', None, 'tensor'), may hold values from -1.5 to 1.5
- attention_scale: float32 [1024], P('tensor'), may hold values from 0.5 to 1.5
- output_matrix: bfloat16 [1024, 1280], P('tensor'), may hold values from -0.1875 to 0.1875
- attention_rate: float32 [1280], replicated, may hold values from 0.05 to 0.5
- up_matrix: bfloat16 [1280, 5120], P(None, 'tensor'), may hold values from -0.15625 to 0.15625
- gate_matrix: bfloat16 [1280, 5120], P(None, 'tensor'), may hold values from -0.15625 to 0.15625
- up_scaling: float32 [5120], P('tensor'), may hold values from 0.5 to 2
- gate_scaling: float32 [5120], P('tensor'), may hold values from 0.5 to 2
- down_matrix: bfloat16 [5120, 1280], P('tensor'), may hold values from -0.078125 to 0.078125
- feedforward_rate: float32 [1280], replicated, may hold values from 0.05 to 0.5
Outputs:
- hidden_out: bfloat16 [32768, 1280], P(('dp', 'tensor'))
The draws below stay inside these ranges and needn't reach their ends.
Inputs may be any that keep to these rules, and one draw needn't show every extreme that they name: Each group's lengths sum to 2048.
All inputs are finite; a program needn't handle non-finite values.
Results may differ from the reference program's by a relative error of at most 0.015.
Values may be sent and summed in bfloat16 or wider, within the bound.
A program may use at most 64 MiB of HBM per device.

```python
import math
import jax
import jax.numpy as jnp
import numpy as np
from jax import lax

MODEL_WIDTH = 1280
ATTENTION_HEADS = 16
HEAD_WIDTH = 64
FF = 5120
ADAPTER_RANK = 16
ADAPTER_TOTAL = 64
GROUP_REQUESTS = 8
PAGE = 64
PPG = 4
GROUPS = 32
GROUP_TOKENS = 2048
TOKENS = 32768
PREFIX_LEN = 256
TOTAL_PAGES = 64
N_DP = 16
N_TENSOR = 16


def touch_ends(entries, rng, smallest, high):
    dims = entries.shape
    place = [jax.random.randint(jax.random.fold_in(rng, axis), (), 0, dims[axis]) for axis in range(len(dims))]
    entries = entries.at[tuple(place)].set(smallest)
    longest = dims.index(max(dims))
    place[longest] = (place[longest] + 1) % dims[longest]
    return entries.at[tuple(place)].set(high)


def steps_of(key, extent, cuts, low, high):
    level = 1.0
    for axis_at, shards_of in cuts:
        heights = jax.random.uniform(jax.random.fold_in(jax.random.fold_in(key, 6), axis_at), (shards_of,), jnp.float32, low / len(cuts), high / len(cuts))
        level = level * jnp.repeat(jnp.exp(heights), extent[axis_at] // shards_of).reshape((-1,) + (1,) * (len(extent) - 1 - axis_at))
    return level


def length_profile(amount, total, limit, skew):
    loads = [(1 << 20) // math.isqrt(standing ** skew) + 1 for standing in range(2, amount + 1)]
    spare, holding = total - limit - (amount - 1), [1] * (amount - 1)
    while spare > 0:
        free = [i for i in range(amount - 1) if holding[i] < limit]
        pool, remaining = sum([loads[i] for i in free]), spare
        for i in free:
            addition = min(limit - holding[i], max(1, remaining * loads[i] // pool), spare)
            holding[i] = holding[i] + addition
            spare = spare - addition
    return np.array([limit] + holding)


def ragged_sizes(rng, number_of, total, most, lean):
    if number_of == 2:
        one = jax.random.randint(rng, (), max(1, total - most), min(most, total - 1) + 1)
        return jnp.stack([one, total - one])
    tallies = jnp.asarray(length_profile(number_of, total, most, lean), jnp.int32)
    pairs = (number_of - 1) // 2
    donor, receiver = tallies[1:1 + 2 * pairs:2], tallies[2:2 + 2 * pairs:2]
    room = jnp.minimum(donor - 1, most - receiver)
    passed = jax.random.randint(jax.random.fold_in(rng, 1), (pairs,), 0, 1 << 20) % (room + 1)
    tallies = tallies.at[1:1 + 2 * pairs:2].set(donor - passed).at[2:2 + 2 * pairs:2].set(receiver + passed)
    return tallies[jax.random.permutation(jax.random.fold_in(rng, 2), number_of)]


def gaussian(stream_key, dims, scale, reach, split=(), kind=jnp.bfloat16):
    factor_of = steps_of(stream_key, dims, split, -0.22, 0.18) if split else 1.0
    result = jax.random.normal(stream_key, dims, jnp.float32) * scale * factor_of
    return jnp.minimum(jnp.maximum(result, -reach), reach).astype(kind)


def setup_inputs(seed: int = 0) -> dict:
    splits = jax.random.split(jax.random.key(seed), 19)
    return {
        "hidden": gaussian(splits[0], (TOKENS, MODEL_WIDTH), 1.0, 6.0, ((0, 256),)),
        "lengths": jax.vmap(lambda own: ragged_sizes(own, GROUP_REQUESTS, GROUP_TOKENS, GROUP_TOKENS // 2, 2))(jax.random.split(splits[1], N_DP)).reshape((N_DP, GROUP_REQUESTS)).astype(jnp.int32),
        "request_prompt": touch_ends(jax.random.randint(splits[2], (N_DP, GROUP_REQUESTS), 0, GROUPS), jax.random.fold_in(splits[2], 1), 0, GROUPS - 1).astype(jnp.int32),
        "request_adapter": touch_ends(jax.random.randint(splits[3], (N_DP, GROUP_REQUESTS), 0, ADAPTER_TOTAL), jax.random.fold_in(splits[3], 1), 0, ADAPTER_TOTAL - 1).astype(jnp.int32),
        "prompt_page_table": touch_ends(jax.random.randint(splits[4], (GROUPS, PPG), 0, TOTAL_PAGES), jax.random.fold_in(splits[4], 1), 0, TOTAL_PAGES - 1).astype(jnp.int32),
        "prefix_page_cache": gaussian(splits[5], (TOTAL_PAGES, PAGE, ATTENTION_HEADS * 2 * HEAD_WIDTH), 1.0, 6.0, ((0, 16), (2, 16))),
        "query_key_value_weight": gaussian(splits[6], (MODEL_WIDTH, ATTENTION_HEADS * 3 * HEAD_WIDTH), MODEL_WIDTH ** -0.5, 0.15625, ((1, 16),)),
        "adapter_down": gaussian(splits[7], (ADAPTER_TOTAL, MODEL_WIDTH, ADAPTER_RANK), MODEL_WIDTH ** -0.5, 0.15625, ((0, 16),)),
        "adapter_up": gaussian(splits[8], (ADAPTER_TOTAL, ADAPTER_RANK, ATTENTION_HEADS * 3 * HEAD_WIDTH), ADAPTER_RANK ** -0.5, 1.5, ((0, 16), (2, 16))),
        "attention_scale": jnp.clip(jnp.exp(math.log(1.5) - 1.0986123 * jax.random.uniform(splits[9], (ATTENTION_HEADS * HEAD_WIDTH,), jnp.float32) ** steps_of(splits[9], (ATTENTION_HEADS * HEAD_WIDTH,), ((0, 16),), -0.2, 0.2)), 0.5, 1.5),
        "output_matrix": gaussian(splits[10], (ATTENTION_HEADS * HEAD_WIDTH, MODEL_WIDTH), (ATTENTION_HEADS * HEAD_WIDTH) ** -0.5, 0.1875, ((0, 16),)),
        "attention_rate": jnp.clip(jnp.exp(jax.random.uniform(splits[11], (MODEL_WIDTH,), jnp.float32, math.log(0.05), math.log(0.5))), 0.05, 0.5),
        "up_matrix": gaussian(splits[12], (MODEL_WIDTH, FF), MODEL_WIDTH ** -0.5, 0.15625, ((1, 16),)),
        "gate_matrix": gaussian(splits[13], (MODEL_WIDTH, FF), MODEL_WIDTH ** -0.5, 0.15625, ((1, 16),)),
        "up_scaling": jnp.clip(jnp.exp(math.log(2.0) - 1.3862944 * jax.random.uniform(splits[14], (FF,), jnp.float32) ** steps_of(splits[14], (FF,), ((0, 16),), -0.2, 0.2)), 0.5, 2.0),
        "gate_scaling": jnp.clip(jnp.exp(math.log(2.0) - 1.3862944 * jax.random.uniform(splits[15], (FF,), jnp.float32) ** steps_of(splits[15], (FF,), ((0, 16),), -0.2, 0.2)), 0.5, 2.0),
        "down_matrix": gaussian(splits[16], (FF, MODEL_WIDTH), FF ** -0.5, 0.078125, ((0, 16),)),
        "feedforward_rate": jnp.clip(jnp.exp(jax.random.uniform(splits[17], (MODEL_WIDTH,), jnp.float32, math.log(0.05), math.log(0.5))), 0.05, 0.5),
    }


adapter_scale = 0.5
epsilon = 1e-06

def renorm(matrix):
    return matrix * lax.rsqrt(lax.optimization_barrier(jnp.mean(matrix * matrix, axis=-1, keepdims=True)) + epsilon)

def to_unit(vectors):
    return vectors * lax.rsqrt(lax.optimization_barrier(jnp.sum(vectors * vectors, axis=-1, keepdims=True)) + epsilon)

def rotate(vectors, position):
    half_size = vectors.shape[-1] // 2
    frequency = jnp.exp(jnp.arange(half_size).astype(jnp.float32) * (-2.0 * math.log(10000.0) / vectors.shape[-1]))
    angles = position[:, None] * frequency[None, :]
    cosine = jnp.cos(angles)[:, None, :]
    sines = jnp.sin(angles)[:, None, :]
    first_half = vectors[..., :half_size]
    second_half = vectors[..., half_size:]
    return jnp.concatenate([first_half * cosine - second_half * sines, first_half * sines + second_half * cosine], axis=-1)

def layout(counts, total_rows):
    row_ends = jnp.cumsum(counts).astype(jnp.int32)
    starts = row_ends - counts
    row_ids = jnp.arange(total_rows, dtype=jnp.int32)
    request_number = lax.optimization_barrier(jnp.sum((row_ids[:, None] >= row_ends[None, :]).astype(jnp.int32), axis=1))
    selected_adapter = request_number[:, None] == jnp.arange(counts.shape[0], dtype=jnp.int32)[None, :]
    offset = row_ids - lax.optimization_barrier(jnp.sum(jnp.where(selected_adapter, starts[None, :], 0), axis=1)).astype(jnp.int32)
    return (request_number, offset)

def attend(queries, key_all, value_all, request_number, key_request, key_row):
    rows_total = queries.shape[0]
    block_rows = min(512, rows_total)
    score_scale = math.sqrt(queries.shape[-1])
    row_ids = jnp.arange(rows_total, dtype=jnp.int32)
    keys_wide = key_all.astype(jnp.float32)
    values_wide = value_all.astype(jnp.float32)

    def one_block(block_index):
        first_row = (block_index * block_rows).astype(jnp.int32)
        query_block = lax.dynamic_slice_in_dim(queries, first_row, block_rows, 0).astype(jnp.float32)
        request_block = lax.dynamic_slice_in_dim(request_number, first_row, block_rows, 0)
        row_block = lax.dynamic_slice_in_dim(row_ids, first_row, block_rows, 0)
        scores = jnp.einsum('qhd,khd->hqk', query_block, keys_wide) * score_scale
        allowed = (request_block[:, None] == key_request[None, :]) & (key_row[None, :] <= row_block[:, None])
        exp_scores = jnp.where(allowed[None], jnp.exp(scores), 0.0)
        weights = (exp_scores / lax.optimization_barrier(jnp.sum(exp_scores, axis=-1, keepdims=True))).astype(jnp.bfloat16)
        mixed_block = jnp.einsum('hqk,khd->qhd', weights.astype(jnp.float32), values_wide)
        return mixed_block.reshape(block_rows, -1).astype(jnp.bfloat16)
    blocks = lax.map(one_block, jnp.arange(rows_total // block_rows, dtype=jnp.int32))
    return blocks.reshape(rows_total, -1)

def split_sum(left_side, right_side):
    part_width = left_side.shape[1] // N_TENSOR

    def add_part(part_index, totals):
        start_col = (part_index * part_width).astype(jnp.int32)
        part_left = lax.dynamic_slice_in_dim(left_side, start_col, part_width, 1)
        part_right = lax.dynamic_slice_in_dim(right_side, start_col, part_width, 0)
        partial_value = jnp.dot(part_left, part_right, preferred_element_type=jnp.float32).astype(jnp.bfloat16)
        partial_value = lax.optimization_barrier(partial_value)
        return totals + partial_value.astype(jnp.float32)
    return lax.fori_loop(jnp.int32(0), jnp.int32(N_TENSOR), add_part, jnp.zeros((left_side.shape[0], right_side.shape[1]), jnp.float32))

def reference(hidden, lengths, request_prompt, request_adapter, prompt_page_table, prefix_page_cache, query_key_value_weight, adapter_down, adapter_up, attention_scale, output_matrix, attention_rate, up_matrix, gate_matrix, up_scaling, gate_scaling, down_matrix, feedforward_rate):
    gain_qk = attention_scale.reshape(ATTENTION_HEADS, HEAD_WIDTH)
    cache_view = prefix_page_cache.reshape(TOTAL_PAGES, PAGE, ATTENTION_HEADS, 2, HEAD_WIDTH)
    cache_keys = (to_unit(cache_view[:, :, :, 0, :].astype(jnp.float32)) * gain_qk).astype(jnp.bfloat16)
    cache_values = cache_view[:, :, :, 1, :]
    request_of_slot = jnp.arange(GROUP_REQUESTS * ADAPTER_RANK, dtype=jnp.int32) // ADAPTER_RANK
    prefix_request = jnp.arange(GROUP_REQUESTS * PREFIX_LEN, dtype=jnp.int32) // PREFIX_LEN
    prefix_row = jnp.full((GROUP_REQUESTS * PREFIX_LEN,), -1, jnp.int32)

    def one_group(inputs):
        row_values, counts, groups, selected_adapter = inputs
        request_number, offset = layout(counts, GROUP_TOKENS)
        position = offset.astype(jnp.float32) + PREFIX_LEN
        plain_projection = jnp.dot(row_values, query_key_value_weight, preferred_element_type=jnp.float32)
        selected_down = jnp.transpose(adapter_down[selected_adapter], (1, 0, 2)).reshape(MODEL_WIDTH, GROUP_REQUESTS * ADAPTER_RANK)
        adapter_middle = jnp.dot(row_values, selected_down, preferred_element_type=jnp.float32)
        adapter_middle = jnp.where(request_number[:, None] == request_of_slot[None, :], adapter_middle, 0.0).astype(jnp.bfloat16)
        selected_up = adapter_up[selected_adapter].reshape(GROUP_REQUESTS * ADAPTER_RANK, ATTENTION_HEADS * 3 * HEAD_WIDTH)
        query_key_value = (plain_projection + adapter_scale * jnp.dot(adapter_middle, selected_up, preferred_element_type=jnp.float32)).reshape(GROUP_TOKENS, ATTENTION_HEADS, 3, HEAD_WIDTH)
        queries = (to_unit(rotate(query_key_value[:, :, 0, :], position)) * gain_qk).astype(jnp.bfloat16)
        key_own = (to_unit(rotate(query_key_value[:, :, 1, :], position)) * gain_qk).astype(jnp.bfloat16)
        value_own = query_key_value[:, :, 2, :].astype(jnp.bfloat16)
        page_list = prompt_page_table[groups].reshape(-1)
        prefix_keys = cache_keys[page_list].reshape(GROUP_REQUESTS * PREFIX_LEN, ATTENTION_HEADS, HEAD_WIDTH)
        prefix_values = cache_values[page_list].reshape(GROUP_REQUESTS * PREFIX_LEN, ATTENTION_HEADS, HEAD_WIDTH)
        key_all = jnp.concatenate([prefix_keys, key_own], axis=0)
        value_all = jnp.concatenate([prefix_values, value_own], axis=0)
        key_request = jnp.concatenate([prefix_request, request_number], axis=0)
        key_row = jnp.concatenate([prefix_row, jnp.arange(GROUP_TOKENS, dtype=jnp.int32)], axis=0)
        attn = attend(queries, key_all, value_all, request_number, key_request, key_row)
        attn_sum = split_sum(attn, output_matrix)
        base_rows = row_values.astype(jnp.float32)
        mixed = renorm(base_rows + attention_rate * (renorm(attn_sum) - base_rows)).astype(jnp.bfloat16)
        up_part = jnp.dot(mixed, up_matrix, preferred_element_type=jnp.float32) * up_scaling
        gate_part = jnp.dot(mixed, gate_matrix, preferred_element_type=jnp.float32) * gate_scaling
        unit_values = (up_part * jax.nn.silu(gate_part)).astype(jnp.bfloat16)
        mlp_sum = split_sum(unit_values, down_matrix)
        mixed_rows = mixed.astype(jnp.float32)
        return renorm(mixed_rows + feedforward_rate * (renorm(mlp_sum) - mixed_rows)).astype(jnp.bfloat16)
    outputs = lax.map(one_group, (hidden.reshape(N_DP, GROUP_TOKENS, MODEL_WIDTH), lengths, request_prompt, request_adapter))
    return outputs.reshape(TOKENS, MODEL_WIDTH)
```

```python
import functools
import math

import jax
import jax.numpy as jnp
from jax import lax
from jax.experimental import pallas as pl
from jax.experimental.pallas import tpu as pltpu
from jax.sharding import PartitionSpec as P

MESH = pl.DeviceIdType.MESH
D = 1280
HW = 64
RANK = 16
NREQ = 8
PREFIX = 256
NT = 16
NZ = 8
ROWS = 128
GROUP = 2048
EPS = 1e-06
F32 = jnp.float32
BF16 = jnp.bfloat16
NT_DIMS = (((1,), (1,)), ((), ()))


def place():
    dp = lax.axis_index("dp")
    t = lax.axis_index("tensor")
    return dp, t, t // 2, t % 2


def delta(i):
    half = (i + 1) // 2
    odd = i % 2
    return half * (1 - 2 * odd)


def at_z(z, d):
    return (z + d + NZ) % NZ


class Ring:
    def __init__(self, chunks, zsend, zrecv, psend, precv):
        self.dp, self.t, self.z, self.c = place()
        self.chunks, self.zsend, self.zrecv = chunks, zsend, zrecv
        self.psend, self.precv = psend, precv
        self.started = []
        self.next = (self.dp, at_z(self.z, 1) * 2 + self.c), (self.dp, at_z(self.z, -1) * 2 + self.c)
        self.other = (self.dp, self.z * 2 + (1 - self.c))

    def spot(self, k, block):
        buf, _, r0, n = self.chunks[k]
        return buf.at[block, pl.ds(r0, n)]

    def ring_copy(self, way, step, k, src, block):
        return pltpu.make_async_remote_copy(
            src_ref=src, dst_ref=self.spot(k, block),
            send_sem=self.zsend.at[way, step - 1, k], recv_sem=self.zrecv.at[way, step - 1, k],
            device_id=self.next[way], device_id_type=MESH)

    def core_copy(self, i, k, src, block):
        return pltpu.make_async_remote_copy(
            src_ref=src, dst_ref=self.spot(k, block),
            send_sem=self.psend.at[i, k], recv_sem=self.precv.at[i, k],
            device_id=self.other, device_id_type=MESH)

    def go(self, copy):
        copy.start()
        self.started.append(copy)

    def source(self, k):
        _, src, r0, n = self.chunks[k]
        return src.at[pl.ds(r0, n)]

    def first(self):
        for k in range(len(self.chunks)):
            for way in range(2):
                self.go(self.ring_copy(way, 1, k, self.source(k), self.t))
        for k in range(len(self.chunks)):
            self.go(self.core_copy(0, k, self.source(k), self.t))

    def step(self, s):
        for k in range(len(self.chunks)):
            for way in range(2):
                if s == 4 and k % 2 != way:
                    continue
                block = at_z(self.z, -s if way == 0 else s) * 2 + self.c
                here = self.spot(k, block)
                self.ring_copy(way, s, k, here, block).wait_recv()
                if s < 3 or (s == 3 and k % 2 == way):
                    self.go(self.ring_copy(way, s + 1, k, here, block))
                i = 7 if s == 4 else (2 * s - 1 if way == 0 else 2 * s)
                self.go(self.core_copy(i, k, here, block))

    def from_core(self, i):
        block = at_z(self.z, delta(i)) * 2 + (1 - self.c)
        for k in range(len(self.chunks)):
            self.core_copy(i, k, self.spot(k, block), block).wait_recv()

    def drain(self):
        for copy in self.started:
            copy.wait_send()


class Plane:
    def __init__(self, number, first_axis, src, buf, send, recv, local):
        dp, t, _, _ = place()
        x, y = dp // 4, dp % 4
        self.src, self.buf, self.n, self.send, self.recv, self.local = src, buf, number, send, recv, local
        self.a, self.b = (x, y) if first_axis == 0 else (y, x)

        def device(a, b):
            return (a * 4 + b if first_axis == 0 else b * 4 + a), t

        up_a, down_a = (self.a + 1) % 4, (self.a + 3) % 4
        up_b, down_b = (self.b + 1) % 4, (self.b + 3) % 4
        self.lo_a, self.hi_a, self.lo_b, self.hi_b = down_a, up_a, down_b, up_b
        self.dev_a = device(up_a, self.b), device(down_a, self.b)
        self.dev_b = device(self.a, up_b), device(self.a, down_b)
        self.started = []

    def copy(self, k, src, dst, dev):
        return pltpu.make_async_remote_copy(
            src_ref=src, dst_ref=dst, send_sem=self.send.at[self.n, k], recv_sem=self.recv.at[self.n, k],
            device_id=dev, device_id_type=MESH)

    def go(self, k, src, dst, dev):
        c = self.copy(k, src, dst, dev)
        c.start()
        self.started.append(c)

    def got(self, k, dst):
        self.copy(k, dst, dst, self.dev_a[0]).wait_recv()

    def halves(self, ref):
        n = ref.shape[0] // 2
        return ref.at[pl.ds(0, n)], ref.at[pl.ds(n, n)]

    def one(self):
        mine = self.buf.at[self.b, self.a]
        self.own = pltpu.make_async_copy(self.src, mine, self.local.at[self.n])
        self.own.start()
        self.go(0, self.src, mine, self.dev_a[0])
        self.go(1, self.src, mine, self.dev_a[1])

    def two(self):
        lo, hi = self.buf.at[self.b, self.lo_a], self.buf.at[self.b, self.hi_a]
        self.got(0, lo)
        self.go(2, self.halves(lo)[0], self.halves(lo)[0], self.dev_a[0])
        self.got(1, hi)
        self.go(3, self.halves(hi)[1], self.halves(hi)[1], self.dev_a[1])

    def three(self):
        far = self.buf.at[self.b, (self.a + 2) % 4]
        self.got(2, self.halves(far)[0])
        self.got(3, self.halves(far)[1])
        self.own.wait()
        row = self.buf.at[self.b]
        self.go(4, row, row, self.dev_b[0])
        self.go(5, row, row, self.dev_b[1])

    def four(self):
        lo, hi = self.buf.at[self.lo_b], self.buf.at[self.hi_b]
        self.got(4, lo)
        self.go(6, self.halves(lo)[0], self.halves(lo)[0], self.dev_b[0])
        self.got(5, hi)
        self.go(7, self.halves(hi)[1], self.halves(hi)[1], self.dev_b[1])

    def five(self):
        far = self.buf.at[(self.b + 2) % 4]
        self.got(6, self.halves(far)[0])
        self.got(7, self.halves(far)[1])

    def drain(self):
        for c in self.started:
            c.wait_send()


def greet(peers):
    barrier = pltpu.get_barrier_semaphore()
    for peer in peers:
        pl.semaphore_signal(barrier, inc=1, device_id=peer, device_id_type=MESH)
    pl.semaphore_wait(barrier, len(peers))


def lanes(shape):
    return lax.broadcasted_iota(jnp.int32, shape, len(shape) - 1)


def row_starts(len_ref, first_row, shape):
    rows = first_row + lax.broadcasted_iota(jnp.int32, shape, 0)
    end = jnp.int32(0)
    req = jnp.zeros(shape, jnp.int32)
    start = jnp.zeros(shape, jnp.int32)
    for r in range(NREQ):
        size = len_ref[0, r]
        end = end + size
        past = rows >= end
        req = req + jnp.where(past, 1, 0)
        start = start + jnp.where(past, size, 0)
    return rows, req, start


def gather_kernel(h_ref, o_ref, pg_ref, up_ref, dn_ref, w_ref, gain_ref, len_ref, ra_ref, rp_ref, pt_ref,
                  q_out, kv_out, pkv_out, o_out,
                  gh, go, pb, ub, db, sd, su, trig,
                  zsend, zrecv, psend, precv, xsend, xrecv, local, dsend, drecv):
    dp, t, z, c = place()
    x, y = dp // 4, dp % 4
    greet([
        (dp, at_z(z, 1) * 2 + c), (dp, at_z(z, -1) * 2 + c), (dp, z * 2 + (1 - c)),
        (((x + 1) % 4) * 4 + y, t), (((x + 3) % 4) * 4 + y, t),
        (x * 4 + (y + 1) % 4, t), (x * 4 + (y + 3) % 4, t),
    ])
    ring = Ring([(gh, h_ref, 0, 64), (gh, h_ref, 64, 64), (go, o_ref, 0, 32), (go, o_ref, 32, 32)],
                zsend, zrecv, psend, precv)
    planes = [
        Plane(0, 1, dn_ref.at[pl.ds(2 * c, 2)], db.at[c], xsend, xrecv, local),
        Plane(1, 0, pg_ref, pb, xsend, xrecv, local),
        Plane(2, 1, up_ref, ub, xsend, xrecv, local),
    ]
    for p in planes:
        p.one()
    ring.first()
    own_h = pltpu.make_async_copy(h_ref, gh.at[t], local.at[3])
    own_h.start()
    own_o = pltpu.make_async_copy(o_ref, go.at[t], local.at[4])
    own_o.start()
    for p in planes:
        p.two()
    for p in planes:
        p.three()

    lane = lanes((256, 128))
    frequency = jnp.exp((lane % 32).astype(F32) * (-2.0 * math.log(10000.0) / HW))
    quarter = jnp.where(lane < HW, 0.0, 0.5 * math.pi)

    @pl.loop(0, NZ)
    def _(b):
        rows, _, start = row_starts(len_ref, b * 256, (256, 128))
        angle = (rows - start + PREFIX).astype(F32) * frequency
        trig[b] = jnp.cos(angle - quarter)

    own_h.wait()
    own_o.wait()
    ring.step(1)
    for p in planes:
        p.four()
    ring.step(2)
    for p in planes:
        p.five()
    swap = pltpu.make_async_remote_copy(
        src_ref=db.at[c], dst_ref=db.at[c], send_sem=dsend, recv_sem=drecv,
        device_id=(dp, z * 2 + (1 - c)), device_id_type=MESH)
    swap.start()

    gain = gain_ref[...]
    low = lane < HW

    def unit(v):
        total = jnp.sum(jnp.where(low, v * v, 0.0), axis=1, keepdims=True)
        return v * lax.rsqrt(total + EPS) * gain

    @pl.loop(0, NREQ)
    def _(r):
        prompt = rp_ref[0, r]
        for j in range(4):
            page = pt_ref[prompt, j]
            owner = page // 4
            raw = pb[owner % 4, owner // 4, page % 4].astype(F32)
            low_p = lanes((64, 128)) < HW
            total = jnp.sum(jnp.where(low_p, raw * raw, 0.0), axis=1, keepdims=True)
            unit_key = raw * lax.rsqrt(total + EPS) * gain
            pkv_out[pl.ds(pl.multiple_of(r * PREFIX + j * 64, 64), 64), :] = jnp.where(
                low_p, unit_key, raw).astype(BF16)

    pltpu.make_async_remote_copy(
        src_ref=db.at[1 - c], dst_ref=db.at[1 - c], send_sem=dsend, recv_sem=drecv,
        device_id=(dp, z * 2 + (1 - c)), device_id_type=MESH).wait_recv()
    for r in range(NREQ):
        adapter = ra_ref[0, r]
        owner = adapter // 4
        within = adapter % 4
        sd[r * RANK:(r + 1) * RANK, :] = db[within // 2, owner // 4, owner % 4, within % 2]
        su[r * RANK:(r + 1) * RANK, :] = ub[owner // 4, owner % 4, within]

    def project(i):
        ring.from_core(i)
        zb = at_z(z, delta(i))
        values = gh[pl.ds(zb * 2, 2)].reshape(256, D)
        _, req, _ = row_starts(len_ref, zb * 256, (256, 128))
        middle = lax.dot_general(values, sd[...], NT_DIMS, preferred_element_type=F32)
        middle = jnp.where(lane // RANK == req, middle, 0.0).astype(BF16)
        both = jnp.dot(values, w_ref[...], preferred_element_type=F32) + 0.5 * jnp.dot(
            middle, su[...], preferred_element_type=F32)
        wave = trig[zb]
        cosine = jnp.where(low, wave, 1.0)
        sine = pltpu.roll(wave, HW, 1)
        sine = jnp.where(lane < 32, -sine, jnp.where(low, sine, 0.0))

        def rotate(v):
            other = jnp.where(lane < 32, pltpu.roll(v, 96, 1), pltpu.roll(v, 32, 1))
            return v * cosine + other * sine

        query, key_value = both[:, :128], both[:, 128:]
        rows = pl.ds(pl.multiple_of(zb * 256, 256), 256)
        q_out[rows, :] = unit(rotate(query)).astype(BF16) * jnp.asarray(8.0, BF16)
        kv_out[rows, :] = jnp.where(low, unit(rotate(key_value)), key_value).astype(BF16)

    pl.loop(0, 3)(project)
    ring.step(3)
    pl.loop(3, 5)(project)
    ring.step(4)
    pl.loop(5, 8)(project)
    out = pltpu.make_async_copy(go, o_out, local.at[5])
    out.start()
    ring.drain()
    for p in planes:
        p.drain()
    swap.wait_send()
    out.wait()


def attend_kernel(q_ref, kv_ref, pkv_ref, len_ref, out_ref, acc):
    lane = lanes((256, 128))
    low_key = lanes((256, 128)) < HW

    @pl.loop(0, NZ)
    def _(i):
        first = i * 256
        query = q_ref[pl.ds(pl.multiple_of(first, 256), 256), :]
        rows, _, start = row_starts(len_ref, first, (256, 256))
        end = jnp.int32(0)
        request_lo, request_hi, start_lo = jnp.int32(0), jnp.int32(0), jnp.int32(0)
        for r in range(NREQ):
            size = len_ref[0, r]
            end = end + size
            request_lo = request_lo + jnp.where(first >= end, 1, 0)
            start_lo = start_lo + jnp.where(first >= end, size, 0)
            request_hi = request_hi + jnp.where(first + 255 >= end, 1, 0)
        acc[...] = jnp.zeros_like(acc)

        def add(keys, allowed):
            score = lax.dot_general(query, keys, NT_DIMS, preferred_element_type=F32)
            weight = jnp.where(allowed, jnp.exp(score), 0.0).astype(BF16)
            ones = jnp.where(low_key, jnp.asarray(1.0, BF16), keys)
            acc[...] += jnp.dot(weight, ones, preferred_element_type=F32)

        def prefix(r, begins):
            add(pkv_ref[pl.ds(pl.multiple_of(r * PREFIX, PREFIX), PREFIX), :], start == begins)
            return begins + len_ref[0, r]

        lax.fori_loop(request_lo, request_hi + 1, prefix, start_lo)

        def own(j, carry):
            column = j * 256 + lanes((256, 256))
            add(kv_ref[pl.ds(pl.multiple_of(j * 256, 256), 256), :], (column >= start) & (column <= rows))
            return carry

        lax.fori_loop(start_lo // 256, i + 1, own, 0)
        total = acc[...]
        result = total / pltpu.roll(total, HW, 1)
        for b in range(2):
            top, bottom = result[b * 128:b * 128 + 64], result[b * 128 + 64:b * 128 + 128]
            out_ref[2 * i + b] = jnp.where(lanes((64, 128)) >= HW, top, pltpu.roll(bottom, HW, 1)).astype(BF16)


def renorm(v):
    return v * lax.rsqrt(jnp.mean(v * v, axis=-1, keepdims=True) + EPS)


def mix_kernel(attn_ref, o_ref, h_ref, wu_ref, wg_ref, wd_ref, su_ref, sg_ref, ra_ref, rf_ref, out_ref,
               heads, lhs, om, wu, wg, wd, mixed, part, peer, rr, rl, sr, sl,
               asend, arecv, zsend, zrecv, psend, precv, qsend, qrecv, rsend, rrecv, local):
    dp, t, z, c = place()
    loads = [pltpu.make_async_copy(a, b, local.at[n])
             for n, (a, b) in enumerate([(o_ref, om), (wu_ref, wu), (wg_ref, wg), (wd_ref, wd)])]
    for copy in loads:
        copy.start()
    greet([(dp, (t + n) % NT) for n in range(1, NT)])
    started = []
    order = [8, 9, 7, 10, 6, 11, 5, 12, 4, 13, 3, 14, 2, 15, 1]
    for n in order:
        to = (t + n) % NT
        copy = pltpu.make_async_remote_copy(
            src_ref=attn_ref.at[to], dst_ref=heads.at[t], send_sem=asend.at[n], recv_sem=arecv.at[n],
            device_id=(dp, to), device_id_type=MESH)
        copy.start()
        started.append(copy)
    own = pltpu.make_async_copy(attn_ref.at[t], heads.at[t], local.at[4])
    own.start()
    own.wait()
    for n in order:
        frm = (t + NT - n) % NT
        pltpu.make_async_remote_copy(
            src_ref=attn_ref.at[t], dst_ref=heads.at[frm], send_sem=asend.at[n], recv_sem=arecv.at[n],
            device_id=(dp, frm), device_id_type=MESH).wait_recv()
    high = lanes((64, 128)) >= HW
    for j in range(NT // 2):
        even, odd = heads[2 * j].astype(F32), heads[2 * j + 1].astype(F32)
        cols = slice(128 * j, 128 * j + 128)
        lhs[0:64, cols] = jnp.where(high, odd, pltpu.roll(even, HW, 1)).astype(BF16)
        lhs[64:128, cols] = jnp.where(high, pltpu.roll(odd, HW, 1), even).astype(BF16)
    loads[0].wait()
    attn_sum = jnp.dot(lhs[...], om[...], preferred_element_type=F32)
    base = h_ref[...].astype(F32)
    mine = renorm(base + ra_ref[...] * (renorm(attn_sum) - base)).astype(BF16)
    mixed[t] = mine
    ring = Ring([(mixed, mixed.at[t], 0, 64), (mixed, mixed.at[t], 64, 64)], zsend, zrecv, psend, precv)
    ring.first()
    for copy in loads[1:]:
        copy.wait()

    def swap(i, zb):
        return pltpu.make_async_remote_copy(
            src_ref=part.at[zb * 2 + (1 - c)], dst_ref=peer.at[zb], send_sem=qsend.at[i], recv_sem=qrecv.at[i],
            device_id=(dp, z * 2 + (1 - c)), device_id_type=MESH)

    def feed(i):
        ring.from_core(i)
        zb = at_z(z, delta(i))
        values = mixed[pl.ds(zb * 2, 2)].reshape(256, D)
        up = jnp.dot(values, wu[...], preferred_element_type=F32) * su_ref[...]
        gate = jnp.dot(values, wg[...], preferred_element_type=F32) * sg_ref[...]
        units = (up * (gate / (1.0 + jnp.exp(-gate)))).astype(BF16)
        result = jnp.dot(units, wd[...], preferred_element_type=F32).astype(BF16)
        part[pl.ds(zb * 2, 2)] = result.reshape(2, ROWS, D)
        swap(i, zb).start()

    pl.loop(0, 1)(feed)
    ring.step(1)
    pl.loop(1, 3)(feed)
    ring.step(2)
    pl.loop(3, 5)(feed)
    ring.step(3)
    pl.loop(5, 7)(feed)
    ring.step(4)
    pl.loop(7, 8)(feed)

    def local_sum(zb, k):
        rows = pl.ds(64 * k, 64)
        return part[zb * 2 + c, rows].astype(F32) + peer[zb, rows].astype(F32)

    def rs_copy(way, d, k, src):
        dst = (rr if way == 0 else rl).at[d - 1, pl.ds(64 * k, 64)]
        dev = (dp, at_z(z, 1 if way == 0 else -1) * 2 + c)
        return pltpu.make_async_remote_copy(
            src_ref=src, dst_ref=dst, send_sem=rsend.at[way, d - 1, k], recv_sem=rrecv.at[way, d - 1, k],
            device_id=dev, device_id_type=MESH)

    for d in (4, 3, 2, 1):
        swap(2 * d - 1, at_z(z, -d)).wait_recv()
        if d < 4:
            swap(2 * d, at_z(z, d)).wait_recv()
        for k in range(2):
            for way in range(2):
                if d == 4 and k != way:
                    continue
                rows = pl.ds(64 * k, 64)
                recv, sent = (rr, sr) if way == 0 else (rl, sl)
                value = local_sum(at_z(z, d if way == 0 else -d), k)
                if d < 3 or (d == 3 and k == way):
                    rs_copy(way, d + 1, k, sent.at[d, rows]).wait_recv()
                    value = value + recv[d, rows].astype(F32)
                sent[d - 1, rows] = value.astype(BF16)
                copy = rs_copy(way, d, k, sent.at[d - 1, rows])
                copy.start()
                started.append(copy)
    swap(0, z).wait_recv()
    for k in range(2):
        rows = pl.ds(64 * k, 64)
        value = local_sum(z, k)
        for way in range(2):
            rs_copy(way, 1, k, (sr if way == 0 else sl).at[0, rows]).wait_recv()
        value = value + rr[0, rows].astype(F32) + rl[0, rows].astype(F32)
        base = mixed[t, rows].astype(F32)
        out_ref[rows, :] = renorm(base + rf_ref[...] * (renorm(value) - base)).astype(BF16)
    ring.drain()
    for copy in started:
        copy.wait_send()
    for i in range(NZ):
        swap(i, at_z(z, delta(i))).wait_send()


VM = pl.BlockSpec(memory_space=pltpu.VMEM)
SM = pl.BlockSpec(memory_space=pltpu.SMEM)
HB = pl.BlockSpec(memory_space=pl.ANY)
DMA = pltpu.SemaphoreType.DMA


def local(hidden, lengths, request_prompt, request_adapter, prompt_page_table, prefix_page_cache,
          query_key_value_weight, adapter_down, adapter_up, attention_scale, output_matrix, attention_rate,
          up_matrix, gate_matrix, up_scaling, gate_scaling, down_matrix, feedforward_rate):
    def spread(m):
        return jnp.concatenate([m[..., :HW], jnp.zeros_like(m[..., :HW]), m[..., HW:]], axis=-1)

    weight = spread(query_key_value_weight)
    up = spread(adapter_up)
    down = jnp.swapaxes(adapter_down, 1, 2)
    gain = jnp.concatenate([attention_scale, jnp.ones_like(attention_scale)]).reshape(1, 128)
    queries, key_values, prefix, matrix = pl.pallas_call(
        gather_kernel,
        out_shape=(
            jax.ShapeDtypeStruct((GROUP, 128), BF16),
            jax.ShapeDtypeStruct((GROUP, 128), BF16),
            jax.ShapeDtypeStruct((NREQ * PREFIX, 128), BF16),
            jax.ShapeDtypeStruct((NT, HW, D), BF16),
        ),
        in_specs=[HB, HB, HB, HB, HB, VM, VM, SM, SM, SM, SM],
        out_specs=(VM, VM, VM, HB),
        scratch_shapes=[
            pltpu.VMEM((NT, ROWS, D), BF16),
            pltpu.VMEM((NT, HW, D), BF16),
            pltpu.VMEM((4, 4, 4, 64, 128), BF16),
            pltpu.VMEM((4, 4, 4, RANK, 256), BF16),
            pltpu.VMEM((2, 4, 4, 2, RANK, D), BF16),
            pltpu.VMEM((128, D), BF16),
            pltpu.VMEM((128, 256), BF16),
            pltpu.VMEM((NZ, 256, 128), F32),
            DMA((2, 4, 4)), DMA((2, 4, 4)), DMA((8, 4)), DMA((8, 4)),
            DMA((3, 8)), DMA((3, 8)), DMA((6,)), DMA, DMA,
        ],
        compiler_params=pltpu.CompilerParams(
            collective_id=0, has_side_effects=True, vmem_limit_bytes=60 * 2**20),
        name="gather_project",
    )(hidden, output_matrix, prefix_page_cache, up, down, weight, gain,
      lengths, request_adapter, request_prompt, prompt_page_table)
    attn = pl.pallas_call(
        attend_kernel,
        out_shape=jax.ShapeDtypeStruct((NT, 64, 128), BF16),
        in_specs=[VM, VM, VM, SM],
        out_specs=VM,
        scratch_shapes=[pltpu.VMEM((256, 128), F32)],
        name="attend",
    )(queries, key_values, prefix, lengths)
    return pl.pallas_call(
        mix_kernel,
        out_shape=jax.ShapeDtypeStruct((ROWS, D), BF16),
        in_specs=[VM, HB, VM, HB, HB, HB, VM, VM, VM, VM],
        out_specs=VM,
        scratch_shapes=[
            pltpu.VMEM((NT, 64, 128), BF16),
            pltpu.VMEM((ROWS, NT * HW), BF16),
            pltpu.VMEM((NT * HW, D), BF16),
            pltpu.VMEM((D, 320), BF16),
            pltpu.VMEM((D, 320), BF16),
            pltpu.VMEM((320, D), BF16),
            pltpu.VMEM((NT, ROWS, D), BF16),
            pltpu.VMEM((NT, ROWS, D), BF16),
            pltpu.VMEM((NZ, ROWS, D), BF16),
            pltpu.VMEM((4, ROWS, D), BF16), pltpu.VMEM((4, ROWS, D), BF16),
            pltpu.VMEM((4, ROWS, D), BF16), pltpu.VMEM((4, ROWS, D), BF16),
            DMA((16,)), DMA((16,)), DMA((2, 4, 2)), DMA((2, 4, 2)), DMA((8, 2)), DMA((8, 2)),
            DMA((8,)), DMA((8,)), DMA((2, 4, 2)), DMA((2, 4, 2)), DMA((5,)),
        ],
        compiler_params=pltpu.CompilerParams(
            collective_id=1, has_side_effects=True, vmem_limit_bytes=60 * 2**20),
        name="mix_feed",
    )(attn, matrix.reshape(NT * HW, D), hidden, up_matrix, gate_matrix, down_matrix,
      up_scaling.reshape(1, -1), gate_scaling.reshape(1, -1),
      attention_rate.reshape(1, -1), feedforward_rate.reshape(1, -1))


def solution(mesh):
    placed = (
        P(("dp", "tensor"), None),
        P("dp", None),
        P("dp", None),
        P("dp", None),
        P(),
        P("dp", None, "tensor"),
        P(None, "tensor"),
        P("dp", None, None),
        P("dp", None, "tensor"),
        P("tensor"),
        P("tensor", None),
        P(),
        P(None, "tensor"),
        P(None, "tensor"),
        P("tensor"),
        P("tensor"),
        P("tensor", None),
        P(),
    )
    return jax.shard_map(
        local, mesh=mesh, in_specs=placed, out_specs=P(("dp", "tensor"), None), check_vma=False
    )
```

```python
import functools
import math

import jax
import jax.numpy as jnp
from jax import lax
from jax.experimental import pallas as pl
from jax.experimental.pallas import tpu as pltpu
from jax.sharding import PartitionSpec as P

MESH = pl.DeviceIdType.MESH
D = 1280
HW = 64
RANK = 16
NREQ = 8
PREFIX = 256
NT = 16
NZ = 8
ROWS = 128
GROUP = 2048
EPS = 1e-06
F32 = jnp.float32
BF16 = jnp.bfloat16
NT_DIMS = (((1,), (1,)), ((), ()))


def place():
    dp = lax.axis_index("dp")
    t = lax.axis_index("tensor")
    return dp, t, t // 2, t % 2


def delta(i):
    half = (i + 1) // 2
    odd = i % 2
    return half * (1 - 2 * odd)


def at_z(z, d):
    return (z + d + NZ) % NZ


class Ring:
    def __init__(self, chunks, zsend, zrecv, psend, precv):
        self.dp, self.t, self.z, self.c = place()
        self.chunks, self.zsend, self.zrecv = chunks, zsend, zrecv
        self.psend, self.precv = psend, precv
        self.started = []
        self.next = (self.dp, at_z(self.z, 1) * 2 + self.c), (self.dp, at_z(self.z, -1) * 2 + self.c)
        self.other = (self.dp, self.z * 2 + (1 - self.c))

    def spot(self, k, block):
        buf, _, r0, n = self.chunks[k]
        return buf.at[block, pl.ds(r0, n)]

    def ring_copy(self, way, step, k, src, block):
        return pltpu.make_async_remote_copy(
            src_ref=src, dst_ref=self.spot(k, block),
            send_sem=self.zsend.at[way, step - 1, k], recv_sem=self.zrecv.at[way, step - 1, k],
            device_id=self.next[way], device_id_type=MESH)

    def core_copy(self, i, k, src, block):
        return pltpu.make_async_remote_copy(
            src_ref=src, dst_ref=self.spot(k, block),
            send_sem=self.psend.at[i, k], recv_sem=self.precv.at[i, k],
            device_id=self.other, device_id_type=MESH)

    def go(self, copy):
        copy.start()
        self.started.append(copy)

    def source(self, k):
        _, src, r0, n = self.chunks[k]
        return src.at[pl.ds(r0, n)]

    def first(self):
        for ks in self.order():
            for way in range(2):
                self.go(self.ring_copy(way, 1, ks[way], self.source(ks[way]), self.t))
        for k in range(len(self.chunks)):
            self.go(self.core_copy(0, k, self.source(k), self.t))

    def order(self):
        n = len(self.chunks)
        return [(k, (k + n // 2) % n) for k in range(n)]

    def step(self, s):
        for n, ks in enumerate(self.order()):
            for way in range(2):
                k, far = ks[way], n < len(self.chunks) // 2
                if s == 4 and not far:
                    continue
                block = at_z(self.z, -s if way == 0 else s) * 2 + self.c
                here = self.spot(k, block)
                self.ring_copy(way, s, k, here, block).wait_recv()
                if s < 3 or (s == 3 and far):
                    self.go(self.ring_copy(way, s + 1, k, here, block))
                i = 7 if s == 4 else (2 * s - 1 if way == 0 else 2 * s)
                self.go(self.core_copy(i, k, here, block))

    def from_core(self, i):
        block = at_z(self.z, delta(i)) * 2 + (1 - self.c)
        for k in range(len(self.chunks)):
            self.core_copy(i, k, self.spot(k, block), block).wait_recv()

    def drain(self):
        for copy in self.started:
            copy.wait_send()


class Plane:
    def __init__(self, number, first_axis, src, buf, send, recv, local):
        dp, t, _, _ = place()
        x, y = dp // 4, dp % 4
        self.src, self.buf, self.n, self.send, self.recv, self.local = src, buf, number, send, recv, local
        self.a, self.b = (x, y) if first_axis == 0 else (y, x)

        def device(a, b):
            return (a * 4 + b if first_axis == 0 else b * 4 + a), t

        up_a, down_a = (self.a + 1) % 4, (self.a + 3) % 4
        up_b, down_b = (self.b + 1) % 4, (self.b + 3) % 4
        self.lo_a, self.hi_a, self.lo_b, self.hi_b = down_a, up_a, down_b, up_b
        self.dev_a = device(up_a, self.b), device(down_a, self.b)
        self.dev_b = device(self.a, up_b), device(self.a, down_b)
        self.started = []

    def copy(self, k, src, dst, dev):
        return pltpu.make_async_remote_copy(
            src_ref=src, dst_ref=dst, send_sem=self.send.at[self.n, k], recv_sem=self.recv.at[self.n, k],
            device_id=dev, device_id_type=MESH)

    def go(self, k, src, dst, dev):
        c = self.copy(k, src, dst, dev)
        c.start()
        self.started.append(c)

    def got(self, k, dst):
        self.copy(k, dst, dst, self.dev_a[0]).wait_recv()

    def halves(self, ref):
        if len(ref.shape) == 2:
            n = ref.shape[1] // 2
            return ref.at[:, pl.ds(0, n)], ref.at[:, pl.ds(n, n)]
        n = ref.shape[0] // 2
        return ref.at[pl.ds(0, n)], ref.at[pl.ds(n, n)]

    def one(self):
        mine = self.buf.at[self.b, self.a]
        self.own = pltpu.make_async_copy(self.src, mine, self.local.at[self.n])
        self.own.start()
        self.go(0, self.src, mine, self.dev_a[0])
        self.go(1, self.src, mine, self.dev_a[1])

    def two(self):
        lo, hi = self.buf.at[self.b, self.lo_a], self.buf.at[self.b, self.hi_a]
        self.got(0, lo)
        self.go(2, self.halves(lo)[0], self.halves(lo)[0], self.dev_a[0])
        self.got(1, hi)
        self.go(3, self.halves(hi)[1], self.halves(hi)[1], self.dev_a[1])

    def three(self):
        far = self.buf.at[self.b, (self.a + 2) % 4]
        self.got(2, self.halves(far)[0])
        self.got(3, self.halves(far)[1])
        self.own.wait()
        row = self.buf.at[self.b]
        self.go(4, row, row, self.dev_b[0])
        self.go(5, row, row, self.dev_b[1])

    def four(self):
        lo, hi = self.buf.at[self.lo_b], self.buf.at[self.hi_b]
        self.got(4, lo)
        self.go(6, self.halves(lo)[0], self.halves(lo)[0], self.dev_b[0])
        self.got(5, hi)
        self.go(7, self.halves(hi)[1], self.halves(hi)[1], self.dev_b[1])

    def five(self):
        far = self.buf.at[(self.b + 2) % 4]
        self.got(6, self.halves(far)[0])
        self.got(7, self.halves(far)[1])

    def drain(self):
        for c in self.started:
            c.wait_send()


def greet(peers):
    barrier = pltpu.get_barrier_semaphore()
    for peer in peers:
        pl.semaphore_signal(barrier, inc=1, device_id=peer, device_id_type=MESH)
    pl.semaphore_wait(barrier, len(peers))


def lanes(shape):
    return lax.broadcasted_iota(jnp.int32, shape, len(shape) - 1)


def row_starts(len_ref, first_row, shape):
    rows = first_row + lax.broadcasted_iota(jnp.int32, shape, 0)
    end = jnp.int32(0)
    req = jnp.zeros(shape, jnp.int32)
    start = jnp.zeros(shape, jnp.int32)
    for r in range(NREQ):
        size = len_ref[0, r]
        end = end + size
        past = rows >= end
        req = req + jnp.where(past, 1, 0)
        start = start + jnp.where(past, size, 0)
    return rows, req, start


def gather_kernel(h_ref, o_ref, pg_ref, up_ref, dn_ref, w_ref, gain_ref, len_ref, ra_ref, rp_ref, pt_ref,
                  q_out, kv_out, o_out,
                  gh, go, pb, ub, db, wide, sel, tail, su, gains, trig,
                  zsend, zrecv, psend, precv, xsend, xrecv, local, dsend, drecv):
    dp, t, z, c = place()
    x, y = dp // 4, dp % 4
    greet([
        (dp, at_z(z, 1) * 2 + c), (dp, at_z(z, -1) * 2 + c), (dp, z * 2 + (1 - c)),
        (((x + 1) % 4) * 4 + y, t), (((x + 3) % 4) * 4 + y, t),
        (x * 4 + (y + 1) % 4, t), (x * 4 + (y + 3) % 4, t),
    ])
    ring = Ring([(gh, h_ref, 0, 64), (go, o_ref, 0, 32), (gh, h_ref, 64, 64), (go, o_ref, 32, 32)],
                zsend, zrecv, psend, precv)
    planes = []
    for half in range(2):
        for src, buf in ((dn_ref.at[2 * c + half], db.at[c, half]),
                         (pg_ref.at[pl.ds(2 * half, 2)], pb.at[half]),
                         (up_ref.at[pl.ds(2 * half, 2)], ub.at[half])):
            planes.append(Plane(len(planes), half, src, buf, xsend, xrecv, local))
    ring.first()
    for p in planes:
        p.one()
    own_h = pltpu.make_async_copy(h_ref, gh.at[t], local.at[6])
    own_h.start()
    own_o = pltpu.make_async_copy(o_ref, go.at[t], local.at[7])
    own_o.start()
    for p in planes:
        p.two()
    for p in planes:
        p.three()

    lane = lanes((256, 128))
    low = lane < HW
    gains[...] = jnp.ones_like(gains)
    gains[:, 0:HW] = jnp.broadcast_to(gain_ref[...].reshape(1, HW), (8, HW))
    gain = gains[0:1, :]
    wide[128:192, :] = w_ref[0:HW, :]
    wide[192:256, :] = jnp.zeros((HW, D), BF16)
    wide[256:384, :] = w_ref[HW:3 * HW, :]
    tail[...] = jnp.zeros_like(tail)
    frequency = jnp.exp((lane % 32).astype(F32) * (-2.0 * math.log(10000.0) / HW))
    quarter = jnp.where(low, 0.0, 0.5 * math.pi)

    @pl.loop(0, NZ)
    def _(b):
        rows, _, start = row_starts(len_ref, b * 256, (256, 128))
        angle = (rows - start + PREFIX).astype(F32) * frequency
        trig[b] = jnp.cos(angle - quarter)

    own_h.wait()
    own_o.wait()
    ring.step(1)
    for p in planes:
        p.four()
    ring.step(2)
    for p in planes:
        p.five()
    swaps = []
    for half in range(2):
        swap = pltpu.make_async_remote_copy(
            src_ref=db.at[c, half], dst_ref=db.at[c, half], send_sem=dsend.at[half], recv_sem=drecv.at[half],
            device_id=(dp, z * 2 + (1 - c)), device_id_type=MESH)
        swap.start()
        swaps.append(swap)

    def unit(v):
        total = jnp.sum(jnp.where(low, v * v, 0.0), axis=1, keepdims=True)
        return v * lax.rsqrt(total + EPS) * gain

    def slot(owner, half):
        a, b = owner // 4, owner % 4
        return b + half * (a - b), a + half * (b - a)

    @pl.loop(0, NREQ)
    def _(r):
        prompt = rp_ref[0, r]
        for j in range(4):
            page = pt_ref[j, prompt]
            half = (page % 4) // 2
            major, minor = slot(page // 4, half)
            raw = pb[half, major, minor, page % 2].astype(F32)
            low_p = lanes((64, 128)) < HW
            total = jnp.sum(jnp.where(low_p, raw * raw, 0.0), axis=1, keepdims=True)
            unit_key = raw * lax.rsqrt(total + EPS) * gain
            kv_out[pl.ds(pl.multiple_of(r * PREFIX + j * 64, 64), 64), :] = jnp.where(
                low_p, unit_key, raw).astype(BF16)

    for half in range(2):
        pltpu.make_async_remote_copy(
            src_ref=db.at[1 - c, half], dst_ref=db.at[1 - c, half],
            send_sem=dsend.at[half], recv_sem=drecv.at[half],
            device_id=(dp, z * 2 + (1 - c)), device_id_type=MESH).wait_recv()
    for r in range(NREQ):
        adapter = ra_ref[0, r]
        within = adapter % 4
        major, minor = slot(adapter // 4, within % 2)
        wide[r * RANK:(r + 1) * RANK, :] = db[within // 2, within % 2, major, minor]
        major, minor = slot(adapter // 4, within // 2)
        sel[r * RANK:(r + 1) * RANK, :] = ub[within // 2, major, minor, within % 2].astype(F32)
    first = sel[:, 0:128]
    tail[:, 0:HW] = sel[:, 128:192]
    low_s = lanes((128, 128)) < HW
    su[:, 0:128] = jnp.where(low_s, first, 0.0).astype(BF16)
    su[:, 128:256] = jnp.where(low_s, pltpu.roll(first, HW, 1), pltpu.roll(tail[...], HW, 1)).astype(BF16)

    def project(i):
        ring.from_core(i)
        zb = at_z(z, delta(i))
        values = gh[pl.ds(zb * 2, 2)].reshape(256, D)
        _, req, _ = row_starts(len_ref, zb * 256, (256, 128))
        every = lax.dot_general(values, wide[...], NT_DIMS, preferred_element_type=F32)
        middle = jnp.where(lane // RANK == req, every[:, 0:128], 0.0).astype(BF16)
        both = every[:, 128:384] + 0.5 * jnp.dot(middle, su[...], preferred_element_type=F32)
        wave = trig[zb]
        cosine = jnp.where(low, wave, 1.0)
        sine = pltpu.roll(wave, HW, 1)
        sine = jnp.where(lane < 32, -sine, jnp.where(low, sine, 0.0))

        def rotate(v):
            other = jnp.where(lane < 32, pltpu.roll(v, 96, 1), pltpu.roll(v, 32, 1))
            return v * cosine + other * sine

        query, key_value = both[:, :128], both[:, 128:]
        row = pl.multiple_of(zb * 256, 256)
        q_out[pl.ds(row, 256), :] = unit(rotate(query)).astype(BF16) * jnp.asarray(8.0, BF16)
        kv_out[pl.ds(row + NREQ * PREFIX, 256), :] = jnp.where(
            low, unit(rotate(key_value)), key_value).astype(BF16)

    pl.loop(0, 3)(project)
    ring.step(3)
    pl.loop(3, 5)(project)
    ring.step(4)
    pl.loop(5, 8)(project)
    out = pltpu.make_async_copy(go, o_out, local.at[8])
    out.start()
    ring.drain()
    for p in planes:
        p.drain()
    for swap in swaps:
        swap.wait_send()
    out.wait()


TILES = 2


def attend_kernel(q_ref, kv_ref, len_ref, out_ref, acc, begins):
    low = lanes((256, 128)) < HW
    begin = jnp.int32(0)
    for r in range(NREQ):
        begins[r] = begin
        begin = begin + len_ref[0, r]
    for r in range(NREQ, 2 * NREQ):
        begins[r] = jnp.int32(0)

    @pl.loop(0, NZ)
    def _(i):
        first = i * 256
        query = q_ref[pl.ds(pl.multiple_of(first, 256), 256), :]
        rows, _, start = row_starts(len_ref, first, (256, 256))
        end = jnp.int32(0)
        request_lo, request_hi, start_lo = jnp.int32(0), jnp.int32(0), jnp.int32(0)
        for r in range(NREQ):
            size = len_ref[0, r]
            end = end + size
            request_lo = request_lo + jnp.where(first >= end, 1, 0)
            start_lo = start_lo + jnp.where(first >= end, size, 0)
            request_hi = request_hi + jnp.where(first + 255 >= end, 1, 0)
        acc[...] = jnp.zeros_like(acc)
        lowest = start_lo // 256
        prefixes = request_hi + 1 - request_lo
        count = prefixes + i + 1 - lowest
        lane = lanes((256, 256))

        @pl.loop(0, (count + TILES - 1) // TILES)
        def _(n):
            total = None
            for u in range(TILES):
                m = jnp.minimum(n * TILES + u, count - 1)
                shared = m < prefixes
                tile = jnp.where(shared, request_lo + m, NREQ + lowest + m - prefixes)
                base = jnp.where(shared, begins[tile], (tile - NREQ) * 256)
                base = jnp.where(n * TILES + u < count, base, 2 * GROUP)
                column = jnp.where(shared, 0, 1) * lane + base
                keys = kv_ref[pl.ds(pl.multiple_of(tile * 256, 256), 256), :]
                score = lax.dot_general(query, keys, NT_DIMS, preferred_element_type=F32)
                weight = jnp.where((column >= start) & (column <= rows), jnp.exp(score), 0.0).astype(BF16)
                ones = jnp.where(low, jnp.asarray(1.0, BF16), keys)
                part = jnp.dot(weight, ones, preferred_element_type=F32)
                total = part if total is None else total + part
            acc[...] += total

        total = acc[...]
        result = total / pltpu.roll(total, HW, 1)
        for b in range(2):
            top, bottom = result[b * 128:b * 128 + 64], result[b * 128 + 64:b * 128 + 128]
            out_ref[2 * i + b] = jnp.where(lanes((64, 128)) >= HW, top, pltpu.roll(bottom, HW, 1)).astype(BF16)


def renorm(v):
    return v * lax.rsqrt(jnp.mean(v * v, axis=-1, keepdims=True) + EPS)


def mix_kernel(attn_ref, o_ref, h_ref, wu_ref, wg_ref, wd_ref, su_ref, sg_ref, ra_ref, sum_out, mixed_out,
               heads, lhs, om, wu, wg, wd, mixed, part, peer, rr, rl, sr, sl,
               asend, arecv, zsend, zrecv, psend, precv, qsend, qrecv, rsend, rrecv, local):
    dp, t, z, c = place()
    greet([(dp, (t + n) % NT) for n in range(1, NT)])
    started = []
    order = [8, 9, 7, 10, 6, 11, 5, 12, 4, 13, 3, 14, 2, 15, 1]
    for n in order:
        to = (t + n) % NT
        copy = pltpu.make_async_remote_copy(
            src_ref=attn_ref.at[to], dst_ref=heads.at[t], send_sem=asend.at[n], recv_sem=arecv.at[n],
            device_id=(dp, to), device_id_type=MESH)
        copy.start()
        started.append(copy)
    own = pltpu.make_async_copy(attn_ref.at[t], heads.at[t], local.at[4])
    own.start()
    loads = [pltpu.make_async_copy(a, b, local.at[n])
             for n, (a, b) in enumerate([(o_ref, om), (wu_ref, wu), (wg_ref, wg), (wd_ref, wd)])]
    for copy in loads:
        copy.start()
    base = h_ref[...].astype(F32)
    own.wait()
    for n in order:
        frm = (t + NT - n) % NT
        pltpu.make_async_remote_copy(
            src_ref=attn_ref.at[t], dst_ref=heads.at[frm], send_sem=asend.at[n], recv_sem=arecv.at[n],
            device_id=(dp, frm), device_id_type=MESH).wait_recv()
    high = lanes((64, 128)) >= HW
    for j in range(NT // 2):
        even, odd = heads[2 * j].astype(F32), heads[2 * j + 1].astype(F32)
        cols = slice(128 * j, 128 * j + 128)
        lhs[0:64, cols] = jnp.where(high, odd, pltpu.roll(even, HW, 1)).astype(BF16)
        lhs[64:128, cols] = jnp.where(high, pltpu.roll(odd, HW, 1), even).astype(BF16)
    loads[0].wait()
    attn_sum = jnp.dot(lhs[...], om[...], preferred_element_type=F32)
    rate = ra_ref[...].reshape(1, D)
    mine = renorm(base + rate * (renorm(attn_sum) - base)).astype(BF16)
    mixed[t] = mine
    ring = Ring([(mixed, mixed.at[t], 32 * k, 32) for k in range(4)], zsend, zrecv, psend, precv)
    ring.first()
    mixed_out[...] = mine
    for copy in loads[1:]:
        copy.wait()
    scale_up, scale_gate = su_ref[...].reshape(1, 320), sg_ref[...].reshape(1, 320)

    def swap(i, zb):
        return pltpu.make_async_remote_copy(
            src_ref=part.at[zb * 2 + (1 - c)], dst_ref=peer.at[zb], send_sem=qsend.at[i], recv_sem=qrecv.at[i],
            device_id=(dp, z * 2 + (1 - c)), device_id_type=MESH)

    def feed(i):
        ring.from_core(i)
        zb = at_z(z, delta(i))
        values = mixed[pl.ds(zb * 2, 2)].reshape(256, D)
        up = lax.dot_general(values, wu[...], NT_DIMS, preferred_element_type=F32) * scale_up
        gate = lax.dot_general(values, wg[...], NT_DIMS, preferred_element_type=F32) * scale_gate
        units = (up * (gate / (1.0 + jnp.exp(-gate)))).astype(BF16)
        result = jnp.dot(units, wd[...], preferred_element_type=F32).astype(BF16)
        part[pl.ds(zb * 2, 2)] = result.reshape(2, ROWS, D)
        swap(i, zb).start()

    def local_sum(zb, k):
        rows = pl.ds(32 * k, 32)
        return part[zb * 2 + c, rows].astype(F32) + peer[zb, rows].astype(F32)

    def rs_copy(way, d, k, src):
        dst = (rr if way == 0 else rl).at[d - 1, pl.ds(32 * k, 32)]
        dev = (dp, at_z(z, 1 if way == 0 else -1) * 2 + c)
        return pltpu.make_async_remote_copy(
            src_ref=src, dst_ref=dst, send_sem=rsend.at[way, d - 1, k], recv_sem=rrecv.at[way, d - 1, k],
            device_id=dev, device_id_type=MESH)

    def pass_on(d, near, far):
        for n in ([2, 3] if near else []) + ([0, 1] if far else []):
            for way in range(2):
                k = (n + 2 * way) % 4
                rows = pl.ds(32 * k, 32)
                recv, sent = (rr, sr) if way == 0 else (rl, sl)
                value = local_sum(at_z(z, d if way == 0 else -d), k)
                if d < 3 or (d == 3 and n < 2):
                    rs_copy(way, d + 1, k, sent.at[d, rows]).wait_recv()
                    value = value + recv[d, rows].astype(F32)
                sent[d - 1, rows] = value.astype(BF16)
                copy = rs_copy(way, d, k, sent.at[d - 1, rows])
                copy.start()
                started.append(copy)

    def swapped(d):
        swap(2 * d - 1, at_z(z, -d)).wait_recv()
        if d < 4:
            swap(2 * d, at_z(z, d)).wait_recv()

    pl.loop(0, 1)(feed)
    ring.step(1)
    pl.loop(1, 3)(feed)
    ring.step(2)
    pl.loop(3, 5)(feed)
    ring.step(3)
    pl.loop(5, 7)(feed)
    swapped(3)
    pass_on(3, True, False)
    ring.step(4)
    pl.loop(7, 8)(feed)
    swapped(4)
    pass_on(4, False, True)
    pass_on(3, False, True)
    swapped(2)
    pass_on(2, True, True)
    swapped(1)
    pass_on(1, True, True)
    swap(0, z).wait_recv()
    for k in range(4):
        rows = pl.ds(32 * k, 32)
        value = local_sum(z, k)
        for way in range(2):
            rs_copy(way, 1, k, (sr if way == 0 else sl).at[0, rows]).wait_recv()
        sum_out[rows, :] = value + rr[0, rows].astype(F32) + rl[0, rows].astype(F32)
    ring.drain()
    for copy in started:
        copy.wait_send()
    for i in range(NZ):
        swap(i, at_z(z, delta(i))).wait_send()


def finish_kernel(sum_ref, mixed_ref, rate_ref, out_ref):
    base = mixed_ref[...].astype(F32)
    rate = rate_ref[...].reshape(1, D)
    out_ref[...] = renorm(base + rate * (renorm(sum_ref[...]) - base)).astype(BF16)


VM = pl.BlockSpec(memory_space=pltpu.VMEM)
SM = pl.BlockSpec(memory_space=pltpu.SMEM)
HB = pl.BlockSpec(memory_space=pl.ANY)
DMA = pltpu.SemaphoreType.DMA


def local(hidden, lengths, request_prompt, request_adapter, prompt_page_table, prefix_page_cache,
          query_key_value_weight, adapter_down, adapter_up, attention_scale, output_matrix, attention_rate,
          up_matrix, gate_matrix, up_scaling, gate_scaling, down_matrix, feedforward_rate):
    queries, key_values, matrix = pl.pallas_call(
        gather_kernel,
        out_shape=(
            jax.ShapeDtypeStruct((GROUP, 128), BF16),
            jax.ShapeDtypeStruct((NREQ * PREFIX + GROUP, 128), BF16),
            jax.ShapeDtypeStruct((NT, HW, D), BF16),
        ),
        in_specs=[HB, HB, HB, HB, HB, VM, VM, SM, SM, SM, SM],
        out_specs=(VM, VM, HB),
        scratch_shapes=[
            pltpu.VMEM((NT, ROWS, D), BF16),
            pltpu.VMEM((NT, HW, D), BF16),
            pltpu.VMEM((2, 4, 4, 2, 64, 128), BF16),
            pltpu.VMEM((2, 4, 4, 2, RANK, 192), BF16),
            pltpu.VMEM((2, 2, 4, 4, RANK, D), BF16),
            pltpu.VMEM((384, D), BF16),
            pltpu.VMEM((128, 192), F32),
            pltpu.VMEM((128, 128), F32),
            pltpu.VMEM((128, 256), BF16),
            pltpu.VMEM((8, 128), F32),
            pltpu.VMEM((NZ, 256, 128), F32),
            DMA((2, 4, 4)), DMA((2, 4, 4)), DMA((8, 4)), DMA((8, 4)),
            DMA((6, 8)), DMA((6, 8)), DMA((9,)), DMA((2,)), DMA((2,)),
        ],
        compiler_params=pltpu.CompilerParams(
            collective_id=0, has_side_effects=True, vmem_limit_bytes=60 * 2**20),
        name="gather_project",
    )(hidden, output_matrix, prefix_page_cache, adapter_up, jnp.swapaxes(adapter_down, 1, 2),
      query_key_value_weight.T, attention_scale,
      lengths, request_adapter, request_prompt, prompt_page_table.T)
    attn = pl.pallas_call(
        attend_kernel,
        out_shape=jax.ShapeDtypeStruct((NT, 64, 128), BF16),
        in_specs=[VM, VM, SM],
        out_specs=VM,
        scratch_shapes=[pltpu.VMEM((256, 128), F32), pltpu.SMEM((2 * NREQ,), jnp.int32)],
        name="attend",
    )(queries, key_values, lengths)
    sums, mixed = pl.pallas_call(
        mix_kernel,
        out_shape=(jax.ShapeDtypeStruct((ROWS, D), F32), jax.ShapeDtypeStruct((ROWS, D), BF16)),
        in_specs=[VM, HB, VM, HB, HB, HB, VM, VM, VM],
        out_specs=(VM, VM),
        scratch_shapes=[
            pltpu.VMEM((NT, 64, 128), BF16),
            pltpu.VMEM((ROWS, NT * HW), BF16),
            pltpu.VMEM((NT * HW, D), BF16),
            pltpu.VMEM((320, D), BF16),
            pltpu.VMEM((320, D), BF16),
            pltpu.VMEM((320, D), BF16),
            pltpu.VMEM((NT, ROWS, D), BF16),
            pltpu.VMEM((NT, ROWS, D), BF16),
            pltpu.VMEM((NZ, ROWS, D), BF16),
            pltpu.VMEM((4, ROWS, D), BF16), pltpu.VMEM((4, ROWS, D), BF16),
            pltpu.VMEM((4, ROWS, D), BF16), pltpu.VMEM((4, ROWS, D), BF16),
            DMA((16,)), DMA((16,)), DMA((2, 4, 4)), DMA((2, 4, 4)), DMA((8, 4)), DMA((8, 4)),
            DMA((8,)), DMA((8,)), DMA((2, 4, 4)), DMA((2, 4, 4)), DMA((5,)),
        ],
        compiler_params=pltpu.CompilerParams(
            collective_id=1, has_side_effects=True, vmem_limit_bytes=60 * 2**20),
        name="mix_feed",
    )(attn, matrix.reshape(NT * HW, D), hidden, up_matrix.T, gate_matrix.T, down_matrix,
      up_scaling, gate_scaling, attention_rate)
    return pl.pallas_call(
        finish_kernel,
        out_shape=jax.ShapeDtypeStruct((ROWS, D), BF16),
        in_specs=[VM, VM, VM],
        out_specs=VM,
        name="finish",
    )(sums, mixed, feedforward_rate)


def solution(mesh):
    placed = (
        P(("dp", "tensor"), None),
        P("dp", None),
        P("dp", None),
        P("dp", None),
        P(),
        P("dp", None, "tensor"),
        P(None, "tensor"),
        P("dp", None, None),
        P("dp", None, "tensor"),
        P("tensor"),
        P("tensor", None),
        P(),
        P(None, "tensor"),
        P(None, "tensor"),
        P("tensor"),
        P("tensor"),
        P("tensor", None),
        P(),
    )
    return jax.shard_map(
        local, mesh=mesh, in_specs=placed, out_specs=P(("dp", "tensor"), None), check_vma=False
    )
```

```python
import functools
import math

import jax
import jax.numpy as jnp
from jax import lax
from jax.experimental import pallas as pl
from jax.experimental.pallas import tpu as pltpu
from jax.sharding import PartitionSpec as P

MESH = pl.DeviceIdType.MESH
D = 1280
HW = 64
RANK = 16
NREQ = 8
PREFIX = 256
NT = 16
NZ = 8
ROWS = 128
GROUP = 2048
EPS = 1e-06
F32 = jnp.float32
BF16 = jnp.bfloat16
NT_DIMS = (((1,), (1,)), ((), ()))


def place():
    dp = lax.axis_index("dp")
    t = lax.axis_index("tensor")
    return dp, t, t // 2, t % 2


def delta(i):
    half = (i + 1) // 2
    odd = i % 2
    return half * (1 - 2 * odd)


def at_z(z, d):
    return (z + d + NZ) % NZ


class Ring:
    def __init__(self, chunks, zsend, zrecv, psend=None, precv=None):
        self.dp, _, self.z, self.c = place()
        self.chunks, self.zsend, self.zrecv = chunks, zsend, zrecv
        self.psend, self.precv = psend, precv
        self.started = []
        self.next = (self.dp, at_z(self.z, 1) * 2 + self.c), (self.dp, at_z(self.z, -1) * 2 + self.c)
        self.other = (self.dp, self.z * 2 + (1 - self.c))

    def spot(self, k, zb, core):
        return self.chunks[k][0](zb, core)

    def ring_copy(self, way, step, k, src, zb):
        return pltpu.make_async_remote_copy(
            src_ref=src, dst_ref=self.spot(k, zb, self.c),
            send_sem=self.zsend.at[way, step - 1, k], recv_sem=self.zrecv.at[way, step - 1, k],
            device_id=self.next[way], device_id_type=MESH)

    def core_copy(self, i, k, src, zb, core):
        return pltpu.make_async_remote_copy(
            src_ref=src, dst_ref=self.spot(k, zb, core),
            send_sem=self.psend.at[i, k], recv_sem=self.precv.at[i, k],
            device_id=self.other, device_id_type=MESH)

    def go(self, copy):
        copy.start()
        self.started.append(copy)

    def turn(self, n):
        count = len(self.chunks)
        return n, (n + count // 2) % count

    def first(self, ns=None):
        ns = range(len(self.chunks)) if ns is None else ns
        for n in ns:
            for way, k in enumerate(self.turn(n)):
                self.go(self.ring_copy(way, 1, k, self.chunks[k][1], self.z))
        if self.psend is not None:
            for n in ns:
                self.go(self.core_copy(0, n, self.chunks[n][1], self.z, self.c))

    def step(self, s, ns=None):
        for n in range(len(self.chunks)) if ns is None else ns:
            far = n < len(self.chunks) // 2
            if s == 4 and not far:
                continue
            for way, k in enumerate(self.turn(n)):
                zb = at_z(self.z, -s if way == 0 else s)
                here = self.spot(k, zb, self.c)
                self.ring_copy(way, s, k, here, zb).wait_recv()
                if s < 3 or (s == 3 and far):
                    self.go(self.ring_copy(way, s + 1, k, here, zb))
                if self.psend is not None:
                    i = 7 if s == 4 else (2 * s - 1 if way == 0 else 2 * s)
                    self.go(self.core_copy(i, k, here, zb, self.c))

    def from_core(self, i):
        zb = at_z(self.z, delta(i))
        for k in range(len(self.chunks)):
            self.core_copy(i, k, self.spot(k, zb, 1 - self.c), zb, 1 - self.c).wait_recv()

    def drain(self):
        for copy in self.started:
            copy.wait_send()


def slab(buf, first_row, rows):
    return lambda zb, core: buf.at[zb * 2 + core, pl.ds(first_row, rows)]


class Plane:
    def __init__(self, number, first_axis, src, buf, send, recv, local):
        dp, t, _, _ = place()
        x, y = dp // 4, dp % 4
        self.src, self.buf, self.n, self.send, self.recv, self.local = src, buf, number, send, recv, local
        self.a, self.b = (x, y) if first_axis == 0 else (y, x)

        def device(a, b):
            return (a * 4 + b if first_axis == 0 else b * 4 + a), t

        up_a, down_a = (self.a + 1) % 4, (self.a + 3) % 4
        up_b, down_b = (self.b + 1) % 4, (self.b + 3) % 4
        self.lo_a, self.hi_a, self.lo_b, self.hi_b = down_a, up_a, down_b, up_b
        self.dev_a = device(up_a, self.b), device(down_a, self.b)
        self.dev_b = device(self.a, up_b), device(self.a, down_b)
        self.started = []

    def copy(self, k, src, dst, dev):
        return pltpu.make_async_remote_copy(
            src_ref=src, dst_ref=dst, send_sem=self.send.at[self.n, k], recv_sem=self.recv.at[self.n, k],
            device_id=dev, device_id_type=MESH)

    def go(self, k, src, dst, dev):
        c = self.copy(k, src, dst, dev)
        c.start()
        self.started.append(c)

    def got(self, k, dst):
        self.copy(k, dst, dst, self.dev_a[0]).wait_recv()

    def halves(self, ref):
        if len(ref.shape) == 2:
            n = ref.shape[1] // 2
            return ref.at[:, pl.ds(0, n)], ref.at[:, pl.ds(n, n)]
        n = ref.shape[0] // 2
        return ref.at[pl.ds(0, n)], ref.at[pl.ds(n, n)]

    def one(self):
        mine = self.buf.at[self.b, self.a]
        self.own = pltpu.make_async_copy(self.src, mine, self.local.at[self.n])
        self.own.start()
        self.go(0, self.src, mine, self.dev_a[0])
        self.go(1, self.src, mine, self.dev_a[1])

    def two(self):
        lo, hi = self.buf.at[self.b, self.lo_a], self.buf.at[self.b, self.hi_a]
        self.got(0, lo)
        self.go(2, self.halves(lo)[0], self.halves(lo)[0], self.dev_a[0])
        self.got(1, hi)
        self.go(3, self.halves(hi)[1], self.halves(hi)[1], self.dev_a[1])

    def three(self):
        far = self.buf.at[self.b, (self.a + 2) % 4]
        self.got(2, self.halves(far)[0])
        self.got(3, self.halves(far)[1])
        self.own.wait()
        row = self.buf.at[self.b]
        self.go(4, row, row, self.dev_b[0])
        self.go(5, row, row, self.dev_b[1])

    def four(self):
        lo, hi = self.buf.at[self.lo_b], self.buf.at[self.hi_b]
        self.got(4, lo)
        self.go(6, self.halves(lo)[0], self.halves(lo)[0], self.dev_b[0])
        self.got(5, hi)
        self.go(7, self.halves(hi)[1], self.halves(hi)[1], self.dev_b[1])

    def five(self):
        far = self.buf.at[(self.b + 2) % 4]
        self.got(6, self.halves(far)[0])
        self.got(7, self.halves(far)[1])

    def drain(self):
        for c in self.started:
            c.wait_send()


class Line:
    def __init__(self, number, axis, at, send, recv):
        dp, t, _, _ = place()
        x, y = dp // 4, dp % 4
        self.n, self.at, self.send, self.recv = number, at, send, recv
        self.a = x if axis == 0 else y

        def device(a):
            return (a * 4 + y if axis == 0 else x * 4 + a), t

        self.lo, self.hi, self.far = (self.a + 3) % 4, (self.a + 1) % 4, (self.a + 2) % 4
        self.devs = device(self.hi), device(self.lo)
        self.started = []

    def copy(self, k, ref, dev):
        return pltpu.make_async_remote_copy(
            src_ref=ref, dst_ref=ref, send_sem=self.send.at[self.n, k], recv_sem=self.recv.at[self.n, k],
            device_id=dev, device_id_type=MESH)

    def go(self, k, ref, dev):
        c = self.copy(k, ref, dev)
        c.start()
        self.started.append(c)

    def one(self):
        for k in range(2):
            self.go(k, self.at(self.a, 0, 8), self.devs[k])

    def two(self):
        self.copy(0, self.at(self.lo, 0, 8), self.devs[0]).wait_recv()
        self.go(2, self.at(self.lo, 0, 4), self.devs[0])
        self.copy(1, self.at(self.hi, 0, 8), self.devs[1]).wait_recv()
        self.go(3, self.at(self.hi, 4, 4), self.devs[1])

    def three(self):
        self.copy(2, self.at(self.far, 0, 4), self.devs[0]).wait_recv()
        self.copy(3, self.at(self.far, 4, 4), self.devs[1]).wait_recv()

    def drain(self):
        for c in self.started:
            c.wait_send()


def greet(peers):
    barrier = pltpu.get_barrier_semaphore()
    for peer in peers:
        pl.semaphore_signal(barrier, inc=1, device_id=peer, device_id_type=MESH)
    pl.semaphore_wait(barrier, len(peers))


def lanes(shape):
    return lax.broadcasted_iota(jnp.int32, shape, len(shape) - 1)


def row_starts(len_ref, first_row, shape):
    rows = first_row + lax.broadcasted_iota(jnp.int32, shape, 0)
    end = jnp.int32(0)
    req = jnp.zeros(shape, jnp.int32)
    start = jnp.zeros(shape, jnp.int32)
    for r in range(NREQ):
        size = len_ref[0, r]
        end = end + size
        past = rows >= end
        req = req + jnp.where(past, 1, 0)
        start = start + jnp.where(past, size, 0)
    return rows, req, start


def gather_kernel(h_ref, o_ref, pg_ref, up_ref, dn_ref, w_ref, gain_ref, len_ref, ra_ref, rp_ref, pt_ref,
                  q_out, kv_out, o_out,
                  gh, ob, pb, ub, db, wide, sel, tail, su, gains, trig,
                  zsend, zrecv, psend, precv, usend, urecv, xsend, xrecv, lsend, lrecv, local, dsend, drecv):
    dp, t, z, c = place()
    x, y = dp // 4, dp % 4
    greet([
        (dp, at_z(z, 1) * 2 + c), (dp, at_z(z, -1) * 2 + c), (dp, z * 2 + (1 - c)),
        (((x + 1) % 4) * 4 + y, t), (((x + 3) % 4) * 4 + y, t),
        (x * 4 + (y + 1) % 4, t), (x * 4 + (y + 3) % 4, t),
    ])
    ring = Ring([(slab(gh, 64 * k, 64), h_ref.at[pl.ds(64 * k, 64)]) for k in range(2)],
                zsend, zrecv, psend, precv)
    quarters = [(x, o_ref.at[pl.ds(pl.multiple_of(16 * x, 16), 16), pl.ds(0, D // 2)]),
                (y, o_ref.at[pl.ds(pl.multiple_of(16 * y, 16), 16), pl.ds(D // 2, D // 2)])]
    oring = Ring([(functools.partial(lambda part, j, zb, core: ob.at[part, j, zb, core], part, j), src)
                  for part, (j, src) in enumerate(quarters)], usend, urecv)
    lines = [Line(part, part, functools.partial(
        lambda part, j, z0, n: ob.at[part, j, pl.ds(z0, n), c], part), lsend, lrecv) for part in range(2)]
    planes = []
    for half in range(2):
        for src, buf in ((dn_ref.at[2 * c + half], db.at[c, half]),
                         (pg_ref.at[pl.ds(2 * half, 2)], pb.at[half]),
                         (up_ref.at[pl.ds(2 * half, 2)], ub.at[half])):
            planes.append(Plane(len(planes), half, src, buf, xsend, xrecv, local))
    oring.first()
    ring.first([0])
    for p in planes:
        p.one()
    owns = [pltpu.make_async_copy(h_ref, gh.at[t], local.at[6])]
    for part, (j, src) in enumerate(quarters):
        owns.append(pltpu.make_async_copy(src, ob.at[part, j, z, c], local.at[7 + part]))
    for own in owns:
        own.start()
    oring.step(1)
    ring.first([1])
    for p in planes:
        p.two()
    for p in planes:
        p.three()
    for own in owns:
        own.wait()
    oring.step(2)
    ring.step(1, [0])

    lane = lanes((256, 128))
    low = lane < HW
    gains[...] = jnp.ones_like(gains)
    gains[:, 0:HW] = jnp.broadcast_to(gain_ref[...].reshape(1, HW), (8, HW))
    gain = gains[0:1, :]
    wide[128:192, :] = w_ref[0:HW, :]
    wide[192:256, :] = jnp.zeros((HW, D), BF16)
    wide[256:384, :] = w_ref[HW:3 * HW, :]
    tail[...] = jnp.zeros_like(tail)
    frequency = jnp.exp((lane % 32).astype(F32) * (-2.0 * math.log(10000.0) / HW))
    quarter = jnp.where(low, 0.0, 0.5 * math.pi)

    def waves(b):
        rows, _, start = row_starts(len_ref, b * 256, (256, 128))
        angle = (rows - start + PREFIX).astype(F32) * frequency
        trig[b] = jnp.cos(angle - quarter)

    pl.loop(0, 4)(waves)
    oring.step(3)
    ring.step(1, [1])
    pl.loop(4, 8)(waves)
    oring.step(4)
    for line in lines:
        line.one()
    ring.step(2, [0])
    for p in planes:
        p.four()
    ring.step(2, [1])
    for line in lines:
        line.two()
    for p in planes:
        p.five()
    swaps = []
    for half in range(2):
        swap = pltpu.make_async_remote_copy(
            src_ref=db.at[c, half], dst_ref=db.at[c, half], send_sem=dsend.at[half], recv_sem=drecv.at[half],
            device_id=(dp, z * 2 + (1 - c)), device_id_type=MESH)
        swap.start()
        swaps.append(swap)

    for line in lines:
        line.three()
    matrix_swap = pltpu.make_async_remote_copy(
        src_ref=ob.at[:, :, :, c], dst_ref=ob.at[:, :, :, c], send_sem=dsend.at[2], recv_sem=drecv.at[2],
        device_id=(dp, z * 2 + (1 - c)), device_id_type=MESH)
    matrix_swap.start()
    swaps.append(matrix_swap)

    def unit(v):
        total = jnp.sum(jnp.where(low, v * v, 0.0), axis=1, keepdims=True)
        return v * lax.rsqrt(total + EPS) * gain

    def slot(owner, half):
        a, b = owner // 4, owner % 4
        return b + half * (a - b), a + half * (b - a)

    @pl.loop(0, NREQ)
    def _(r):
        prompt = rp_ref[0, r]
        for j in range(4):
            page = pt_ref[j, prompt]
            half = (page % 4) // 2
            major, minor = slot(page // 4, half)
            raw = pb[half, major, minor, page % 2].astype(F32)
            low_p = lanes((64, 128)) < HW
            total = jnp.sum(jnp.where(low_p, raw * raw, 0.0), axis=1, keepdims=True)
            unit_key = raw * lax.rsqrt(total + EPS) * gain
            kv_out[pl.ds(pl.multiple_of(r * PREFIX + j * 64, 64), 64), :] = jnp.where(
                low_p, unit_key, raw).astype(BF16)

    for half in range(2):
        pltpu.make_async_remote_copy(
            src_ref=db.at[1 - c, half], dst_ref=db.at[1 - c, half],
            send_sem=dsend.at[half], recv_sem=drecv.at[half],
            device_id=(dp, z * 2 + (1 - c)), device_id_type=MESH).wait_recv()
    for r in range(NREQ):
        adapter = ra_ref[0, r]
        within = adapter % 4
        major, minor = slot(adapter // 4, within % 2)
        wide[r * RANK:(r + 1) * RANK, :] = db[within // 2, within % 2, major, minor]
        major, minor = slot(adapter // 4, within // 2)
        sel[r * RANK:(r + 1) * RANK, :] = ub[within // 2, major, minor, within % 2].astype(F32)
    first = sel[:, 0:128]
    tail[:, 0:HW] = sel[:, 128:192]
    low_s = lanes((128, 128)) < HW
    su[:, 0:128] = jnp.where(low_s, first, 0.0).astype(BF16)
    su[:, 128:256] = jnp.where(low_s, pltpu.roll(first, HW, 1), pltpu.roll(tail[...], HW, 1)).astype(BF16)

    def project(i):
        ring.from_core(i)
        zb = at_z(z, delta(i))
        values = gh[pl.ds(zb * 2, 2)].reshape(256, D)
        _, req, _ = row_starts(len_ref, zb * 256, (256, 128))
        every = lax.dot_general(values, wide[...], NT_DIMS, preferred_element_type=F32)
        middle = jnp.where(lane // RANK == req, every[:, 0:128], 0.0).astype(BF16)
        both = every[:, 128:384] + 0.5 * jnp.dot(middle, su[...], preferred_element_type=F32)
        wave = trig[zb]
        cosine = jnp.where(low, wave, 1.0)
        sine = pltpu.roll(wave, HW, 1)
        sine = jnp.where(lane < 32, -sine, jnp.where(low, sine, 0.0))

        def rotate(v):
            other = jnp.where(lane < 32, pltpu.roll(v, 96, 1), pltpu.roll(v, 32, 1))
            return v * cosine + other * sine

        query, key_value = both[:, :128], both[:, 128:]
        row = pl.multiple_of(zb * 256, 256)
        q_out[pl.ds(row, 256), :] = unit(rotate(query)).astype(BF16) * jnp.asarray(8.0, BF16)
        kv_out[pl.ds(row + NREQ * PREFIX, 256), :] = jnp.where(
            low, unit(rotate(key_value)), key_value).astype(BF16)

    pl.loop(0, 3)(project)
    ring.step(3)
    pl.loop(3, 5)(project)
    pltpu.make_async_remote_copy(
        src_ref=ob.at[:, :, :, 1 - c], dst_ref=ob.at[:, :, :, 1 - c], send_sem=dsend.at[2], recv_sem=drecv.at[2],
        device_id=(dp, z * 2 + (1 - c)), device_id_type=MESH).wait_recv()
    out = pltpu.make_async_copy(ob, o_out, local.at[9])
    out.start()
    ring.step(4)
    pl.loop(5, 8)(project)
    for part in [ring, oring] + planes + lines:
        part.drain()
    for swap in swaps:
        swap.wait_send()
    out.wait()


TILES = 2


def attend_kernel(q_ref, kv_ref, len_ref, out_ref, acc, begins):
    low = lanes((256, 128)) < HW
    begin = jnp.int32(0)
    for r in range(NREQ):
        begins[r] = begin
        begin = begin + len_ref[0, r]
    for r in range(NREQ, 2 * NREQ):
        begins[r] = jnp.int32(0)

    @pl.loop(0, NZ)
    def _(i):
        first = i * 256
        query = q_ref[pl.ds(pl.multiple_of(first, 256), 256), :]
        rows, _, start = row_starts(len_ref, first, (256, 256))
        end = jnp.int32(0)
        request_lo, request_hi, start_lo = jnp.int32(0), jnp.int32(0), jnp.int32(0)
        for r in range(NREQ):
            size = len_ref[0, r]
            end = end + size
            request_lo = request_lo + jnp.where(first >= end, 1, 0)
            start_lo = start_lo + jnp.where(first >= end, size, 0)
            request_hi = request_hi + jnp.where(first + 255 >= end, 1, 0)
        acc[...] = jnp.zeros_like(acc)
        lowest = start_lo // 256
        prefixes = request_hi + 1 - request_lo
        count = prefixes + i + 1 - lowest
        lane = lanes((256, 256))

        @pl.loop(0, (count + TILES - 1) // TILES)
        def _(n):
            total = None
            for u in range(TILES):
                m = jnp.minimum(n * TILES + u, count - 1)
                shared = m < prefixes
                tile = jnp.where(shared, request_lo + m, NREQ + lowest + m - prefixes)
                base = jnp.where(shared, begins[tile], (tile - NREQ) * 256)
                base = jnp.where(n * TILES + u < count, base, 2 * GROUP)
                column = jnp.where(shared, 0, 1) * lane + base
                keys = kv_ref[pl.ds(pl.multiple_of(tile * 256, 256), 256), :]
                score = lax.dot_general(query, keys, NT_DIMS, preferred_element_type=F32)
                weight = jnp.where((column >= start) & (column <= rows), jnp.exp(score), 0.0).astype(BF16)
                ones = jnp.where(low, jnp.asarray(1.0, BF16), keys)
                part = jnp.dot(weight, ones, preferred_element_type=F32)
                total = part if total is None else total + part
            acc[...] += total

        total = acc[...]
        result = total / pltpu.roll(total, HW, 1)
        for b in range(2):
            top, bottom = result[b * 128:b * 128 + 64], result[b * 128 + 64:b * 128 + 128]
            out_ref[2 * i + b] = jnp.where(lanes((64, 128)) >= HW, top, pltpu.roll(bottom, HW, 1)).astype(BF16)


def renorm(v):
    return v * lax.rsqrt(jnp.mean(v * v, axis=-1, keepdims=True) + EPS)


def mix_kernel(attn_ref, o_ref, h_ref, wu_ref, wg_ref, wd_ref, su_ref, sg_ref, ra_ref, sum_out, mixed_out,
               heads, lhs, om, wu, wg, wd, mixed, part, peer, rr, rl, sr, sl,
               asend, arecv, zsend, zrecv, psend, precv, qsend, qrecv, rsend, rrecv, local):
    dp, t, z, c = place()
    greet([(dp, (t + n) % NT) for n in range(1, NT)])
    started = []
    order = [8, 9, 7, 10, 6, 11, 5, 12, 4, 13, 3, 14, 2, 15, 1]
    for n in order:
        to = (t + n) % NT
        copy = pltpu.make_async_remote_copy(
            src_ref=attn_ref.at[to], dst_ref=heads.at[t], send_sem=asend.at[n], recv_sem=arecv.at[n],
            device_id=(dp, to), device_id_type=MESH)
        copy.start()
        started.append(copy)
    own = pltpu.make_async_copy(attn_ref.at[t], heads.at[t], local.at[11])
    own.start()
    moves = [(o_ref.at[part, j], om.at[:, :, j, :, pl.ds(part * (D // 2), D // 2)])
             for part in range(2) for j in range(4)] + [(wu_ref, wu), (wg_ref, wg), (wd_ref, wd)]
    loads = [pltpu.make_async_copy(a, b, local.at[n]) for n, (a, b) in enumerate(moves)]
    for copy in loads:
        copy.start()
    base = h_ref[...].astype(F32)
    own.wait()
    for n in order:
        frm = (t + NT - n) % NT
        pltpu.make_async_remote_copy(
            src_ref=attn_ref.at[t], dst_ref=heads.at[frm], send_sem=asend.at[n], recv_sem=arecv.at[n],
            device_id=(dp, frm), device_id_type=MESH).wait_recv()
    high = lanes((64, 128)) >= HW
    for j in range(NT // 2):
        even, odd = heads[2 * j].astype(F32), heads[2 * j + 1].astype(F32)
        cols = slice(128 * j, 128 * j + 128)
        lhs[0:64, cols] = jnp.where(high, odd, pltpu.roll(even, HW, 1)).astype(BF16)
        lhs[64:128, cols] = jnp.where(high, pltpu.roll(odd, HW, 1), even).astype(BF16)
    for copy in loads[:8]:
        copy.wait()
    attn_sum = jnp.dot(lhs[...], om[...].reshape(NT * HW, D), preferred_element_type=F32)
    rate = ra_ref[...].reshape(1, D)
    mine = renorm(base + rate * (renorm(attn_sum) - base)).astype(BF16)
    mixed[t] = mine
    ring = Ring([(slab(mixed, 32 * k, 32), mixed.at[t, pl.ds(32 * k, 32)]) for k in range(4)], zsend, zrecv, psend, precv)
    ring.first()
    mixed_out[...] = mine
    for copy in loads[8:]:
        copy.wait()
    scale_up, scale_gate = su_ref[...].reshape(1, 320), sg_ref[...].reshape(1, 320)

    def swap(i, zb):
        return pltpu.make_async_remote_copy(
            src_ref=part.at[zb * 2 + (1 - c)], dst_ref=peer.at[zb], send_sem=qsend.at[i], recv_sem=qrecv.at[i],
            device_id=(dp, z * 2 + (1 - c)), device_id_type=MESH)

    def feed(i):
        ring.from_core(i)
        zb = at_z(z, delta(i))
        values = mixed[pl.ds(zb * 2, 2)].reshape(256, D)
        up = lax.dot_general(values, wu[...], NT_DIMS, preferred_element_type=F32) * scale_up
        gate = lax.dot_general(values, wg[...], NT_DIMS, preferred_element_type=F32) * scale_gate
        units = (up * (gate / (1.0 + jnp.exp(-gate)))).astype(BF16)
        result = jnp.dot(units, wd[...], preferred_element_type=F32).astype(BF16)
        part[pl.ds(zb * 2, 2)] = result.reshape(2, ROWS, D)
        swap(i, zb).start()

    def local_sum(zb, k):
        rows = pl.ds(32 * k, 32)
        return part[zb * 2 + c, rows].astype(F32) + peer[zb, rows].astype(F32)

    def rs_copy(way, d, k, src):
        dst = (rr if way == 0 else rl).at[d - 1, pl.ds(32 * k, 32)]
        dev = (dp, at_z(z, 1 if way == 0 else -1) * 2 + c)
        return pltpu.make_async_remote_copy(
            src_ref=src, dst_ref=dst, send_sem=rsend.at[way, d - 1, k], recv_sem=rrecv.at[way, d - 1, k],
            device_id=dev, device_id_type=MESH)

    def pass_on(d, near, far):
        for n in ([2, 3] if near else []) + ([0, 1] if far else []):
            for way in range(2):
                k = (n + 2 * way) % 4
                rows = pl.ds(32 * k, 32)
                recv, sent = (rr, sr) if way == 0 else (rl, sl)
                value = local_sum(at_z(z, d if way == 0 else -d), k)
                if d < 3 or (d == 3 and n < 2):
                    rs_copy(way, d + 1, k, sent.at[d, rows]).wait_recv()
                    value = value + recv[d, rows].astype(F32)
                sent[d - 1, rows] = value.astype(BF16)
                copy = rs_copy(way, d, k, sent.at[d - 1, rows])
                copy.start()
                started.append(copy)

    def swapped(d):
        swap(2 * d - 1, at_z(z, -d)).wait_recv()
        if d < 4:
            swap(2 * d, at_z(z, d)).wait_recv()

    pl.loop(0, 1)(feed)
    ring.step(1)
    pl.loop(1, 3)(feed)
    ring.step(2)
    pl.loop(3, 5)(feed)
    ring.step(3)
    pl.loop(5, 7)(feed)
    swapped(3)
    pass_on(3, True, False)
    ring.step(4)
    pl.loop(7, 8)(feed)
    swapped(4)
    pass_on(4, False, True)
    pass_on(3, False, True)
    swapped(2)
    pass_on(2, True, True)
    swapped(1)
    pass_on(1, True, True)
    swap(0, z).wait_recv()
    for k in range(4):
        rows = pl.ds(32 * k, 32)
        value = local_sum(z, k)
        for way in range(2):
            rs_copy(way, 1, k, (sr if way == 0 else sl).at[0, rows]).wait_recv()
        sum_out[rows, :] = value + rr[0, rows].astype(F32) + rl[0, rows].astype(F32)
    ring.drain()
    for copy in started:
        copy.wait_send()
    for i in range(NZ):
        swap(i, at_z(z, delta(i))).wait_send()


def finish_kernel(sum_ref, mixed_ref, rate_ref, out_ref):
    base = mixed_ref[...].astype(F32)
    rate = rate_ref[...].reshape(1, D)
    out_ref[...] = renorm(base + rate * (renorm(sum_ref[...]) - base)).astype(BF16)


VM = pl.BlockSpec(memory_space=pltpu.VMEM)
SM = pl.BlockSpec(memory_space=pltpu.SMEM)
HB = pl.BlockSpec(memory_space=pl.ANY)
DMA = pltpu.SemaphoreType.DMA


def local(hidden, lengths, request_prompt, request_adapter, prompt_page_table, prefix_page_cache,
          query_key_value_weight, adapter_down, adapter_up, attention_scale, output_matrix, attention_rate,
          up_matrix, gate_matrix, up_scaling, gate_scaling, down_matrix, feedforward_rate):
    queries, key_values, matrix = pl.pallas_call(
        gather_kernel,
        out_shape=(
            jax.ShapeDtypeStruct((GROUP, 128), BF16),
            jax.ShapeDtypeStruct((NREQ * PREFIX + GROUP, 128), BF16),
            jax.ShapeDtypeStruct((2, 4, NZ, 2, 16, D // 2), BF16),
        ),
        in_specs=[HB, HB, HB, HB, HB, VM, VM, SM, SM, SM, SM],
        out_specs=(VM, VM, HB),
        scratch_shapes=[
            pltpu.VMEM((NT, ROWS, D), BF16),
            pltpu.VMEM((2, 4, NZ, 2, 16, D // 2), BF16),
            pltpu.VMEM((2, 4, 4, 2, 64, 128), BF16),
            pltpu.VMEM((2, 4, 4, 2, RANK, 192), BF16),
            pltpu.VMEM((2, 2, 4, 4, RANK, D), BF16),
            pltpu.VMEM((384, D), BF16),
            pltpu.VMEM((128, 192), F32),
            pltpu.VMEM((128, 128), F32),
            pltpu.VMEM((128, 256), BF16),
            pltpu.VMEM((8, 128), F32),
            pltpu.VMEM((NZ, 256, 128), F32),
            DMA((2, 4, 2)), DMA((2, 4, 2)), DMA((8, 2)), DMA((8, 2)), DMA((2, 4, 2)), DMA((2, 4, 2)),
            DMA((6, 8)), DMA((6, 8)), DMA((2, 4)), DMA((2, 4)), DMA((10,)), DMA((3,)), DMA((3,)),
        ],
        compiler_params=pltpu.CompilerParams(
            collective_id=0, has_side_effects=True, vmem_limit_bytes=60 * 2**20),
        name="gather_project",
    )(hidden, output_matrix, prefix_page_cache, adapter_up, jnp.swapaxes(adapter_down, 1, 2),
      query_key_value_weight.T, attention_scale,
      lengths, request_adapter, request_prompt, prompt_page_table.T)
    attn = pl.pallas_call(
        attend_kernel,
        out_shape=jax.ShapeDtypeStruct((NT, 64, 128), BF16),
        in_specs=[VM, VM, SM],
        out_specs=VM,
        scratch_shapes=[pltpu.VMEM((256, 128), F32), pltpu.SMEM((2 * NREQ,), jnp.int32)],
        name="attend",
    )(queries, key_values, lengths)
    sums, mixed = pl.pallas_call(
        mix_kernel,
        out_shape=(jax.ShapeDtypeStruct((ROWS, D), F32), jax.ShapeDtypeStruct((ROWS, D), BF16)),
        in_specs=[VM, HB, VM, HB, HB, HB, VM, VM, VM],
        out_specs=(VM, VM),
        scratch_shapes=[
            pltpu.VMEM((NT, 64, 128), BF16),
            pltpu.VMEM((ROWS, NT * HW), BF16),
            pltpu.VMEM((NZ, 2, 4, 16, D), BF16),
            pltpu.VMEM((320, D), BF16),
            pltpu.VMEM((320, D), BF16),
            pltpu.VMEM((320, D), BF16),
            pltpu.VMEM((NT, ROWS, D), BF16),
            pltpu.VMEM((NT, ROWS, D), BF16),
            pltpu.VMEM((NZ, ROWS, D), BF16),
            pltpu.VMEM((4, ROWS, D), BF16), pltpu.VMEM((4, ROWS, D), BF16),
            pltpu.VMEM((4, ROWS, D), BF16), pltpu.VMEM((4, ROWS, D), BF16),
            DMA((16,)), DMA((16,)), DMA((2, 4, 4)), DMA((2, 4, 4)), DMA((8, 4)), DMA((8, 4)),
            DMA((8,)), DMA((8,)), DMA((2, 4, 4)), DMA((2, 4, 4)), DMA((12,)),
        ],
        compiler_params=pltpu.CompilerParams(
            collective_id=1, has_side_effects=True, vmem_limit_bytes=60 * 2**20),
        name="mix_feed",
    )(attn, matrix, hidden, up_matrix.T, gate_matrix.T, down_matrix,
      up_scaling, gate_scaling, attention_rate)
    return pl.pallas_call(
        finish_kernel,
        out_shape=jax.ShapeDtypeStruct((ROWS, D), BF16),
        in_specs=[VM, VM, VM],
        out_specs=VM,
        name="finish",
    )(sums, mixed, feedforward_rate)


def solution(mesh):
    placed = (
        P(("dp", "tensor"), None),
        P("dp", None),
        P("dp", None),
        P("dp", None),
        P(),
        P("dp", None, "tensor"),
        P(None, "tensor"),
        P("dp", None, None),
        P("dp", None, "tensor"),
        P("tensor"),
        P("tensor", None),
        P(),
        P(None, "tensor"),
        P(None, "tensor"),
        P("tensor"),
        P("tensor"),
        P("tensor", None),
        P(),
    )
    return jax.shard_map(
        local, mesh=mesh, in_specs=placed, out_specs=P(("dp", "tensor"), None), check_vma=False
    )
```

```python
import functools
import math

import jax
import jax.numpy as jnp
from jax import lax
from jax.experimental import pallas as pl
from jax.experimental.pallas import tpu as pltpu
from jax.sharding import PartitionSpec as P

MESH = pl.DeviceIdType.MESH
D = 1280
HW = 64
RANK = 16
NREQ = 8
PREFIX = 256
NT = 16
NZ = 8
ROWS = 128
GROUP = 2048
EPS = 1e-06
F32 = jnp.float32
BF16 = jnp.bfloat16
NT_DIMS = (((1,), (1,)), ((), ()))


def place():
    dp = lax.axis_index("dp")
    t = lax.axis_index("tensor")
    return dp, t, t // 2, t % 2


def delta(i):
    half = (i + 1) // 2
    odd = i % 2
    return half * (1 - 2 * odd)


def at_z(z, d):
    return (z + d + NZ) % NZ


class Ring:
    def __init__(self, chunks, zsend, zrecv, psend=None, precv=None):
        self.dp, _, self.z, self.c = place()
        self.chunks, self.zsend, self.zrecv = chunks, zsend, zrecv
        self.psend, self.precv = psend, precv
        self.started = []
        self.next = (self.dp, at_z(self.z, 1) * 2 + self.c), (self.dp, at_z(self.z, -1) * 2 + self.c)
        self.other = (self.dp, self.z * 2 + (1 - self.c))

    def spot(self, k, zb, core):
        return self.chunks[k][0](zb, core)

    def ring_copy(self, way, step, k, src, zb):
        return pltpu.make_async_remote_copy(
            src_ref=src, dst_ref=self.spot(k, zb, self.c),
            send_sem=self.zsend.at[way, step - 1, k], recv_sem=self.zrecv.at[way, step - 1, k],
            device_id=self.next[way], device_id_type=MESH)

    def core_copy(self, i, k, src, zb, core):
        return pltpu.make_async_remote_copy(
            src_ref=src, dst_ref=self.spot(k, zb, core),
            send_sem=self.psend.at[i, k], recv_sem=self.precv.at[i, k],
            device_id=self.other, device_id_type=MESH)

    def go(self, copy):
        copy.start()
        self.started.append(copy)

    def turn(self, n):
        count = len(self.chunks)
        return n, (n + count // 2) % count

    def first(self, ns=None):
        ns = range(len(self.chunks)) if ns is None else ns
        for n in ns:
            for way, k in enumerate(self.turn(n)):
                self.go(self.ring_copy(way, 1, k, self.chunks[k][1], self.z))
        if self.psend is not None:
            for n in ns:
                self.go(self.core_copy(0, n, self.chunks[n][1], self.z, self.c))

    def step(self, s, ns=None):
        for n in range(len(self.chunks)) if ns is None else ns:
            far = n < len(self.chunks) // 2
            if s == 4 and not far:
                continue
            for way, k in enumerate(self.turn(n)):
                zb = at_z(self.z, -s if way == 0 else s)
                here = self.spot(k, zb, self.c)
                self.ring_copy(way, s, k, here, zb).wait_recv()
                if s < 3 or (s == 3 and far):
                    self.go(self.ring_copy(way, s + 1, k, here, zb))
                if self.psend is not None:
                    i = 7 if s == 4 else (2 * s - 1 if way == 0 else 2 * s)
                    self.go(self.core_copy(i, k, here, zb, self.c))

    def from_core(self, i):
        zb = at_z(self.z, delta(i))
        for k in range(len(self.chunks)):
            self.core_copy(i, k, self.spot(k, zb, 1 - self.c), zb, 1 - self.c).wait_recv()

    def drain(self):
        for copy in self.started:
            copy.wait_send()


def slab(buf, first_row, rows):
    return lambda zb, core: buf.at[zb * 2 + core, pl.ds(first_row, rows)]


class Plane:
    def __init__(self, number, first_axis, src, buf, send, recv, local):
        dp, t, _, _ = place()
        x, y = dp // 4, dp % 4
        self.src, self.buf, self.n, self.send, self.recv, self.local = src, buf, number, send, recv, local
        self.a, self.b = (x, y) if first_axis == 0 else (y, x)

        def device(a, b):
            return (a * 4 + b if first_axis == 0 else b * 4 + a), t

        up_a, down_a = (self.a + 1) % 4, (self.a + 3) % 4
        up_b, down_b = (self.b + 1) % 4, (self.b + 3) % 4
        self.lo_a, self.hi_a, self.lo_b, self.hi_b = down_a, up_a, down_b, up_b
        self.dev_a = device(up_a, self.b), device(down_a, self.b)
        self.dev_b = device(self.a, up_b), device(self.a, down_b)
        self.started = []

    def copy(self, k, src, dst, dev):
        return pltpu.make_async_remote_copy(
            src_ref=src, dst_ref=dst, send_sem=self.send.at[self.n, k], recv_sem=self.recv.at[self.n, k],
            device_id=dev, device_id_type=MESH)

    def go(self, k, src, dst, dev):
        c = self.copy(k, src, dst, dev)
        c.start()
        self.started.append(c)

    def got(self, k, dst):
        self.copy(k, dst, dst, self.dev_a[0]).wait_recv()

    def halves(self, ref):
        if len(ref.shape) == 2:
            n = ref.shape[1] // 2
            return ref.at[:, pl.ds(0, n)], ref.at[:, pl.ds(n, n)]
        n = ref.shape[0] // 2
        return ref.at[pl.ds(0, n)], ref.at[pl.ds(n, n)]

    def one(self):
        mine = self.buf.at[self.b, self.a]
        self.own = pltpu.make_async_copy(self.src, mine, self.local.at[self.n])
        self.own.start()
        self.go(0, self.src, mine, self.dev_a[0])
        self.go(1, self.src, mine, self.dev_a[1])

    def two(self):
        lo, hi = self.buf.at[self.b, self.lo_a], self.buf.at[self.b, self.hi_a]
        self.got(0, lo)
        self.go(2, self.halves(lo)[0], self.halves(lo)[0], self.dev_a[0])
        self.got(1, hi)
        self.go(3, self.halves(hi)[1], self.halves(hi)[1], self.dev_a[1])

    def three(self):
        far = self.buf.at[self.b, (self.a + 2) % 4]
        self.got(2, self.halves(far)[0])
        self.got(3, self.halves(far)[1])
        self.own.wait()

    def turn(self):
        row = self.buf.at[self.b]
        self.go(4, row, row, self.dev_b[0])
        self.go(5, row, row, self.dev_b[1])

    def four(self):
        lo, hi = self.buf.at[self.lo_b], self.buf.at[self.hi_b]
        self.got(4, lo)
        self.go(6, self.halves(lo)[0], self.halves(lo)[0], self.dev_b[0])
        self.got(5, hi)
        self.go(7, self.halves(hi)[1], self.halves(hi)[1], self.dev_b[1])

    def five(self):
        far = self.buf.at[(self.b + 2) % 4]
        self.got(6, self.halves(far)[0])
        self.got(7, self.halves(far)[1])

    def drain(self):
        for c in self.started:
            c.wait_send()


class Line:
    def __init__(self, number, axis, at, send, recv):
        dp, t, _, _ = place()
        x, y = dp // 4, dp % 4
        self.n, self.at, self.send, self.recv = number, at, send, recv
        self.a = x if axis == 0 else y

        def device(a):
            return (a * 4 + y if axis == 0 else x * 4 + a), t

        self.lo, self.hi, self.far = (self.a + 3) % 4, (self.a + 1) % 4, (self.a + 2) % 4
        self.devs = device(self.hi), device(self.lo)
        self.started = []

    def copy(self, k, ref, dev):
        return pltpu.make_async_remote_copy(
            src_ref=ref, dst_ref=ref, send_sem=self.send.at[self.n, k], recv_sem=self.recv.at[self.n, k],
            device_id=dev, device_id_type=MESH)

    def go(self, k, ref, dev):
        c = self.copy(k, ref, dev)
        c.start()
        self.started.append(c)

    def one(self):
        for k in range(2):
            self.go(k, self.at(self.a, 0, 8), self.devs[k])

    def two(self):
        self.copy(0, self.at(self.lo, 0, 8), self.devs[0]).wait_recv()
        self.go(2, self.at(self.lo, 0, 4), self.devs[0])
        self.copy(1, self.at(self.hi, 0, 8), self.devs[1]).wait_recv()
        self.go(3, self.at(self.hi, 4, 4), self.devs[1])

    def three(self):
        self.copy(2, self.at(self.far, 0, 4), self.devs[0]).wait_recv()
        self.copy(3, self.at(self.far, 4, 4), self.devs[1]).wait_recv()

    def drain(self):
        for c in self.started:
            c.wait_send()


def greet(peers):
    barrier = pltpu.get_barrier_semaphore()
    for peer in peers:
        pl.semaphore_signal(barrier, inc=1, device_id=peer, device_id_type=MESH)
    pl.semaphore_wait(barrier, len(peers))


def lanes(shape):
    return lax.broadcasted_iota(jnp.int32, shape, len(shape) - 1)


def row_starts(len_ref, first_row, shape):
    rows = first_row + lax.broadcasted_iota(jnp.int32, shape, 0)
    end = jnp.int32(0)
    req = jnp.zeros(shape, jnp.int32)
    start = jnp.zeros(shape, jnp.int32)
    for r in range(NREQ):
        size = len_ref[0, r]
        end = end + size
        past = rows >= end
        req = req + jnp.where(past, 1, 0)
        start = start + jnp.where(past, size, 0)
    return rows, req, start


def gather_kernel(h_ref, o_ref, pg_ref, up_ref, dn_ref, w_ref, gain_ref, len_ref, ra_ref, rp_ref, pt_ref,
                  q_out, kv_out, ob,
                  gh, pb, ub, db, wide, sel, tail, su, gains, trig,
                  zsend, zrecv, psend, precv, usend, urecv, xsend, xrecv, lsend, lrecv, local, dsend, drecv):
    dp, t, z, c = place()
    x, y = dp // 4, dp % 4
    greet([
        (dp, at_z(z, 1) * 2 + c), (dp, at_z(z, -1) * 2 + c), (dp, z * 2 + (1 - c)),
        (((x + 1) % 4) * 4 + y, t), (((x + 3) % 4) * 4 + y, t),
        (x * 4 + (y + 1) % 4, t), (x * 4 + (y + 3) % 4, t),
    ])
    ring = Ring([(slab(gh, 64 * k, 64), h_ref.at[pl.ds(64 * k, 64)]) for k in range(2)],
                zsend, zrecv, psend, precv)
    quarters = [(x, o_ref.at[pl.ds(pl.multiple_of(16 * x, 16), 16), pl.ds(0, D // 2)]),
                (y, o_ref.at[pl.ds(pl.multiple_of(16 * y, 16), 16), pl.ds(D // 2, D // 2)])]
    oring = Ring([(functools.partial(lambda part, j, zb, core: ob.at[part, j, zb, core], part, j), src)
                  for part, (j, src) in enumerate(quarters)], usend, urecv)
    lines = [Line(part, part, functools.partial(
        lambda part, j, z0, n: ob.at[part, j, pl.ds(z0, n), c], part), lsend, lrecv) for part in range(2)]
    adapters, pages = [], []
    for half in range(2):
        adapters.append(Plane(half, half, dn_ref.at[2 * c + half], db.at[c, half], xsend, xrecv, local))
        adapters.append(Plane(2 + half, half, up_ref.at[pl.ds(2 * half, 2)], ub.at[half], xsend, xrecv, local))
        pages.append(Plane(4 + half, half, pg_ref.at[pl.ds(2 * half, 2)], pb.at[half], xsend, xrecv, local))
    planes = adapters + pages
    oring.first()
    ring.first([0])
    for p in planes:
        p.one()
    owns = [pltpu.make_async_copy(h_ref, gh.at[t], local.at[6])]
    for part, (j, src) in enumerate(quarters):
        owns.append(pltpu.make_async_copy(src, ob.at[part, j, z, c], local.at[7 + part]))
    owns.append(pltpu.make_async_copy(
        w_ref.at[pl.ds(0, HW)], wide.at[pl.ds(128, HW)], local.at[9]))
    owns.append(pltpu.make_async_copy(
        w_ref.at[pl.ds(HW, 2 * HW)], wide.at[pl.ds(256, 2 * HW)], local.at[10]))
    for own in owns:
        own.start()
    oring.step(1)
    ring.first([1])
    for p in planes:
        p.two()
    for p in adapters:
        p.three()
        p.turn()
    for own in owns:
        own.wait()
    oring.step(2)
    ring.step(1, [0])

    lane = lanes((256, 128))
    low = lane < HW
    gains[...] = jnp.ones_like(gains)
    gains[:, 0:HW] = jnp.broadcast_to(gain_ref[...].reshape(1, HW), (8, HW))
    gain = gains[0:1, :]
    wide[192:256, :] = jnp.zeros((HW, D), BF16)
    tail[...] = jnp.zeros_like(tail)
    frequency = jnp.exp((lane % 32).astype(F32) * (-2.0 * math.log(10000.0) / HW))
    quarter = jnp.where(low, 0.0, 0.5 * math.pi)

    def waves(b):
        rows, _, start = row_starts(len_ref, b * 256, (256, 128))
        angle = (rows - start + PREFIX).astype(F32) * frequency
        trig[b] = jnp.cos(angle - quarter)

    pl.loop(0, 4)(waves)
    for p in pages:
        p.three()
    oring.step(3)
    ring.step(1, [1])
    for p in adapters:
        p.four()
    for p in pages:
        p.turn()
    pl.loop(4, 8)(waves)
    for p in adapters:
        p.five()
    other = (dp, z * 2 + (1 - c))

    def to_other(n, mine, theirs):
        send = pltpu.make_async_remote_copy(
            src_ref=mine, dst_ref=mine, send_sem=dsend.at[n], recv_sem=drecv.at[n],
            device_id=other, device_id_type=MESH)
        receive = pltpu.make_async_remote_copy(
            src_ref=theirs, dst_ref=theirs, send_sem=dsend.at[n], recv_sem=drecv.at[n],
            device_id=other, device_id_type=MESH)
        send.start()
        return send, receive

    swaps = [to_other(half, db.at[c, half], db.at[1 - c, half]) for half in range(2)]
    oring.step(4)
    for line in lines:
        line.one()
    ring.step(2, [0])

    def unit(v):
        total = jnp.sum(jnp.where(low, v * v, 0.0), axis=1, keepdims=True)
        return v * lax.rsqrt(total + EPS) * gain

    def slot(owner, half):
        a, b = owner // 4, owner % 4
        return b + half * (a - b), a + half * (b - a)

    def prefix(r):
        prompt = rp_ref[0, r]
        for j in range(4):
            page = pt_ref[j, prompt]
            half = (page % 4) // 2
            major, minor = slot(page // 4, half)
            raw = pb[half, major, minor, page % 2].astype(F32)
            low_p = lanes((64, 128)) < HW
            total = jnp.sum(jnp.where(low_p, raw * raw, 0.0), axis=1, keepdims=True)
            unit_key = raw * lax.rsqrt(total + EPS) * gain
            kv_out[pl.ds(pl.multiple_of(r * PREFIX + j * 64, 64), 64), :] = jnp.where(
                low_p, unit_key, raw).astype(BF16)

    for _, receive in swaps:
        receive.wait_recv()
    for r in range(NREQ):
        adapter = ra_ref[0, r]
        within = adapter % 4
        major, minor = slot(adapter // 4, within % 2)
        wide[r * RANK:(r + 1) * RANK, :] = db[within // 2, within % 2, major, minor]
        major, minor = slot(adapter // 4, within // 2)
        sel[r * RANK:(r + 1) * RANK, :] = ub[within // 2, major, minor, within % 2].astype(F32)
    first = sel[:, 0:128]
    tail[:, 0:HW] = sel[:, 128:192]
    low_s = lanes((128, 128)) < HW
    su[:, 0:128] = jnp.where(low_s, first, 0.0).astype(BF16)
    su[:, 128:256] = jnp.where(low_s, pltpu.roll(first, HW, 1), pltpu.roll(tail[...], HW, 1)).astype(BF16)

    def project(i):
        ring.from_core(i)
        zb = at_z(z, delta(i))
        values = gh[pl.ds(zb * 2, 2)].reshape(256, D)
        _, req, _ = row_starts(len_ref, zb * 256, (256, 128))
        every = lax.dot_general(values, wide[...], NT_DIMS, preferred_element_type=F32)
        middle = jnp.where(lane // RANK == req, every[:, 0:128], 0.0).astype(BF16)
        both = every[:, 128:384] + 0.5 * jnp.dot(middle, su[...], preferred_element_type=F32)
        wave = trig[zb]
        cosine = jnp.where(low, wave, 1.0)
        sine = pltpu.roll(wave, HW, 1)
        sine = jnp.where(lane < 32, -sine, jnp.where(low, sine, 0.0))

        def rotate(v):
            other = jnp.where(lane < 32, pltpu.roll(v, 96, 1), pltpu.roll(v, 32, 1))
            return v * cosine + other * sine

        query, key_value = both[:, :128], both[:, 128:]
        row = pl.multiple_of(zb * 256, 256)
        q_out[pl.ds(row, 256), :] = unit(rotate(query)).astype(BF16) * jnp.asarray(8.0, BF16)
        kv_out[pl.ds(row + NREQ * PREFIX, 256), :] = jnp.where(
            low, unit(rotate(key_value)), key_value).astype(BF16)

    pl.loop(0, 1)(project)
    ring.step(2, [1])
    pl.loop(1, 2)(project)
    for p in pages:
        p.four()
    pl.loop(2, 3)(project)
    ring.step(3, [0])
    for line in lines:
        line.two()
    pl.loop(3, 4)(project)
    ring.step(3, [1])
    for p in pages:
        p.five()
    pl.loop(4, 5)(project)
    pl.loop(0, NREQ)(prefix)
    pl.loop(5, 6)(project)
    ring.step(4)
    pl.loop(6, 8)(project)
    for line in lines:
        line.three()
    for part in [ring, oring] + planes + lines:
        part.drain()
    for send, _ in swaps:
        send.wait_send()


TILES = 2


def attend_kernel(q_ref, kv_ref, len_ref, out_ref, acc, begins):
    low = lanes((256, 128)) < HW
    begin = jnp.int32(0)
    for r in range(NREQ):
        begins[r] = begin
        begin = begin + len_ref[0, r]
    for r in range(NREQ, 2 * NREQ):
        begins[r] = jnp.int32(0)

    @pl.loop(0, NZ)
    def _(i):
        first = i * 256
        query = q_ref[pl.ds(pl.multiple_of(first, 256), 256), :]
        rows, _, start = row_starts(len_ref, first, (256, 256))
        end = jnp.int32(0)
        request_lo, request_hi, start_lo = jnp.int32(0), jnp.int32(0), jnp.int32(0)
        for r in range(NREQ):
            size = len_ref[0, r]
            end = end + size
            request_lo = request_lo + jnp.where(first >= end, 1, 0)
            start_lo = start_lo + jnp.where(first >= end, size, 0)
            request_hi = request_hi + jnp.where(first + 255 >= end, 1, 0)
        acc[...] = jnp.zeros_like(acc)
        lowest = start_lo // 256
        prefixes = request_hi + 1 - request_lo
        count = prefixes + i + 1 - lowest
        lane = lanes((256, 256))

        @pl.loop(0, (count + TILES - 1) // TILES)
        def _(n):
            total = None
            for u in range(TILES):
                m = jnp.minimum(n * TILES + u, count - 1)
                shared = m < prefixes
                tile = jnp.where(shared, request_lo + m, NREQ + lowest + m - prefixes)
                base = jnp.where(shared, begins[tile], (tile - NREQ) * 256)
                base = jnp.where(n * TILES + u < count, base, 2 * GROUP)
                column = jnp.where(shared, 0, 1) * lane + base
                keys = kv_ref[pl.ds(pl.multiple_of(tile * 256, 256), 256), :]
                score = lax.dot_general(query, keys, NT_DIMS, preferred_element_type=F32)
                weight = jnp.where((column >= start) & (column <= rows), jnp.exp(score), 0.0).astype(BF16)
                ones = jnp.where(low, jnp.asarray(1.0, BF16), keys)
                part = jnp.dot(weight, ones, preferred_element_type=F32)
                total = part if total is None else total + part
            acc[...] += total

        total = acc[...]
        result = total / pltpu.roll(total, HW, 1)
        for b in range(2):
            top, bottom = result[b * 128:b * 128 + 64], result[b * 128 + 64:b * 128 + 128]
            out_ref[2 * i + b] = jnp.where(lanes((64, 128)) >= HW, top, pltpu.roll(bottom, HW, 1)).astype(BF16)


def renorm(v):
    return v * lax.rsqrt(jnp.mean(v * v, axis=-1, keepdims=True) + EPS)


def mix_kernel(attn_ref, o_ref, h_ref, wu_ref, wg_ref, wd_ref, su_ref, sg_ref, ra_ref, sum_out, mixed_out,
               heads, lhs, om, wu, wg, wd, mixed, part, peer, rr, rl, sr, sl,
               asend, arecv, msend, mrecv, zsend, zrecv, psend, precv, qsend, qrecv, rsend, rrecv, local):
    dp, t, z, c = place()
    greet([(dp, (t + n) % NT) for n in range(1, NT)])
    started = []
    order = [8, 9, 7, 10, 6, 11, 5, 12, 4, 13, 3, 14, 2, 15, 1]
    for n in order:
        to = (t + n) % NT
        copy = pltpu.make_async_remote_copy(
            src_ref=attn_ref.at[to], dst_ref=heads.at[t], send_sem=asend.at[n], recv_sem=arecv.at[n],
            device_id=(dp, to), device_id_type=MESH)
        copy.start()
        started.append(copy)
    own = pltpu.make_async_copy(attn_ref.at[t], heads.at[t], local.at[11])
    own.start()
    eighths = [(part, j) for part in range(2) for j in range(4)]

    def place_in(part, j, core):
        return om.at[:, core, j, :, pl.ds(part * (D // 2), D // 2)]

    def matrix_copy(n, core):
        part, j = eighths[n]
        return pltpu.make_async_remote_copy(
            src_ref=o_ref.at[part, j, :, c], dst_ref=place_in(part, j, core), send_sem=msend.at[n],
            recv_sem=mrecv.at[n], device_id=(dp, z * 2 + (1 - c)), device_id_type=MESH)

    for n in range(8):
        copy = matrix_copy(n, c)
        copy.start()
        started.append(copy)
    moves = [(o_ref.at[part, j, :, c], place_in(part, j, c)) for part, j in eighths]
    moves += [(wu_ref, wu), (wg_ref, wg), (wd_ref, wd)]
    loads = [pltpu.make_async_copy(a, b, local.at[n]) for n, (a, b) in enumerate(moves)]
    for copy in loads:
        copy.start()
    base = h_ref[...].astype(F32)
    own.wait()
    for n in order:
        frm = (t + NT - n) % NT
        pltpu.make_async_remote_copy(
            src_ref=attn_ref.at[t], dst_ref=heads.at[frm], send_sem=asend.at[n], recv_sem=arecv.at[n],
            device_id=(dp, frm), device_id_type=MESH).wait_recv()
    high = lanes((64, 128)) >= HW
    for j in range(NT // 2):
        even, odd = heads[2 * j].astype(F32), heads[2 * j + 1].astype(F32)
        cols = slice(128 * j, 128 * j + 128)
        lhs[0:64, cols] = jnp.where(high, odd, pltpu.roll(even, HW, 1)).astype(BF16)
        lhs[64:128, cols] = jnp.where(high, pltpu.roll(odd, HW, 1), even).astype(BF16)
    for n in range(8):
        loads[n].wait()
        matrix_copy(n, 1 - c).wait_recv()
    attn_sum = jnp.dot(lhs[...], om[...].reshape(NT * HW, D), preferred_element_type=F32)
    rate = ra_ref[...].reshape(1, D)
    mine = renorm(base + rate * (renorm(attn_sum) - base)).astype(BF16)
    mixed[t] = mine
    ring = Ring([(slab(mixed, 32 * k, 32), mixed.at[t, pl.ds(32 * k, 32)]) for k in range(4)], zsend, zrecv, psend, precv)
    ring.first()
    mixed_out[...] = mine
    for copy in loads[8:]:
        copy.wait()
    scale_up, scale_gate = su_ref[...].reshape(1, 320), sg_ref[...].reshape(1, 320)

    def swap(i, zb):
        return pltpu.make_async_remote_copy(
            src_ref=part.at[zb * 2 + (1 - c)], dst_ref=peer.at[zb], send_sem=qsend.at[i], recv_sem=qrecv.at[i],
            device_id=(dp, z * 2 + (1 - c)), device_id_type=MESH)

    def feed(i):
        ring.from_core(i)
        zb = at_z(z, delta(i))
        values = mixed[pl.ds(zb * 2, 2)].reshape(256, D)
        up = lax.dot_general(values, wu[...], NT_DIMS, preferred_element_type=F32) * scale_up
        gate = lax.dot_general(values, wg[...], NT_DIMS, preferred_element_type=F32) * scale_gate
        units = (up * (gate / (1.0 + jnp.exp(-gate)))).astype(BF16)
        result = jnp.dot(units, wd[...], preferred_element_type=F32).astype(BF16)
        part[pl.ds(zb * 2, 2)] = result.reshape(2, ROWS, D)
        swap(i, zb).start()

    def local_sum(zb, k):
        rows = pl.ds(32 * k, 32)
        return part[zb * 2 + c, rows].astype(F32) + peer[zb, rows].astype(F32)

    def rs_copy(way, d, k, src):
        dst = (rr if way == 0 else rl).at[d - 1, pl.ds(32 * k, 32)]
        dev = (dp, at_z(z, 1 if way == 0 else -1) * 2 + c)
        return pltpu.make_async_remote_copy(
            src_ref=src, dst_ref=dst, send_sem=rsend.at[way, d - 1, k], recv_sem=rrecv.at[way, d - 1, k],
            device_id=dev, device_id_type=MESH)

    def pass_on(d, near, far):
        for n in ([2, 3] if near else []) + ([0, 1] if far else []):
            for way in range(2):
                k = (n + 2 * way) % 4
                rows = pl.ds(32 * k, 32)
                recv, sent = (rr, sr) if way == 0 else (rl, sl)
                value = local_sum(at_z(z, d if way == 0 else -d), k)
                if d < 3 or (d == 3 and n < 2):
                    rs_copy(way, d + 1, k, sent.at[d, rows]).wait_recv()
                    value = value + recv[d, rows].astype(F32)
                sent[d - 1, rows] = value.astype(BF16)
                copy = rs_copy(way, d, k, sent.at[d - 1, rows])
                copy.start()
                started.append(copy)

    def swapped(d):
        swap(2 * d - 1, at_z(z, -d)).wait_recv()
        if d < 4:
            swap(2 * d, at_z(z, d)).wait_recv()

    pl.loop(0, 1)(feed)
    ring.step(1)
    pl.loop(1, 3)(feed)
    ring.step(2)
    pl.loop(3, 5)(feed)
    ring.step(3)
    pl.loop(5, 7)(feed)
    swapped(3)
    pass_on(3, True, False)
    ring.step(4)
    pl.loop(7, 8)(feed)
    swapped(4)
    pass_on(4, False, True)
    pass_on(3, False, True)
    swapped(2)
    pass_on(2, True, True)
    swapped(1)
    pass_on(1, True, True)
    swap(0, z).wait_recv()
    for k in range(4):
        rows = pl.ds(32 * k, 32)
        value = local_sum(z, k)
        for way in range(2):
            rs_copy(way, 1, k, (sr if way == 0 else sl).at[0, rows]).wait_recv()
        sum_out[rows, :] = value + rr[0, rows].astype(F32) + rl[0, rows].astype(F32)
    ring.drain()
    for copy in started:
        copy.wait_send()
    for i in range(NZ):
        swap(i, at_z(z, delta(i))).wait_send()


def finish_kernel(sum_ref, mixed_ref, rate_ref, out_ref):
    base = mixed_ref[...].astype(F32)
    rate = rate_ref[...].reshape(1, D)
    out_ref[...] = renorm(base + rate * (renorm(sum_ref[...]) - base)).astype(BF16)


VM = pl.BlockSpec(memory_space=pltpu.VMEM)
SM = pl.BlockSpec(memory_space=pltpu.SMEM)
HB = pl.BlockSpec(memory_space=pl.ANY)
DMA = pltpu.SemaphoreType.DMA


def stay(array):
    return pltpu.with_memory_space_constraint(array, pltpu.VMEM)


def far(array):
    return pltpu.with_memory_space_constraint(array, pltpu.HBM)


def local(hidden, lengths, request_prompt, request_adapter, prompt_page_table, prefix_page_cache,
          query_key_value_weight, adapter_down, adapter_up, attention_scale, output_matrix, attention_rate,
          up_matrix, gate_matrix, up_scaling, gate_scaling, down_matrix, feedforward_rate):
    lengths = far(lengths)
    queries, key_values, matrix = pl.pallas_call(
        gather_kernel,
        out_shape=(
            pltpu.VMEM((GROUP, 128), BF16),
            pltpu.VMEM((NREQ * PREFIX + GROUP, 128), BF16),
            pltpu.VMEM((2, 4, NZ, 2, 16, D // 2), BF16),
        ),
        in_specs=[HB, HB, HB, HB, HB, HB, VM, SM, SM, SM, SM],
        out_specs=(VM, VM, VM),
        scratch_shapes=[
            pltpu.VMEM((NT, ROWS, D), BF16),
            pltpu.VMEM((2, 4, 4, 2, 64, 128), BF16),
            pltpu.VMEM((2, 4, 4, 2, RANK, 192), BF16),
            pltpu.VMEM((2, 2, 4, 4, RANK, D), BF16),
            pltpu.VMEM((384, D), BF16),
            pltpu.VMEM((128, 192), F32),
            pltpu.VMEM((128, 128), F32),
            pltpu.VMEM((128, 256), BF16),
            pltpu.VMEM((8, 128), F32),
            pltpu.VMEM((NZ, 256, 128), F32),
            DMA((2, 4, 2)), DMA((2, 4, 2)), DMA((8, 2)), DMA((8, 2)), DMA((2, 4, 2)), DMA((2, 4, 2)),
            DMA((6, 8)), DMA((6, 8)), DMA((2, 4)), DMA((2, 4)), DMA((11,)), DMA((2,)), DMA((2,)),
        ],
        compiler_params=pltpu.CompilerParams(
            collective_id=0, has_side_effects=True, vmem_limit_bytes=32 * 2**20),
        name="gather_project",
    )(*[far(a) for a in (
        hidden, output_matrix, prefix_page_cache, adapter_up, jnp.swapaxes(adapter_down, 1, 2),
        query_key_value_weight.T, attention_scale)],
      lengths, *[far(a) for a in (request_adapter, request_prompt, prompt_page_table.T)])
    attn = pl.pallas_call(
        attend_kernel,
        out_shape=pltpu.VMEM((NT, 64, 128), BF16),
        in_specs=[VM, VM, SM],
        out_specs=VM,
        scratch_shapes=[pltpu.VMEM((256, 128), F32), pltpu.SMEM((2 * NREQ,), jnp.int32)],
        compiler_params=pltpu.CompilerParams(vmem_limit_bytes=16 * 2**20),
        name="attend",
    )(stay(queries), stay(key_values), lengths)
    sums, mixed = pl.pallas_call(
        mix_kernel,
        out_shape=(pltpu.VMEM((ROWS, D), F32), pltpu.VMEM((ROWS, D), BF16)),
        in_specs=[VM, VM, VM, HB, HB, HB, VM, VM, VM],
        out_specs=(VM, VM),
        scratch_shapes=[
            pltpu.VMEM((NT, 64, 128), BF16),
            pltpu.VMEM((ROWS, NT * HW), BF16),
            pltpu.VMEM((NZ, 2, 4, 16, D), BF16),
            pltpu.VMEM((320, D), BF16),
            pltpu.VMEM((320, D), BF16),
            pltpu.VMEM((320, D), BF16),
            pltpu.VMEM((NT, ROWS, D), BF16),
            pltpu.VMEM((NT, ROWS, D), BF16),
            pltpu.VMEM((NZ, ROWS, D), BF16),
            pltpu.VMEM((4, ROWS, D), BF16), pltpu.VMEM((4, ROWS, D), BF16),
            pltpu.VMEM((4, ROWS, D), BF16), pltpu.VMEM((4, ROWS, D), BF16),
            DMA((16,)), DMA((16,)), DMA((8,)), DMA((8,)),
            DMA((2, 4, 4)), DMA((2, 4, 4)), DMA((8, 4)), DMA((8, 4)),
            DMA((8,)), DMA((8,)), DMA((2, 4, 4)), DMA((2, 4, 4)), DMA((12,)),
        ],
        compiler_params=pltpu.CompilerParams(
            collective_id=1, has_side_effects=True, vmem_limit_bytes=44 * 2**20),
        name="mix_feed",
    )(stay(attn), stay(matrix), hidden, up_matrix.T, gate_matrix.T, down_matrix,
      up_scaling, gate_scaling, attention_rate)
    return pl.pallas_call(
        finish_kernel,
        out_shape=jax.ShapeDtypeStruct((ROWS, D), BF16),
        in_specs=[VM, VM, VM],
        out_specs=VM,
        compiler_params=pltpu.CompilerParams(vmem_limit_bytes=16 * 2**20),
        name="finish",
    )(stay(sums), stay(mixed), feedforward_rate)


def solution(mesh):
    placed = (
        P(("dp", "tensor"), None),
        P("dp", None),
        P("dp", None),
        P("dp", None),
        P(),
        P("dp", None, "tensor"),
        P(None, "tensor"),
        P("dp", None, None),
        P("dp", None, "tensor"),
        P("tensor"),
        P("tensor", None),
        P(),
        P(None, "tensor"),
        P(None, "tensor"),
        P("tensor"),
        P("tensor"),
        P("tensor", None),
        P(),
    )
    return jax.shard_map(
        local, mesh=mesh, in_specs=placed, out_specs=P(("dp", "tensor"), None), check_vma=False
    )
```

```python
import functools
import math

import jax
import jax.numpy as jnp
from jax import lax
from jax.experimental import pallas as pl
from jax.experimental.pallas import tpu as pltpu
from jax.sharding import PartitionSpec as P

MESH = pl.DeviceIdType.MESH
D = 1280
HW = 64
RANK = 16
NREQ = 8
PREFIX = 256
NT = 16
NZ = 8
ROWS = 128
GROUP = 2048
EPS = 1e-06
F32 = jnp.float32
BF16 = jnp.bfloat16
NT_DIMS = (((1,), (1,)), ((), ()))


def place():
    dp = lax.axis_index("dp")
    t = lax.axis_index("tensor")
    return dp, t, t // 2, t % 2


def delta(i):
    half = (i + 1) // 2
    odd = i % 2
    return half * (1 - 2 * odd)


def at_z(z, d):
    return (z + d + NZ) % NZ


class Ring:
    def __init__(self, chunks, zsend, zrecv, psend=None, precv=None, in_order=False):
        self.dp, _, self.z, self.c = place()
        self.chunks, self.zsend, self.zrecv = chunks, zsend, zrecv
        self.psend, self.precv, self.in_order = psend, precv, in_order
        self.started = []
        self.next = (self.dp, at_z(self.z, 1) * 2 + self.c), (self.dp, at_z(self.z, -1) * 2 + self.c)
        self.other = (self.dp, self.z * 2 + (1 - self.c))

    def spot(self, k, zb, core):
        return self.chunks[k][0](zb, core)

    def ring_copy(self, way, step, k, src, zb):
        return pltpu.make_async_remote_copy(
            src_ref=src, dst_ref=self.spot(k, zb, self.c),
            send_sem=self.zsend.at[way, step - 1, k], recv_sem=self.zrecv.at[way, step - 1, k],
            device_id=self.next[way], device_id_type=MESH)

    def core_copy(self, i, k, src, zb, core):
        return pltpu.make_async_remote_copy(
            src_ref=src, dst_ref=self.spot(k, zb, core),
            send_sem=self.psend.at[i, k], recv_sem=self.precv.at[i, k],
            device_id=self.other, device_id_type=MESH)

    def go(self, copy):
        copy.start()
        self.started.append(copy)

    def turn(self, n):
        return (n, n) if self.in_order else (n, n + 1 - 2 * (n % 2))

    def start(self, ks):
        for k in ks:
            for way in range(2):
                self.go(self.ring_copy(way, 1, k, self.chunks[k][1], self.z))
            self.go(self.core_copy(0, k, self.chunks[k][1], self.z, self.c))

    def first(self, ns=None):
        ns = range(len(self.chunks)) if ns is None else ns
        for n in ns:
            for way, k in enumerate(self.turn(n)):
                self.go(self.ring_copy(way, 1, k, self.chunks[k][1], self.z))
        if self.psend is not None:
            for n in ns:
                self.go(self.core_copy(0, n, self.chunks[n][1], self.z, self.c))

    def step(self, s, ns=None):
        for n in range(len(self.chunks)) if ns is None else ns:
            for way, k in enumerate(self.turn(n)):
                far = k % 2 == way
                if s == 4 and not far:
                    continue
                zb = at_z(self.z, -s if way == 0 else s)
                here = self.spot(k, zb, self.c)
                self.ring_copy(way, s, k, here, zb).wait_recv()
                if s < 3 or (s == 3 and far):
                    self.go(self.ring_copy(way, s + 1, k, here, zb))
                if self.psend is not None:
                    i = 7 if s == 4 else (2 * s - 1 if way == 0 else 2 * s)
                    self.go(self.core_copy(i, k, here, zb, self.c))

    def from_core(self, i):
        zb = at_z(self.z, delta(i))
        for k in range(len(self.chunks)):
            self.core_copy(i, k, self.spot(k, zb, 1 - self.c), zb, 1 - self.c).wait_recv()

    def drain(self):
        for copy in self.started:
            copy.wait_send()


def slab(buf, first_row, rows):
    return lambda zb, core: buf.at[zb * 2 + core, pl.ds(first_row, rows)]


class Plane:
    def __init__(self, number, first_axis, src, buf, send, recv, local):
        dp, t, _, _ = place()
        x, y = dp // 4, dp % 4
        self.src, self.buf, self.n, self.send, self.recv, self.local = src, buf, number, send, recv, local
        self.a, self.b = (x, y) if first_axis == 0 else (y, x)

        def device(a, b):
            return (a * 4 + b if first_axis == 0 else b * 4 + a), t

        up_a, down_a = (self.a + 1) % 4, (self.a + 3) % 4
        up_b, down_b = (self.b + 1) % 4, (self.b + 3) % 4
        self.lo_a, self.hi_a, self.lo_b, self.hi_b = down_a, up_a, down_b, up_b
        self.dev_a = device(up_a, self.b), device(down_a, self.b)
        self.dev_b = device(self.a, up_b), device(self.a, down_b)
        self.started = []

    def copy(self, k, src, dst, dev):
        return pltpu.make_async_remote_copy(
            src_ref=src, dst_ref=dst, send_sem=self.send.at[self.n, k], recv_sem=self.recv.at[self.n, k],
            device_id=dev, device_id_type=MESH)

    def go(self, k, src, dst, dev):
        c = self.copy(k, src, dst, dev)
        c.start()
        self.started.append(c)

    def got(self, k, dst):
        self.copy(k, dst, dst, self.dev_a[0]).wait_recv()

    def halves(self, ref):
        if len(ref.shape) == 2:
            n = ref.shape[1] // 2
            return ref.at[:, pl.ds(0, n)], ref.at[:, pl.ds(n, n)]
        n = ref.shape[0] // 2
        return ref.at[pl.ds(0, n)], ref.at[pl.ds(n, n)]

    def one(self):
        mine = self.buf.at[self.b, self.a]
        self.own = pltpu.make_async_copy(self.src, mine, self.local.at[self.n])
        self.own.start()
        self.go(0, self.src, mine, self.dev_a[0])
        self.go(1, self.src, mine, self.dev_a[1])

    def two(self):
        lo, hi = self.buf.at[self.b, self.lo_a], self.buf.at[self.b, self.hi_a]
        self.got(0, lo)
        self.go(2, self.halves(lo)[0], self.halves(lo)[0], self.dev_a[0])
        self.got(1, hi)
        self.go(3, self.halves(hi)[1], self.halves(hi)[1], self.dev_a[1])

    def three(self):
        far = self.buf.at[self.b, (self.a + 2) % 4]
        self.got(2, self.halves(far)[0])
        self.got(3, self.halves(far)[1])
        self.own.wait()

    def turn(self):
        row = self.buf.at[self.b]
        self.go(4, row, row, self.dev_b[0])
        self.go(5, row, row, self.dev_b[1])

    def four(self):
        lo, hi = self.buf.at[self.lo_b], self.buf.at[self.hi_b]
        self.got(4, lo)
        self.go(6, self.halves(lo)[0], self.halves(lo)[0], self.dev_b[0])
        self.got(5, hi)
        self.go(7, self.halves(hi)[1], self.halves(hi)[1], self.dev_b[1])

    def five(self):
        far = self.buf.at[(self.b + 2) % 4]
        self.got(6, self.halves(far)[0])
        self.got(7, self.halves(far)[1])

    def drain(self):
        for c in self.started:
            c.wait_send()


class Line:
    def __init__(self, number, axis, at, send, recv):
        dp, t, _, _ = place()
        x, y = dp // 4, dp % 4
        self.n, self.at, self.send, self.recv = number, at, send, recv
        self.a = x if axis == 0 else y

        def device(a):
            return (a * 4 + y if axis == 0 else x * 4 + a), t

        self.lo, self.hi, self.far = (self.a + 3) % 4, (self.a + 1) % 4, (self.a + 2) % 4
        self.devs = device(self.hi), device(self.lo)
        self.started = []

    def copy(self, k, ref, dev):
        return pltpu.make_async_remote_copy(
            src_ref=ref, dst_ref=ref, send_sem=self.send.at[self.n, k], recv_sem=self.recv.at[self.n, k],
            device_id=dev, device_id_type=MESH)

    def go(self, k, ref, dev):
        c = self.copy(k, ref, dev)
        c.start()
        self.started.append(c)

    def one(self):
        for k in range(2):
            self.go(k, self.at(self.a, 0, 8), self.devs[k])

    def two(self):
        self.copy(0, self.at(self.lo, 0, 8), self.devs[0]).wait_recv()
        self.go(2, self.at(self.lo, 0, 4), self.devs[0])
        self.copy(1, self.at(self.hi, 0, 8), self.devs[1]).wait_recv()
        self.go(3, self.at(self.hi, 4, 4), self.devs[1])

    def three(self):
        self.copy(2, self.at(self.far, 0, 4), self.devs[0]).wait_recv()
        self.copy(3, self.at(self.far, 4, 4), self.devs[1]).wait_recv()

    def drain(self):
        for c in self.started:
            c.wait_send()


def greet(peers):
    barrier = pltpu.get_barrier_semaphore()
    for peer in peers:
        pl.semaphore_signal(barrier, inc=1, device_id=peer, device_id_type=MESH)
    pl.semaphore_wait(barrier, len(peers))


def lanes(shape):
    return lax.broadcasted_iota(jnp.int32, shape, len(shape) - 1)


def row_starts(len_ref, first_row, shape):
    rows = first_row + lax.broadcasted_iota(jnp.int32, shape, 0)
    end = jnp.int32(0)
    req = jnp.zeros(shape, jnp.int32)
    start = jnp.zeros(shape, jnp.int32)
    for r in range(NREQ):
        size = len_ref[0, r]
        end = end + size
        past = rows >= end
        req = req + jnp.where(past, 1, 0)
        start = start + jnp.where(past, size, 0)
    return rows, req, start


def gather_kernel(h_ref, o_ref, pg_ref, up_ref, dn_ref, w_ref, gain_ref, len_ref, ra_ref, rp_ref, pt_ref,
                  q_out, kv_out, ob,
                  gh, pb, ub, db, wide, sel, tail, su, gains, trig,
                  zsend, zrecv, psend, precv, usend, urecv, xsend, xrecv, lsend, lrecv, local, dsend, drecv):
    dp, t, z, c = place()
    x, y = dp // 4, dp % 4
    greet([
        (dp, at_z(z, 1) * 2 + c), (dp, at_z(z, -1) * 2 + c), (dp, z * 2 + (1 - c)),
        (((x + 1) % 4) * 4 + y, t), (((x + 3) % 4) * 4 + y, t),
        (x * 4 + (y + 1) % 4, t), (x * 4 + (y + 3) % 4, t),
    ])
    ring = Ring([(slab(gh, 64 * k, 64), h_ref.at[pl.ds(64 * k, 64)]) for k in range(2)],
                zsend, zrecv, psend, precv)
    quarters = [(x, o_ref.at[pl.ds(pl.multiple_of(16 * x, 16), 16), pl.ds(0, D // 2)]),
                (y, o_ref.at[pl.ds(pl.multiple_of(16 * y, 16), 16), pl.ds(D // 2, D // 2)])]
    oring = Ring([(functools.partial(lambda part, j, zb, core: ob.at[part, j, zb, core], part, j), src)
                  for part, (j, src) in enumerate(quarters)], usend, urecv)
    lines = [Line(part, part, functools.partial(
        lambda part, j, z0, n: ob.at[part, j, pl.ds(z0, n), c], part), lsend, lrecv) for part in range(2)]
    adapters, pages = [], []
    for half in range(2):
        adapters.append(Plane(half, half, dn_ref.at[2 * c + half], db.at[c, half], xsend, xrecv, local))
        adapters.append(Plane(2 + half, half, up_ref.at[pl.ds(2 * half, 2)], ub.at[half], xsend, xrecv, local))
        pages.append(Plane(4 + half, half, pg_ref.at[pl.ds(2 * half, 2)], pb.at[half], xsend, xrecv, local))
    planes = adapters + pages
    oring.first()
    ring.first([0])
    for p in planes:
        p.one()
    owns = [pltpu.make_async_copy(h_ref, gh.at[t], local.at[6])]
    for part, (j, src) in enumerate(quarters):
        owns.append(pltpu.make_async_copy(src, ob.at[part, j, z, c], local.at[7 + part]))
    owns.append(pltpu.make_async_copy(
        w_ref.at[pl.ds(0, HW)], wide.at[pl.ds(128, HW)], local.at[9]))
    owns.append(pltpu.make_async_copy(
        w_ref.at[pl.ds(HW, 2 * HW)], wide.at[pl.ds(256, 2 * HW)], local.at[10]))
    for own in owns:
        own.start()
    oring.step(1)
    ring.first([1])
    for p in planes:
        p.two()
    for p in adapters:
        p.three()
        p.turn()
    for own in owns:
        own.wait()
    oring.step(2)
    ring.step(1, [0])

    lane = lanes((256, 128))
    low = lane < HW
    gains[...] = jnp.ones_like(gains)
    gains[:, 0:HW] = jnp.broadcast_to(gain_ref[...].reshape(1, HW), (8, HW))
    gain = gains[0:1, :]
    wide[192:256, :] = jnp.zeros((HW, D), BF16)
    tail[...] = jnp.zeros_like(tail)
    frequency = jnp.exp((lane % 32).astype(F32) * (-2.0 * math.log(10000.0) / HW))
    quarter = jnp.where(low, 0.0, 0.5 * math.pi)

    def waves(b):
        rows, _, start = row_starts(len_ref, b * 256, (256, 128))
        angle = (rows - start + PREFIX).astype(F32) * frequency
        trig[b] = jnp.cos(angle - quarter)

    pl.loop(0, 4)(waves)
    for p in pages:
        p.three()
    oring.step(3)
    ring.step(1, [1])
    for p in adapters:
        p.four()
    for p in pages:
        p.turn()
    pl.loop(4, 8)(waves)
    for p in adapters:
        p.five()
    other = (dp, z * 2 + (1 - c))

    def to_other(n, mine, theirs):
        send = pltpu.make_async_remote_copy(
            src_ref=mine, dst_ref=mine, send_sem=dsend.at[n], recv_sem=drecv.at[n],
            device_id=other, device_id_type=MESH)
        receive = pltpu.make_async_remote_copy(
            src_ref=theirs, dst_ref=theirs, send_sem=dsend.at[n], recv_sem=drecv.at[n],
            device_id=other, device_id_type=MESH)
        send.start()
        return send, receive

    swaps = [to_other(half, db.at[c, half], db.at[1 - c, half]) for half in range(2)]
    oring.step(4)
    for line in lines:
        line.one()
    ring.step(2, [0])

    def unit(v):
        total = jnp.sum(jnp.where(low, v * v, 0.0), axis=1, keepdims=True)
        return v * lax.rsqrt(total + EPS) * gain

    def slot(owner, half):
        a, b = owner // 4, owner % 4
        return b + half * (a - b), a + half * (b - a)

    def prefix(r):
        prompt = rp_ref[0, r]
        for j in range(4):
            page = pt_ref[j, prompt]
            half = (page % 4) // 2
            major, minor = slot(page // 4, half)
            raw = pb[half, major, minor, page % 2].astype(F32)
            low_p = lanes((64, 128)) < HW
            total = jnp.sum(jnp.where(low_p, raw * raw, 0.0), axis=1, keepdims=True)
            unit_key = raw * lax.rsqrt(total + EPS) * gain
            kv_out[pl.ds(pl.multiple_of(r * PREFIX + j * 64, 64), 64), :] = jnp.where(
                low_p, unit_key, raw).astype(BF16)

    for _, receive in swaps:
        receive.wait_recv()
    for r in range(NREQ):
        adapter = ra_ref[0, r]
        within = adapter % 4
        major, minor = slot(adapter // 4, within % 2)
        wide[r * RANK:(r + 1) * RANK, :] = db[within // 2, within % 2, major, minor]
        major, minor = slot(adapter // 4, within // 2)
        sel[r * RANK:(r + 1) * RANK, :] = ub[within // 2, major, minor, within % 2].astype(F32)
    first = sel[:, 0:128]
    tail[:, 0:HW] = sel[:, 128:192]
    low_s = lanes((128, 128)) < HW
    su[:, 0:128] = jnp.where(low_s, first, 0.0).astype(BF16)
    su[:, 128:256] = jnp.where(low_s, pltpu.roll(first, HW, 1), pltpu.roll(tail[...], HW, 1)).astype(BF16)

    def project(i):
        ring.from_core(i)
        zb = at_z(z, delta(i))
        values = gh[pl.ds(zb * 2, 2)].reshape(256, D)
        _, req, _ = row_starts(len_ref, zb * 256, (256, 128))
        every = lax.dot_general(values, wide[...], NT_DIMS, preferred_element_type=F32)
        middle = jnp.where(lane // RANK == req, every[:, 0:128], 0.0).astype(BF16)
        both = every[:, 128:384] + 0.5 * jnp.dot(middle, su[...], preferred_element_type=F32)
        wave = trig[zb]
        cosine = jnp.where(low, wave, 1.0)
        sine = pltpu.roll(wave, HW, 1)
        sine = jnp.where(lane < 32, -sine, jnp.where(low, sine, 0.0))

        def rotate(v):
            other = jnp.where(lane < 32, pltpu.roll(v, 96, 1), pltpu.roll(v, 32, 1))
            return v * cosine + other * sine

        query, key_value = both[:, :128], both[:, 128:]
        row = pl.multiple_of(zb * 256, 256)
        q_out[pl.ds(row, 256), :] = unit(rotate(query)).astype(BF16) * jnp.asarray(8.0, BF16)
        kv_out[pl.ds(row + NREQ * PREFIX, 256), :] = jnp.where(
            low, unit(rotate(key_value)), key_value).astype(BF16)

    pl.loop(0, 1)(project)
    ring.step(2, [1])
    pl.loop(1, 2)(project)
    for p in pages:
        p.four()
    pl.loop(2, 3)(project)
    ring.step(3, [0])
    for line in lines:
        line.two()
    pl.loop(3, 5)(project)
    ring.step(3, [1])
    for p in pages:
        p.five()
    pl.loop(5, 7)(project)
    ring.step(4)
    pl.loop(0, NREQ)(prefix)
    pl.loop(7, 8)(project)
    for line in lines:
        line.three()
    for part in [ring, oring] + planes + lines:
        part.drain()
    for send, _ in swaps:
        send.wait_send()


TILES = 2


def attend_kernel(q_ref, kv_ref, len_ref, out_ref, acc, begins):
    low = lanes((256, 128)) < HW
    begin = jnp.int32(0)
    for r in range(NREQ):
        begins[r] = begin
        begin = begin + len_ref[0, r]
    for r in range(NREQ, 2 * NREQ):
        begins[r] = jnp.int32(0)

    @pl.loop(0, NZ)
    def _(i):
        first = i * 256
        query = q_ref[pl.ds(pl.multiple_of(first, 256), 256), :]
        rows, _, start = row_starts(len_ref, first, (256, 256))
        end = jnp.int32(0)
        request_lo, request_hi, start_lo = jnp.int32(0), jnp.int32(0), jnp.int32(0)
        for r in range(NREQ):
            size = len_ref[0, r]
            end = end + size
            request_lo = request_lo + jnp.where(first >= end, 1, 0)
            start_lo = start_lo + jnp.where(first >= end, size, 0)
            request_hi = request_hi + jnp.where(first + 255 >= end, 1, 0)
        acc[...] = jnp.zeros_like(acc)
        lowest = start_lo // 256
        prefixes = request_hi + 1 - request_lo
        count = prefixes + i + 1 - lowest
        lane = lanes((256, 256))

        @pl.loop(0, (count + TILES - 1) // TILES)
        def _(n):
            total = None
            for u in range(TILES):
                m = jnp.minimum(n * TILES + u, count - 1)
                shared = m < prefixes
                tile = jnp.where(shared, request_lo + m, NREQ + lowest + m - prefixes)
                base = jnp.where(shared, begins[tile], (tile - NREQ) * 256)
                base = jnp.where(n * TILES + u < count, base, 2 * GROUP)
                column = jnp.where(shared, 0, 1) * lane + base
                keys = kv_ref[pl.ds(pl.multiple_of(tile * 256, 256), 256), :]
                score = lax.dot_general(query, keys, NT_DIMS, preferred_element_type=F32)
                weight = jnp.where((column >= start) & (column <= rows), jnp.exp(score), 0.0).astype(BF16)
                ones = jnp.where(low, jnp.asarray(1.0, BF16), keys)
                part = jnp.dot(weight, ones, preferred_element_type=F32)
                total = part if total is None else total + part
            acc[...] += total

        total = acc[...]
        result = total / pltpu.roll(total, HW, 1)
        for b in range(4):
            top, bottom = result[b * 64:b * 64 + 32], result[b * 64 + 32:b * 64 + 64]
            out_ref[2 * i + b // 2, b % 2] = jnp.where(
                lanes((32, 128)) >= HW, top, pltpu.roll(bottom, HW, 1)).astype(BF16)


def renorm(v):
    return v * lax.rsqrt(jnp.mean(v * v, axis=-1, keepdims=True) + EPS)


def mix_kernel(attn_ref, o_ref, h_ref, wu_ref, wg_ref, wd_ref, su_ref, sg_ref, ra_ref, sum_out, mixed_out,
               heads, lhs, om, wu, wg, wd, mixed, part, peer, rr, rl, sr, sl,
               asend, arecv, msend, mrecv, zsend, zrecv, psend, precv, qsend, qrecv, rsend, rrecv, local):
    dp, t, z, c = place()
    greet([(dp, (t + n) % NT) for n in range(1, NT)])
    started = []
    order = [8, 9, 7, 10, 6, 11, 5, 12, 4, 13, 3, 14, 2, 15, 1]

    def exchange(half, n, to, origin):
        return pltpu.make_async_remote_copy(
            src_ref=attn_ref.at[to, half], dst_ref=heads.at[half, origin], send_sem=asend.at[half, n],
            recv_sem=arecv.at[half, n], device_id=(dp, to), device_id_type=MESH)

    for half in range(2):
        for n in order:
            copy = exchange(half, n, (t + n) % NT, t)
            copy.start()
            started.append(copy)
    owns = [pltpu.make_async_copy(attn_ref.at[t, half], heads.at[half, t], local.at[11 + half])
            for half in range(2)]
    for own in owns:
        own.start()
    eighths = [(part, j) for part in range(2) for j in range(4)]

    def place_in(part, j, core):
        return om.at[:, core, j, :, pl.ds(part * (D // 2), D // 2)]

    def matrix_copy(n, core):
        part, j = eighths[n]
        return pltpu.make_async_remote_copy(
            src_ref=o_ref.at[part, j, :, c], dst_ref=place_in(part, j, core), send_sem=msend.at[n],
            recv_sem=mrecv.at[n], device_id=(dp, z * 2 + (1 - c)), device_id_type=MESH)

    for n in range(8):
        copy = matrix_copy(n, c)
        copy.start()
        started.append(copy)
    moves = [(o_ref.at[part, j, :, c], place_in(part, j, c)) for part, j in eighths]
    moves += [(wu_ref, wu), (wg_ref, wg), (wd_ref, wd)]
    loads = [pltpu.make_async_copy(a, b, local.at[n]) for n, (a, b) in enumerate(moves)]
    for copy in loads:
        copy.start()
    rate = ra_ref[...].reshape(1, D)
    high = lanes((32, 128)) >= HW
    ring = Ring([(slab(mixed, 32 * k, 32), mixed.at[t, pl.ds(32 * k, 32)]) for k in range(4)],
                zsend, zrecv, psend, precv, in_order=True)
    for half in range(2):
        owns[half].wait()
        for n in order:
            frm = (t + NT - n) % NT
            exchange(half, n, t, frm).wait_recv()
        for j in range(NT // 2):
            even, odd = heads[half, 2 * j].astype(F32), heads[half, 2 * j + 1].astype(F32)
            cols = slice(128 * j, 128 * j + 128)
            lhs[0:32, cols] = jnp.where(high, odd, pltpu.roll(even, HW, 1)).astype(BF16)
            lhs[32:64, cols] = jnp.where(high, pltpu.roll(odd, HW, 1), even).astype(BF16)
        if half == 0:
            for n in range(8):
                loads[n].wait()
                matrix_copy(n, 1 - c).wait_recv()
        attn_sum = jnp.dot(lhs[...], om[...].reshape(NT * HW, D), preferred_element_type=F32)
        rows = slice(64 * half, 64 * half + 64)
        base = h_ref[rows, :].astype(F32)
        mine = renorm(base + rate * (renorm(attn_sum) - base)).astype(BF16)
        mixed[t, rows] = mine
        ring.start([2 * half, 2 * half + 1])
        mixed_out[rows, :] = mine
    for copy in loads[8:]:
        copy.wait()
    scale_up, scale_gate = su_ref[...].reshape(1, 320), sg_ref[...].reshape(1, 320)

    def swap(i, zb):
        return pltpu.make_async_remote_copy(
            src_ref=part.at[zb * 2 + (1 - c)], dst_ref=peer.at[zb], send_sem=qsend.at[i], recv_sem=qrecv.at[i],
            device_id=(dp, z * 2 + (1 - c)), device_id_type=MESH)

    def feed(i):
        ring.from_core(i)
        zb = at_z(z, delta(i))
        values = mixed[pl.ds(zb * 2, 2)].reshape(256, D)
        up = lax.dot_general(values, wu[...], NT_DIMS, preferred_element_type=F32) * scale_up
        gate = lax.dot_general(values, wg[...], NT_DIMS, preferred_element_type=F32) * scale_gate
        units = (up * (gate / (1.0 + jnp.exp(-gate)))).astype(BF16)
        result = jnp.dot(units, wd[...], preferred_element_type=F32).astype(BF16)
        part[pl.ds(zb * 2, 2)] = result.reshape(2, ROWS, D)
        swap(i, zb).start()

    def local_sum(zb, k):
        rows = pl.ds(32 * k, 32)
        return part[zb * 2 + c, rows].astype(F32) + peer[zb, rows].astype(F32)

    def rs_copy(way, d, k, src):
        dst = (rr if way == 0 else rl).at[d - 1, pl.ds(32 * k, 32)]
        dev = (dp, at_z(z, 1 if way == 0 else -1) * 2 + c)
        return pltpu.make_async_remote_copy(
            src_ref=src, dst_ref=dst, send_sem=rsend.at[way, d - 1, k], recv_sem=rrecv.at[way, d - 1, k],
            device_id=dev, device_id_type=MESH)

    def pass_on(d, near, far):
        for n in ([2, 3] if near else []) + ([0, 1] if far else []):
            for way in range(2):
                k = way + 2 * n if n < 2 else 1 - way + 2 * (n - 2)
                rows = pl.ds(32 * k, 32)
                recv, sent = (rr, sr) if way == 0 else (rl, sl)
                value = local_sum(at_z(z, d if way == 0 else -d), k)
                if d < 3 or (d == 3 and n < 2):
                    rs_copy(way, d + 1, k, sent.at[d, rows]).wait_recv()
                    value = value + recv[d, rows].astype(F32)
                sent[d - 1, rows] = value.astype(BF16)
                copy = rs_copy(way, d, k, sent.at[d - 1, rows])
                copy.start()
                started.append(copy)

    def swapped(d):
        swap(2 * d - 1, at_z(z, -d)).wait_recv()
        if d < 4:
            swap(2 * d, at_z(z, d)).wait_recv()

    pl.loop(0, 1)(feed)
    ring.step(1)
    pl.loop(1, 3)(feed)
    ring.step(2)
    pl.loop(3, 5)(feed)
    ring.step(3)
    pl.loop(5, 7)(feed)
    ring.step(4)
    swapped(3)
    pass_on(3, True, False)
    pl.loop(7, 8)(feed)
    swapped(4)
    pass_on(4, False, True)
    pass_on(3, False, True)
    swapped(2)
    pass_on(2, True, True)
    swapped(1)
    pass_on(1, True, True)
    swap(0, z).wait_recv()
    for k in range(4):
        rows = pl.ds(32 * k, 32)
        value = local_sum(z, k)
        for way in range(2):
            rs_copy(way, 1, k, (sr if way == 0 else sl).at[0, rows]).wait_recv()
        sum_out[rows, :] = value + rr[0, rows].astype(F32) + rl[0, rows].astype(F32)
    ring.drain()
    for copy in started:
        copy.wait_send()
    for i in range(NZ):
        swap(i, at_z(z, delta(i))).wait_send()


def finish_kernel(sum_ref, mixed_ref, rate_ref, out_ref):
    base = mixed_ref[...].astype(F32)
    rate = rate_ref[...].reshape(1, D)
    out_ref[...] = renorm(base + rate * (renorm(sum_ref[...]) - base)).astype(BF16)


VM = pl.BlockSpec(memory_space=pltpu.VMEM)
SM = pl.BlockSpec(memory_space=pltpu.SMEM)
HB = pl.BlockSpec(memory_space=pl.ANY)
DMA = pltpu.SemaphoreType.DMA


def stay(array):
    return pltpu.with_memory_space_constraint(array, pltpu.VMEM)


def far(array):
    return pltpu.with_memory_space_constraint(array, pltpu.HBM)


def local(hidden, lengths, request_prompt, request_adapter, prompt_page_table, prefix_page_cache,
          query_key_value_weight, adapter_down, adapter_up, attention_scale, output_matrix, attention_rate,
          up_matrix, gate_matrix, up_scaling, gate_scaling, down_matrix, feedforward_rate):
    lengths = far(lengths)
    queries, key_values, matrix = pl.pallas_call(
        gather_kernel,
        out_shape=(
            pltpu.VMEM((GROUP, 128), BF16),
            pltpu.VMEM((NREQ * PREFIX + GROUP, 128), BF16),
            pltpu.VMEM((2, 4, NZ, 2, 16, D // 2), BF16),
        ),
        in_specs=[HB, HB, HB, HB, HB, HB, VM, SM, SM, SM, SM],
        out_specs=(VM, VM, VM),
        scratch_shapes=[
            pltpu.VMEM((NT, ROWS, D), BF16),
            pltpu.VMEM((2, 4, 4, 2, 64, 128), BF16),
            pltpu.VMEM((2, 4, 4, 2, RANK, 192), BF16),
            pltpu.VMEM((2, 2, 4, 4, RANK, D), BF16),
            pltpu.VMEM((384, D), BF16),
            pltpu.VMEM((128, 192), F32),
            pltpu.VMEM((128, 128), F32),
            pltpu.VMEM((128, 256), BF16),
            pltpu.VMEM((8, 128), F32),
            pltpu.VMEM((NZ, 256, 128), F32),
            DMA((2, 4, 2)), DMA((2, 4, 2)), DMA((8, 2)), DMA((8, 2)), DMA((2, 4, 2)), DMA((2, 4, 2)),
            DMA((6, 8)), DMA((6, 8)), DMA((2, 4)), DMA((2, 4)), DMA((11,)), DMA((2,)), DMA((2,)),
        ],
        compiler_params=pltpu.CompilerParams(
            collective_id=0, has_side_effects=True, vmem_limit_bytes=32 * 2**20),
        name="gather_project",
    )(*[far(a) for a in (
        hidden, output_matrix, prefix_page_cache, adapter_up, jnp.swapaxes(adapter_down, 1, 2),
        query_key_value_weight.T, attention_scale)],
      lengths, *[far(a) for a in (request_adapter, request_prompt, prompt_page_table.T)])
    attn = pl.pallas_call(
        attend_kernel,
        out_shape=pltpu.VMEM((NT, 2, 32, 128), BF16),
        in_specs=[VM, VM, SM],
        out_specs=VM,
        scratch_shapes=[pltpu.VMEM((256, 128), F32), pltpu.SMEM((2 * NREQ,), jnp.int32)],
        compiler_params=pltpu.CompilerParams(vmem_limit_bytes=16 * 2**20),
        name="attend",
    )(stay(queries), stay(key_values), lengths)
    sums, mixed = pl.pallas_call(
        mix_kernel,
        out_shape=(pltpu.VMEM((ROWS, D), F32), pltpu.VMEM((ROWS, D), BF16)),
        in_specs=[VM, VM, VM, HB, HB, HB, VM, VM, VM],
        out_specs=(VM, VM),
        scratch_shapes=[
            pltpu.VMEM((2, NT, 32, 128), BF16),
            pltpu.VMEM((64, NT * HW), BF16),
            pltpu.VMEM((NZ, 2, 4, 16, D), BF16),
            pltpu.VMEM((320, D), BF16),
            pltpu.VMEM((320, D), BF16),
            pltpu.VMEM((320, D), BF16),
            pltpu.VMEM((NT, ROWS, D), BF16),
            pltpu.VMEM((NT, ROWS, D), BF16),
            pltpu.VMEM((NZ, ROWS, D), BF16),
            pltpu.VMEM((4, ROWS, D), BF16), pltpu.VMEM((4, ROWS, D), BF16),
            pltpu.VMEM((4, ROWS, D), BF16), pltpu.VMEM((4, ROWS, D), BF16),
            DMA((2, 16)), DMA((2, 16)), DMA((8,)), DMA((8,)),
            DMA((2, 4, 4)), DMA((2, 4, 4)), DMA((8, 4)), DMA((8, 4)),
            DMA((8,)), DMA((8,)), DMA((2, 4, 4)), DMA((2, 4, 4)), DMA((13,)),
        ],
        compiler_params=pltpu.CompilerParams(
            collective_id=1, has_side_effects=True, vmem_limit_bytes=44 * 2**20),
        name="mix_feed",
    )(stay(attn), stay(matrix), hidden, up_matrix.T, gate_matrix.T, down_matrix,
      up_scaling, gate_scaling, attention_rate)
    return pl.pallas_call(
        finish_kernel,
        out_shape=jax.ShapeDtypeStruct((ROWS, D), BF16),
        in_specs=[VM, VM, VM],
        out_specs=VM,
        compiler_params=pltpu.CompilerParams(vmem_limit_bytes=16 * 2**20),
        name="finish",
    )(stay(sums), stay(mixed), feedforward_rate)


def solution(mesh):
    placed = (
        P(("dp", "tensor"), None),
        P("dp", None),
        P("dp", None),
        P("dp", None),
        P(),
        P("dp", None, "tensor"),
        P(None, "tensor"),
        P("dp", None, None),
        P("dp", None, "tensor"),
        P("tensor"),
        P("tensor", None),
        P(),
        P(None, "tensor"),
        P(None, "tensor"),
        P("tensor"),
        P("tensor"),
        P("tensor", None),
        P(),
    )
    return jax.shard_map(
        local, mesh=mesh, in_specs=placed, out_specs=P(("dp", "tensor"), None), check_vma=False
    )
```

```python
import functools
import math

import jax
import jax.numpy as jnp
from jax import lax
from jax.experimental import pallas as pl
from jax.experimental.pallas import tpu as pltpu
from jax.sharding import PartitionSpec as P

MESH = pl.DeviceIdType.MESH
D = 1280
HW = 64
RANK = 16
NREQ = 8
PREFIX = 256
NT = 16
NZ = 8
ROWS = 128
GROUP = 2048
EPS = 1e-06
F32 = jnp.float32
BF16 = jnp.bfloat16
NT_DIMS = (((1,), (1,)), ((), ()))


def place():
    dp = lax.axis_index("dp")
    t = lax.axis_index("tensor")
    return dp, t, t // 2, t % 2


def delta(i):
    half = (i + 1) // 2
    odd = i % 2
    return half * (1 - 2 * odd)


def at_z(z, d):
    return (z + d + NZ) % NZ


class Ring:
    def __init__(self, chunks, zsend, zrecv, psend=None, precv=None, in_order=False):
        self.dp, _, self.z, self.c = place()
        self.chunks, self.zsend, self.zrecv = chunks, zsend, zrecv
        self.psend, self.precv, self.in_order = psend, precv, in_order
        self.started = []
        self.next = (self.dp, at_z(self.z, 1) * 2 + self.c), (self.dp, at_z(self.z, -1) * 2 + self.c)
        self.other = (self.dp, self.z * 2 + (1 - self.c))

    def spot(self, k, zb, core):
        return self.chunks[k][0](zb, core)

    def ring_copy(self, way, step, k, src, zb):
        return pltpu.make_async_remote_copy(
            src_ref=src, dst_ref=self.spot(k, zb, self.c),
            send_sem=self.zsend.at[way, step - 1, k], recv_sem=self.zrecv.at[way, step - 1, k],
            device_id=self.next[way], device_id_type=MESH)

    def core_copy(self, i, k, src, zb, core):
        return pltpu.make_async_remote_copy(
            src_ref=src, dst_ref=self.spot(k, zb, core),
            send_sem=self.psend.at[i, k], recv_sem=self.precv.at[i, k],
            device_id=self.other, device_id_type=MESH)

    def go(self, copy):
        copy.start()
        self.started.append(copy)

    def turn(self, n):
        return (n, n) if self.in_order else (n, n + 1 - 2 * (n % 2))

    def start(self, ks):
        for k in ks:
            for way in range(2):
                self.go(self.ring_copy(way, 1, k, self.chunks[k][1], self.z))
            self.go(self.core_copy(0, k, self.chunks[k][1], self.z, self.c))

    def first(self, ns=None):
        ns = range(len(self.chunks)) if ns is None else ns
        for n in ns:
            for way, k in enumerate(self.turn(n)):
                self.go(self.ring_copy(way, 1, k, self.chunks[k][1], self.z))
        if self.psend is not None:
            for n in ns:
                self.go(self.core_copy(0, n, self.chunks[n][1], self.z, self.c))

    def step(self, s, ns=None):
        for n in range(len(self.chunks)) if ns is None else ns:
            for way, k in enumerate(self.turn(n)):
                far = k % 2 == way
                if s == 4 and not far:
                    continue
                zb = at_z(self.z, -s if way == 0 else s)
                here = self.spot(k, zb, self.c)
                self.ring_copy(way, s, k, here, zb).wait_recv()
                if s < 3 or (s == 3 and far):
                    self.go(self.ring_copy(way, s + 1, k, here, zb))
                if self.psend is not None:
                    i = 7 if s == 4 else (2 * s - 1 if way == 0 else 2 * s)
                    self.go(self.core_copy(i, k, here, zb, self.c))

    def from_core(self, i):
        zb = at_z(self.z, delta(i))
        for k in range(len(self.chunks)):
            self.core_copy(i, k, self.spot(k, zb, 1 - self.c), zb, 1 - self.c).wait_recv()

    def drain(self):
        for copy in self.started:
            copy.wait_send()


def slab(buf, first_row, rows):
    return lambda zb, core: buf.at[zb * 2 + core, pl.ds(first_row, rows)]


class Plane:
    def __init__(self, number, first_axis, src, buf, send, recv, local):
        dp, t, _, _ = place()
        x, y = dp // 4, dp % 4
        self.src, self.buf, self.n, self.send, self.recv, self.local = src, buf, number, send, recv, local
        self.a, self.b = (x, y) if first_axis == 0 else (y, x)

        def device(a, b):
            return (a * 4 + b if first_axis == 0 else b * 4 + a), t

        up_a, down_a = (self.a + 1) % 4, (self.a + 3) % 4
        up_b, down_b = (self.b + 1) % 4, (self.b + 3) % 4
        self.lo_a, self.hi_a, self.lo_b, self.hi_b = down_a, up_a, down_b, up_b
        self.dev_a = device(up_a, self.b), device(down_a, self.b)
        self.dev_b = device(self.a, up_b), device(self.a, down_b)
        self.started = []

    def copy(self, k, src, dst, dev):
        return pltpu.make_async_remote_copy(
            src_ref=src, dst_ref=dst, send_sem=self.send.at[self.n, k], recv_sem=self.recv.at[self.n, k],
            device_id=dev, device_id_type=MESH)

    def go(self, k, src, dst, dev):
        c = self.copy(k, src, dst, dev)
        c.start()
        self.started.append(c)

    def got(self, k, dst):
        self.copy(k, dst, dst, self.dev_a[0]).wait_recv()

    def halves(self, ref):
        if len(ref.shape) == 2:
            n = ref.shape[1] // 2
            return ref.at[:, pl.ds(0, n)], ref.at[:, pl.ds(n, n)]
        n = ref.shape[0] // 2
        return ref.at[pl.ds(0, n)], ref.at[pl.ds(n, n)]

    def one(self):
        mine = self.buf.at[self.b, self.a]
        self.own = pltpu.make_async_copy(self.src, mine, self.local.at[self.n])
        self.own.start()
        self.go(0, self.src, mine, self.dev_a[0])
        self.go(1, self.src, mine, self.dev_a[1])

    def two(self):
        lo, hi = self.buf.at[self.b, self.lo_a], self.buf.at[self.b, self.hi_a]
        self.got(0, lo)
        self.go(2, self.halves(lo)[0], self.halves(lo)[0], self.dev_a[0])
        self.got(1, hi)
        self.go(3, self.halves(hi)[1], self.halves(hi)[1], self.dev_a[1])

    def three(self):
        far = self.buf.at[self.b, (self.a + 2) % 4]
        self.got(2, self.halves(far)[0])
        self.got(3, self.halves(far)[1])
        self.own.wait()

    def turn(self):
        row = self.buf.at[self.b]
        self.go(4, row, row, self.dev_b[0])
        self.go(5, row, row, self.dev_b[1])

    def four(self):
        lo, hi = self.buf.at[self.lo_b], self.buf.at[self.hi_b]
        self.got(4, lo)
        self.go(6, self.halves(lo)[0], self.halves(lo)[0], self.dev_b[0])
        self.got(5, hi)
        self.go(7, self.halves(hi)[1], self.halves(hi)[1], self.dev_b[1])

    def five(self):
        far = self.buf.at[(self.b + 2) % 4]
        self.got(6, self.halves(far)[0])
        self.got(7, self.halves(far)[1])

    def drain(self):
        for c in self.started:
            c.wait_send()


class Line:
    def __init__(self, number, axis, at, send, recv):
        dp, t, _, _ = place()
        x, y = dp // 4, dp % 4
        self.n, self.at, self.send, self.recv = number, at, send, recv
        self.a = x if axis == 0 else y

        def device(a):
            return (a * 4 + y if axis == 0 else x * 4 + a), t

        self.lo, self.hi, self.far = (self.a + 3) % 4, (self.a + 1) % 4, (self.a + 2) % 4
        self.devs = device(self.hi), device(self.lo)
        self.started = []

    def copy(self, k, ref, dev):
        return pltpu.make_async_remote_copy(
            src_ref=ref, dst_ref=ref, send_sem=self.send.at[self.n, k], recv_sem=self.recv.at[self.n, k],
            device_id=dev, device_id_type=MESH)

    def go(self, k, ref, dev):
        c = self.copy(k, ref, dev)
        c.start()
        self.started.append(c)

    def one(self):
        for k in range(2):
            self.go(k, self.at(self.a, 0, 8), self.devs[k])

    def two(self):
        self.copy(0, self.at(self.lo, 0, 8), self.devs[0]).wait_recv()
        self.go(2, self.at(self.lo, 0, 4), self.devs[0])
        self.copy(1, self.at(self.hi, 0, 8), self.devs[1]).wait_recv()
        self.go(3, self.at(self.hi, 4, 4), self.devs[1])

    def three(self):
        self.copy(2, self.at(self.far, 0, 4), self.devs[0]).wait_recv()
        self.copy(3, self.at(self.far, 4, 4), self.devs[1]).wait_recv()

    def drain(self):
        for c in self.started:
            c.wait_send()


def greet(peers):
    barrier = pltpu.get_barrier_semaphore()
    for peer in peers:
        pl.semaphore_signal(barrier, inc=1, device_id=peer, device_id_type=MESH)
    pl.semaphore_wait(barrier, len(peers))


def lanes(shape):
    return lax.broadcasted_iota(jnp.int32, shape, len(shape) - 1)


def row_starts(len_ref, first_row, shape):
    rows = first_row + lax.broadcasted_iota(jnp.int32, shape, 0)
    end = jnp.int32(0)
    req = jnp.zeros(shape, jnp.int32)
    start = jnp.zeros(shape, jnp.int32)
    for r in range(NREQ):
        size = len_ref[0, r]
        end = end + size
        past = rows >= end
        req = req + jnp.where(past, 1, 0)
        start = start + jnp.where(past, size, 0)
    return rows, req, start


def gather_kernel(h_ref, o_ref, pg_ref, up_ref, dn_ref, w_ref, gain_ref, len_ref, ra_ref, rp_ref, pt_ref,
                  q_out, kv_out, ob,
                  gh, pb, ub, db, wide, sel, tail, su, gains, cosines, sines, mine,
                  zsend, zrecv, psend, precv, usend, urecv, xsend, xrecv, lsend, lrecv, local, dsend, drecv):
    dp, t, z, c = place()
    x, y = dp // 4, dp % 4
    greet([
        (dp, at_z(z, 1) * 2 + c), (dp, at_z(z, -1) * 2 + c), (dp, z * 2 + (1 - c)),
        (((x + 1) % 4) * 4 + y, t), (((x + 3) % 4) * 4 + y, t),
        (x * 4 + (y + 1) % 4, t), (x * 4 + (y + 3) % 4, t),
    ])
    ring = Ring([(slab(gh, 32 * k, 32), h_ref.at[pl.ds(32 * k, 32)]) for k in range(4)],
                zsend, zrecv, psend, precv)
    quarters = [(x, o_ref.at[pl.ds(pl.multiple_of(16 * x, 16), 16), pl.ds(0, D // 2)]),
                (y, o_ref.at[pl.ds(pl.multiple_of(16 * y, 16), 16), pl.ds(D // 2, D // 2)])]
    oring = Ring([(functools.partial(lambda part, j, zb, core: ob.at[part, j, zb, core], part, j), src)
                  for part, (j, src) in enumerate(quarters)], usend, urecv)
    lines = [Line(part, part, functools.partial(
        lambda part, j, z0, n: ob.at[part, j, pl.ds(z0, n), c], part), lsend, lrecv) for part in range(2)]
    adapters, pages = [], []
    for half in range(2):
        adapters.append(Plane(half, half, dn_ref.at[2 * c + half], db.at[c, half], xsend, xrecv, local))
        adapters.append(Plane(2 + half, half, up_ref.at[pl.ds(2 * half, 2)], ub.at[half], xsend, xrecv, local))
        pages.append(Plane(4 + half, half, pg_ref.at[pl.ds(2 * half, 2)], pb.at[half], xsend, xrecv, local))
    planes = adapters + pages
    oring.first()
    ring.first([0, 1])
    for p in planes:
        p.one()
    owns = [pltpu.make_async_copy(h_ref, gh.at[t], local.at[6])]
    for part, (j, src) in enumerate(quarters):
        owns.append(pltpu.make_async_copy(src, ob.at[part, j, z, c], local.at[7 + part]))
    owns.append(pltpu.make_async_copy(
        w_ref.at[pl.ds(0, HW)], wide.at[pl.ds(128, HW)], local.at[9]))
    owns.append(pltpu.make_async_copy(
        w_ref.at[pl.ds(HW, 2 * HW)], wide.at[pl.ds(256, 2 * HW)], local.at[10]))
    for own in owns:
        own.start()
    oring.step(1)
    ring.first([2, 3])
    for p in planes:
        p.two()
    for p in adapters:
        p.three()
        p.turn()
    for own in owns:
        own.wait()
    oring.step(2)
    ring.step(1, [0, 1])

    lane = lanes((256, 128))
    low = lane < HW
    gains[...] = jnp.ones_like(gains)
    gains[:, 0:HW] = jnp.broadcast_to(gain_ref[...].reshape(1, HW), (8, HW))
    gain = gains[0:1, :]
    wide[192:256, :] = jnp.zeros((HW, D), BF16)
    tail[...] = jnp.zeros_like(tail)
    frequency = jnp.exp((lane % 32).astype(F32) * (-2.0 * math.log(10000.0) / HW))
    quarter = jnp.where(low, 0.0, 0.5 * math.pi)

    def waves(b):
        rows, req, start = row_starts(len_ref, b * 256, (256, 128))
        angle = (rows - start + PREFIX).astype(F32) * frequency
        wave = jnp.cos(angle - quarter)
        cosines[b] = jnp.where(low, wave, 1.0)
        sine = pltpu.roll(wave, HW, 1)
        sines[b] = jnp.where(lane < 32, -sine, jnp.where(low, sine, 0.0))
        mine[b] = jnp.where(lane // RANK == req, 1.0, 0.0).astype(BF16)

    pl.loop(0, 4)(waves)
    for p in pages:
        p.three()
    oring.step(3)
    ring.step(1, [2, 3])
    for p in adapters:
        p.four()
    for p in pages:
        p.turn()
    pl.loop(4, 8)(waves)
    for p in adapters:
        p.five()
    other = (dp, z * 2 + (1 - c))

    def to_other(n, mine, theirs):
        send = pltpu.make_async_remote_copy(
            src_ref=mine, dst_ref=mine, send_sem=dsend.at[n], recv_sem=drecv.at[n],
            device_id=other, device_id_type=MESH)
        receive = pltpu.make_async_remote_copy(
            src_ref=theirs, dst_ref=theirs, send_sem=dsend.at[n], recv_sem=drecv.at[n],
            device_id=other, device_id_type=MESH)
        send.start()
        return send, receive

    swaps = [to_other(half, db.at[c, half], db.at[1 - c, half]) for half in range(2)]
    oring.step(4)
    for line in lines:
        line.one()
    ring.step(2, [0, 1])

    def unit(v):
        total = jnp.sum(jnp.where(low, v * v, 0.0), axis=1, keepdims=True)
        return v * lax.rsqrt(total + EPS) * gain

    def slot(owner, half):
        a, b = owner // 4, owner % 4
        return b + half * (a - b), a + half * (b - a)

    def prefix(r):
        prompt = rp_ref[0, r]
        for j in range(4):
            page = pt_ref[j, prompt]
            half = (page % 4) // 2
            major, minor = slot(page // 4, half)
            raw = pb[half, major, minor, page % 2].astype(F32)
            low_p = lanes((64, 128)) < HW
            total = jnp.sum(jnp.where(low_p, raw * raw, 0.0), axis=1, keepdims=True)
            unit_key = raw * lax.rsqrt(total + EPS) * gain
            kv_out[pl.ds(pl.multiple_of(r * PREFIX + j * 64, 64), 64), :] = jnp.where(
                low_p, unit_key, raw).astype(BF16)

    for _, receive in swaps:
        receive.wait_recv()
    for r in range(NREQ):
        adapter = ra_ref[0, r]
        within = adapter % 4
        major, minor = slot(adapter // 4, within % 2)
        wide[r * RANK:(r + 1) * RANK, :] = db[within // 2, within % 2, major, minor]
        major, minor = slot(adapter // 4, within // 2)
        sel[r * RANK:(r + 1) * RANK, :] = ub[within // 2, major, minor, within % 2].astype(F32)
    first = sel[:, 0:128]
    tail[:, 0:HW] = sel[:, 128:192]
    low_s = lanes((128, 128)) < HW
    su[:, 0:128] = jnp.where(low_s, first, 0.0).astype(BF16)
    su[:, 128:256] = jnp.where(low_s, pltpu.roll(first, HW, 1), pltpu.roll(tail[...], HW, 1)).astype(BF16)

    def project(i):
        ring.from_core(i)
        zb = at_z(z, delta(i))
        values = gh[pl.ds(zb * 2, 2)].reshape(256, D)
        every = lax.dot_general(values, wide[...], NT_DIMS, preferred_element_type=F32)
        middle = every[:, 0:128].astype(BF16) * mine[zb]
        both = every[:, 128:384] + 0.5 * jnp.dot(middle, su[...], preferred_element_type=F32)
        cosine, sine = cosines[zb], sines[zb]

        def rotate(v):
            other = jnp.where(lane < 32, pltpu.roll(v, 96, 1), pltpu.roll(v, 32, 1))
            return v * cosine + other * sine

        query, key_value = both[:, :128], both[:, 128:]
        row = pl.multiple_of(zb * 256, 256)
        q_out[pl.ds(row, 256), :] = unit(rotate(query)).astype(BF16) * jnp.asarray(8.0, BF16)
        kv_out[pl.ds(row + NREQ * PREFIX, 256), :] = jnp.where(
            low, unit(rotate(key_value)), key_value).astype(BF16)

    pl.loop(0, 1)(project)
    ring.step(2, [2, 3])
    pl.loop(1, 2)(project)
    for p in pages:
        p.four()
    pl.loop(2, 3)(project)
    ring.step(3, [0, 1])
    for line in lines:
        line.two()
    pl.loop(3, 5)(project)
    ring.step(3, [2, 3])
    for p in pages:
        p.five()
    pl.loop(5, 7)(project)
    ring.step(4)
    pl.loop(0, NREQ)(prefix)
    pl.loop(7, 8)(project)
    for line in lines:
        line.three()
    for part in [ring, oring] + planes + lines:
        part.drain()
    for send, _ in swaps:
        send.wait_send()


TILES = 2


def attend_kernel(q_ref, kv_ref, len_ref, out_ref, acc, begins):
    low = lanes((256, 128)) < HW
    begin = jnp.int32(0)
    for r in range(NREQ):
        begins[r] = begin
        begin = begin + len_ref[0, r]
    for r in range(NREQ, 2 * NREQ):
        begins[r] = jnp.int32(0)

    @pl.loop(0, NZ)
    def _(i):
        first = i * 256
        query = q_ref[pl.ds(pl.multiple_of(first, 256), 256), :]
        rows, _, start = row_starts(len_ref, first, (256, 256))
        end = jnp.int32(0)
        request_lo, request_hi, start_lo = jnp.int32(0), jnp.int32(0), jnp.int32(0)
        for r in range(NREQ):
            size = len_ref[0, r]
            end = end + size
            request_lo = request_lo + jnp.where(first >= end, 1, 0)
            start_lo = start_lo + jnp.where(first >= end, size, 0)
            request_hi = request_hi + jnp.where(first + 255 >= end, 1, 0)
        acc[...] = jnp.zeros_like(acc)
        lowest = start_lo // 256
        prefixes = request_hi + 1 - request_lo
        count = prefixes + i + 1 - lowest
        lane = lanes((256, 256))

        @pl.loop(0, (count + TILES - 1) // TILES)
        def _(n):
            total = None
            for u in range(TILES):
                m = jnp.minimum(n * TILES + u, count - 1)
                shared = m < prefixes
                tile = jnp.where(shared, request_lo + m, NREQ + lowest + m - prefixes)
                base = jnp.where(shared, begins[tile], (tile - NREQ) * 256)
                base = jnp.where(n * TILES + u < count, base, 2 * GROUP)
                column = jnp.where(shared, 0, 1) * lane + base
                keys = kv_ref[pl.ds(pl.multiple_of(tile * 256, 256), 256), :]
                score = lax.dot_general(query, keys, NT_DIMS, preferred_element_type=F32)
                weight = jnp.where((column >= start) & (column <= rows), jnp.exp(score), 0.0).astype(BF16)
                ones = jnp.where(low, jnp.asarray(1.0, BF16), keys)
                part = jnp.dot(weight, ones, preferred_element_type=F32)
                total = part if total is None else total + part
            acc[...] += total

        total = acc[...]
        result = total / pltpu.roll(total, HW, 1)
        for b in range(4):
            top, bottom = result[b * 64:b * 64 + 32], result[b * 64 + 32:b * 64 + 64]
            out_ref[2 * i + b // 2, b % 2] = jnp.where(
                lanes((32, 128)) >= HW, top, pltpu.roll(bottom, HW, 1)).astype(BF16)


def renorm(v):
    return v * lax.rsqrt(jnp.mean(v * v, axis=-1, keepdims=True) + EPS)


def mix_kernel(attn_ref, o_ref, h_ref, wu_ref, wg_ref, wd_ref, su_ref, sg_ref, ra_ref, rf_ref, rows_out,
               heads, lhs, om, wu, wg, wd, mixed, part, peer, rr, rl, sr, sl,
               asend, arecv, msend, mrecv, zsend, zrecv, psend, precv, qsend, qrecv, rsend, rrecv, local):
    dp, t, z, c = place()
    greet([(dp, (t + n) % NT) for n in range(1, NT)])
    started = []
    order = [8, 9, 7, 10, 6, 11, 5, 12, 4, 13, 3, 14, 2, 15, 1]

    def exchange(half, n, to, origin):
        return pltpu.make_async_remote_copy(
            src_ref=attn_ref.at[to, half], dst_ref=heads.at[half, origin], send_sem=asend.at[half, n],
            recv_sem=arecv.at[half, n], device_id=(dp, to), device_id_type=MESH)

    for half in range(2):
        for n in order:
            copy = exchange(half, n, (t + n) % NT, t)
            copy.start()
            started.append(copy)
    owns = [pltpu.make_async_copy(attn_ref.at[t, half], heads.at[half, t], local.at[11 + half])
            for half in range(2)]
    for own in owns:
        own.start()
    eighths = [(part, j) for part in range(2) for j in range(4)]

    def place_in(part, j, core):
        return om.at[:, core, j, :, pl.ds(part * (D // 2), D // 2)]

    def matrix_copy(n, core):
        part, j = eighths[n]
        return pltpu.make_async_remote_copy(
            src_ref=o_ref.at[part, j, :, c], dst_ref=place_in(part, j, core), send_sem=msend.at[n],
            recv_sem=mrecv.at[n], device_id=(dp, z * 2 + (1 - c)), device_id_type=MESH)

    for n in range(8):
        copy = matrix_copy(n, c)
        copy.start()
        started.append(copy)
    moves = [(o_ref.at[part, j, :, c], place_in(part, j, c)) for part, j in eighths]
    moves += [(wu_ref, wu), (wg_ref, wg), (wd_ref, wd)]
    loads = [pltpu.make_async_copy(a, b, local.at[n]) for n, (a, b) in enumerate(moves)]
    for copy in loads:
        copy.start()
    rate = ra_ref[...].reshape(1, D)
    high = lanes((32, 128)) >= HW
    ring = Ring([(slab(mixed, 32 * k, 32), mixed.at[t, pl.ds(32 * k, 32)]) for k in range(4)],
                zsend, zrecv, psend, precv, in_order=True)
    for half in range(2):
        owns[half].wait()
        for n in order:
            frm = (t + NT - n) % NT
            exchange(half, n, t, frm).wait_recv()
        for j in range(NT // 2):
            even, odd = heads[half, 2 * j].astype(F32), heads[half, 2 * j + 1].astype(F32)
            cols = slice(128 * j, 128 * j + 128)
            lhs[0:32, cols] = jnp.where(high, odd, pltpu.roll(even, HW, 1)).astype(BF16)
            lhs[32:64, cols] = jnp.where(high, pltpu.roll(odd, HW, 1), even).astype(BF16)
        if half == 0:
            for n in range(8):
                loads[n].wait()
                matrix_copy(n, 1 - c).wait_recv()
        attn_sum = jnp.dot(lhs[...], om[...].reshape(NT * HW, D), preferred_element_type=F32)
        rows = slice(64 * half, 64 * half + 64)
        base = h_ref[rows, :].astype(F32)
        mine = renorm(base + rate * (renorm(attn_sum) - base)).astype(BF16)
        mixed[t, rows] = mine
        ring.start([2 * half, 2 * half + 1])
    for copy in loads[8:]:
        copy.wait()
    scale_up, scale_gate = su_ref[...].reshape(1, 320), sg_ref[...].reshape(1, 320)

    def swap(i, zb):
        return pltpu.make_async_remote_copy(
            src_ref=part.at[zb * 2 + (1 - c)], dst_ref=peer.at[zb], send_sem=qsend.at[i], recv_sem=qrecv.at[i],
            device_id=(dp, z * 2 + (1 - c)), device_id_type=MESH)

    def feed(i):
        ring.from_core(i)
        zb = at_z(z, delta(i))
        values = mixed[pl.ds(zb * 2, 2)].reshape(256, D)
        up = lax.dot_general(values, wu[...], NT_DIMS, preferred_element_type=F32) * scale_up
        gate = lax.dot_general(values, wg[...], NT_DIMS, preferred_element_type=F32) * scale_gate
        units = (up * (gate / (1.0 + jnp.exp(-gate)))).astype(BF16)
        result = jnp.dot(units, wd[...], preferred_element_type=F32).astype(BF16)
        part[pl.ds(zb * 2, 2)] = result.reshape(2, ROWS, D)
        swap(i, zb).start()

    def local_sum(zb, k):
        rows = pl.ds(32 * k, 32)
        return part[zb * 2 + c, rows].astype(F32) + peer[zb, rows].astype(F32)

    def rs_copy(way, d, k, src):
        dst = (rr if way == 0 else rl).at[d - 1, pl.ds(32 * k, 32)]
        dev = (dp, at_z(z, 1 if way == 0 else -1) * 2 + c)
        return pltpu.make_async_remote_copy(
            src_ref=src, dst_ref=dst, send_sem=rsend.at[way, d - 1, k], recv_sem=rrecv.at[way, d - 1, k],
            device_id=dev, device_id_type=MESH)

    def pass_on(d, near, far):
        for n in ([2, 3] if near else []) + ([0, 1] if far else []):
            for way in range(2):
                k = way + 2 * n if n < 2 else 1 - way + 2 * (n - 2)
                rows = pl.ds(32 * k, 32)
                recv, sent = (rr, sr) if way == 0 else (rl, sl)
                value = local_sum(at_z(z, d if way == 0 else -d), k)
                if d < 3 or (d == 3 and n < 2):
                    rs_copy(way, d + 1, k, sent.at[d, rows]).wait_recv()
                    value = value + recv[d, rows].astype(F32)
                sent[d - 1, rows] = value.astype(BF16)
                copy = rs_copy(way, d, k, sent.at[d - 1, rows])
                copy.start()
                started.append(copy)

    def swapped(d):
        swap(2 * d - 1, at_z(z, -d)).wait_recv()
        if d < 4:
            swap(2 * d, at_z(z, d)).wait_recv()

    pl.loop(0, 1)(feed)
    ring.step(1)
    pl.loop(1, 3)(feed)
    ring.step(2)
    pl.loop(3, 5)(feed)
    ring.step(3)
    pl.loop(5, 7)(feed)
    ring.step(4)
    swapped(3)
    pass_on(3, True, False)
    pl.loop(7, 8)(feed)
    swapped(4)
    pass_on(4, False, True)
    pass_on(3, False, True)
    swapped(2)
    pass_on(2, True, True)
    swapped(1)
    pass_on(1, True, True)
    swap(0, z).wait_recv()
    last_rate = rf_ref[...].reshape(1, D)
    for k in range(4):
        rows = pl.ds(32 * k, 32)
        value = local_sum(z, k)
        for way in range(2):
            rs_copy(way, 1, k, (sr if way == 0 else sl).at[0, rows]).wait_recv()
        value = value + rr[0, rows].astype(F32) + rl[0, rows].astype(F32)
        base = mixed[t, rows].astype(F32)
        rows_out[rows, :] = renorm(base + last_rate * (renorm(value) - base)).astype(BF16)
    ring.drain()
    for copy in started:
        copy.wait_send()
    for i in range(NZ):
        swap(i, at_z(z, delta(i))).wait_send()


def finish_kernel(rows_ref, out_ref, sem):
    copy = pltpu.make_async_copy(rows_ref, out_ref, sem)
    copy.start()
    copy.wait()


VM = pl.BlockSpec(memory_space=pltpu.VMEM)
SM = pl.BlockSpec(memory_space=pltpu.SMEM)
HB = pl.BlockSpec(memory_space=pl.ANY)
DMA = pltpu.SemaphoreType.DMA


def stay(array):
    return pltpu.with_memory_space_constraint(array, pltpu.VMEM)


def far(array):
    return pltpu.with_memory_space_constraint(array, pltpu.HBM)


def local(hidden, lengths, request_prompt, request_adapter, prompt_page_table, prefix_page_cache,
          query_key_value_weight, adapter_down, adapter_up, attention_scale, output_matrix, attention_rate,
          up_matrix, gate_matrix, up_scaling, gate_scaling, down_matrix, feedforward_rate):
    lengths = far(lengths)
    queries, key_values, matrix = pl.pallas_call(
        gather_kernel,
        out_shape=(
            pltpu.VMEM((GROUP, 128), BF16),
            pltpu.VMEM((NREQ * PREFIX + GROUP, 128), BF16),
            pltpu.VMEM((2, 4, NZ, 2, 16, D // 2), BF16),
        ),
        in_specs=[HB, HB, HB, HB, HB, HB, VM, SM, SM, SM, SM],
        out_specs=(VM, VM, VM),
        scratch_shapes=[
            pltpu.VMEM((NT, ROWS, D), BF16),
            pltpu.VMEM((2, 4, 4, 2, 64, 128), BF16),
            pltpu.VMEM((2, 4, 4, 2, RANK, 192), BF16),
            pltpu.VMEM((2, 2, 4, 4, RANK, D), BF16),
            pltpu.VMEM((384, D), BF16),
            pltpu.VMEM((128, 192), F32),
            pltpu.VMEM((128, 128), F32),
            pltpu.VMEM((128, 256), BF16),
            pltpu.VMEM((8, 128), F32),
            pltpu.VMEM((NZ, 256, 128), F32),
            pltpu.VMEM((NZ, 256, 128), F32),
            pltpu.VMEM((NZ, 256, 128), BF16),
            DMA((2, 4, 4)), DMA((2, 4, 4)), DMA((8, 4)), DMA((8, 4)), DMA((2, 4, 2)), DMA((2, 4, 2)),
            DMA((6, 8)), DMA((6, 8)), DMA((2, 4)), DMA((2, 4)), DMA((11,)), DMA((2,)), DMA((2,)),
        ],
        compiler_params=pltpu.CompilerParams(
            collective_id=0, has_side_effects=True, vmem_limit_bytes=32 * 2**20),
        name="gather_project",
    )(*[far(a) for a in (
        hidden, output_matrix, prefix_page_cache, adapter_up, jnp.swapaxes(adapter_down, 1, 2),
        query_key_value_weight.T, attention_scale)],
      lengths, *[far(a) for a in (request_adapter, request_prompt, prompt_page_table.T)])
    attn = pl.pallas_call(
        attend_kernel,
        out_shape=pltpu.VMEM((NT, 2, 32, 128), BF16),
        in_specs=[VM, VM, SM],
        out_specs=VM,
        scratch_shapes=[pltpu.VMEM((256, 128), F32), pltpu.SMEM((2 * NREQ,), jnp.int32)],
        compiler_params=pltpu.CompilerParams(vmem_limit_bytes=16 * 2**20),
        name="attend",
    )(stay(queries), stay(key_values), lengths)
    rows = pl.pallas_call(
        mix_kernel,
        out_shape=pltpu.VMEM((ROWS, D), BF16),
        in_specs=[VM, VM, VM, HB, HB, HB, VM, VM, VM, VM],
        out_specs=VM,
        scratch_shapes=[
            pltpu.VMEM((2, NT, 32, 128), BF16),
            pltpu.VMEM((64, NT * HW), BF16),
            pltpu.VMEM((NZ, 2, 4, 16, D), BF16),
            pltpu.VMEM((320, D), BF16),
            pltpu.VMEM((320, D), BF16),
            pltpu.VMEM((320, D), BF16),
            pltpu.VMEM((NT, ROWS, D), BF16),
            pltpu.VMEM((NT, ROWS, D), BF16),
            pltpu.VMEM((NZ, ROWS, D), BF16),
            pltpu.VMEM((4, ROWS, D), BF16), pltpu.VMEM((4, ROWS, D), BF16),
            pltpu.VMEM((4, ROWS, D), BF16), pltpu.VMEM((4, ROWS, D), BF16),
            DMA((2, 16)), DMA((2, 16)), DMA((8,)), DMA((8,)),
            DMA((2, 4, 4)), DMA((2, 4, 4)), DMA((8, 4)), DMA((8, 4)),
            DMA((8,)), DMA((8,)), DMA((2, 4, 4)), DMA((2, 4, 4)), DMA((13,)),
        ],
        compiler_params=pltpu.CompilerParams(
            collective_id=1, has_side_effects=True, vmem_limit_bytes=44 * 2**20),
        name="mix_feed",
    )(stay(attn), stay(matrix), hidden, up_matrix.T, gate_matrix.T, down_matrix,
      up_scaling, gate_scaling, attention_rate, feedforward_rate)
    return pl.pallas_call(
        finish_kernel,
        out_shape=jax.ShapeDtypeStruct((ROWS, D), BF16),
        in_specs=[VM],
        out_specs=HB,
        scratch_shapes=[DMA],
        compiler_params=pltpu.CompilerParams(vmem_limit_bytes=16 * 2**20),
        name="finish",
    )(stay(rows))


def solution(mesh):
    placed = (
        P(("dp", "tensor"), None),
        P("dp", None),
        P("dp", None),
        P("dp", None),
        P(),
        P("dp", None, "tensor"),
        P(None, "tensor"),
        P("dp", None, None),
        P("dp", None, "tensor"),
        P("tensor"),
        P("tensor", None),
        P(),
        P(None, "tensor"),
        P(None, "tensor"),
        P("tensor"),
        P("tensor"),
        P("tensor", None),
        P(),
    )
    return jax.shard_map(
        local, mesh=mesh, in_specs=placed, out_specs=P(("dp", "tensor"), None), check_vma=False
    )
```
